128 devices in a mesh: tile: 32 (over z_hi, x, y), face: 4 (over z_lo, core).
Axes of the slice: x: 4, y: 4, z: 4 (z_hi: 2, z_lo: 2; z = z_hi * 2 + z_lo), core: 2. Of those that a mesh axis runs over, the one named last changes fastest.
Arguments:
- adjoint_seed: float32 [64, 4, 512, 1024], P(None, None, 'tile', 'face'), may hold values from -6 to 6
- face_flow: float32 [2, 64, 512, 1024], P(None, None, 'tile', 'face'), may hold values from -0.4 to 0.4
- vert_diff: float32 [64, 512, 1024], P(None, 'tile', 'face'), may hold values from 0.1 to 10
- wet_mask: int32 [64, 512, 1024], P(None, 'tile', 'face'), may hold values 0 or 1
- smooth_weights: float32 [2, 512, 1024], P(None, ('tile', 'face')), may hold values from 0.02 to 0.24
Outputs:
- adjoint: float32 [64, 4, 512, 1024], P(None, None, 'tile', 'face')
- controls: float32 [132, 512, 1024], P(None, ('tile', 'face'))
The draws below stay inside these ranges and needn't reach their ends.
All inputs are finite; a program needn't handle non-finite values. No bound on the sum of `wet_mask` on one device may be relied on, other than what follows from the above.
Results may differ from the reference program's by a relative error of at most 0.00011.
Values sent between devices are 32-bit elements; how exact they have to be, the bound alone decides.
No kernel may reach another device: no remote copies, remote signals or barrier semaphores. Data moves between devices by JAX's collectives and lax.ppermute only.
A program may use at most 128 MiB of HBM per device.

```python
import math
import jax
import jax.numpy as jnp

LEV = 64
NY = 512
NX = 1024


def touch_ends(drawn, rng, smallest, high):
    longest = drawn.shape.index(max(drawn.shape))
    spots = []
    for shift in (0, 1):
        where = [jax.random.randint(jax.random.fold_in(rng, axis), (), 0, length) for axis, length in enumerate(drawn.shape)]
        where[longest] = (where[longest] + shift) % drawn.shape[longest]
        spots.append(tuple(where))
    return drawn.at[spots[0]].set(smallest).at[spots[1]].set(high)


def shard_levels(own_key, shape, cuts, smallest, top_value):
    def one(dim, shards_of):
        steps = jax.random.uniform(jax.random.fold_in(jax.random.fold_in(own_key, 6), dim), (shards_of,), jnp.float32, smallest / len(cuts), top_value / len(cuts))
        return jnp.repeat(jnp.exp(steps), shape[dim] // shards_of).reshape((-1,) + (1,) * (len(shape) - dim - 1))

    level = one(*cuts[0])
    for cut in cuts[1:]:
        level = level * one(*cut)
    return level


def bell_draw(own_key, shape, width, bound, pieces=(), kind=jnp.bfloat16):
    level = shard_levels(own_key, shape, pieces, -0.22, 0.18) if pieces else 1.0
    values = jax.random.normal(own_key, shape, jnp.float32) * width * level
    return jnp.minimum(jnp.maximum(values, -bound), bound).astype(kind)


def setup_inputs(seed: int = 0) -> dict:
    keys = jax.random.split(jax.random.key(seed), 6)
    adjoint_seed = bell_draw(keys[0], (LEV, 4, NY, NX), 1.0, 6.0, ((2, 32), (3, 4)), jnp.float32)
    face_flow = jnp.clip(jax.random.uniform(keys[1], (2, LEV, NY, NX), jnp.float32, -0.4, 0.4) * shard_levels(keys[1], (2, LEV, NY, NX), ((2, 32), (3, 4)), -0.4, 0.0), -0.4, 0.4)
    vert_diff = jnp.clip(jnp.exp(math.log(10.0) - 4.6051702 * jax.random.uniform(keys[2], (LEV, NY, NX), jnp.float32) ** shard_levels(keys[2], (LEV, NY, NX), ((1, 32), (2, 4)), -0.2, 0.2)), 0.1, 10.0)
    wet_mask = touch_ends((jax.random.randint(keys[3], (LEV, NY, NX), 0, 5) < 4).astype(jnp.int32), jax.random.fold_in(keys[3], 1), 0, 1)
    smooth_weights = jnp.clip(0.02 + 0.22 * jax.random.uniform(keys[4], (2, NY, NX), jnp.float32) ** shard_levels(keys[4], (2, NY, NX), ((1, 128),), -0.2, 0.2), 0.02, 0.24)
    return dict(adjoint_seed=adjoint_seed, face_flow=face_flow, vert_diff=vert_diff, wet_mask=wet_mask, smooth_weights=smooth_weights)


horizontal_kappa = 0.15


def solve_levels(rhs, vert_diff, wetness):
    upper = vert_diff * wetness * jnp.concatenate([wetness[1:], jnp.zeros_like(wetness[:1])], 0)
    lower = jnp.concatenate([jnp.zeros_like(upper[:1]), upper[:-1]], 0)
    centre_coef = 1.0 + lower + upper
    levels = rhs.shape[0]
    ratio_prev = jnp.zeros(upper.shape[1:], jnp.float32)
    value_prev = jnp.zeros(rhs.shape[1:], jnp.float32)
    ratios = []
    values = []
    for level in range(levels):
        denominator = centre_coef[level] - lower[level] * ratio_prev
        ratio_prev = upper[level] / denominator
        value_prev = (rhs[level] + lower[level][None] * value_prev) / denominator[None]
        ratios.append(ratio_prev)
        values.append(value_prev)
    following = jnp.zeros(rhs.shape[1:], jnp.float32)
    solved = [following] * levels
    for level in range(levels - 1, -1, -1):
        following = values[level] + ratios[level][None] * following
        solved[level] = following
    return jnp.stack(solved, 0)


def inner(array, shift_y, shift_x):
    rows = array.shape[-2]
    cols = array.shape[-1]
    return array[..., 1 + shift_y:rows - 1 + shift_y, 1 + shift_x:cols - 1 + shift_x]


def adjoint_stencil(padded, flow_pad, wet_pad):
    wet_centre = inner(wet_pad, 0, 0)
    open_east = wet_centre * inner(wet_pad, 0, 1)
    open_west = wet_centre * inner(wet_pad, 0, -1)
    open_north = wet_centre * inner(wet_pad, 1, 0)
    open_south = wet_centre * inner(wet_pad, -1, 0)
    east_u = (inner(flow_pad[0], 0, 0) * open_east)[:, None]
    west_u = (inner(flow_pad[0], 0, -1) * open_west)[:, None]
    north_v = (inner(flow_pad[1], 0, 0) * open_north)[:, None]
    south_v = (inner(flow_pad[1], -1, 0) * open_south)[:, None]
    centre = inner(padded, 0, 0)
    east = inner(padded, 0, 1)
    west = inner(padded, 0, -1)
    north = inner(padded, 1, 0)
    south = inner(padded, -1, 0)
    transport = -0.5 * ((east_u - west_u) * centre + west_u * west - east_u * east)
    transport = transport - 0.5 * ((north_v - south_v) * centre + south_v * south - north_v * north)
    mixing = open_east[:, None] * (east - centre) + open_west[:, None] * (west - centre)
    mixing = mixing + open_north[:, None] * (north - centre) + open_south[:, None] * (south - centre)
    return wet_centre[:, None] * (centre + transport + horizontal_kappa * mixing)


def smooth_once(padded, weight_pad):
    centre = inner(padded, 0, 0)
    w_east = inner(weight_pad[0], 0, 0)
    w_west = inner(weight_pad[0], 0, -1)
    w_north = inner(weight_pad[1], 0, 0)
    w_south = inner(weight_pad[1], -1, 0)
    result = centre + w_east * (inner(padded, 0, 1) - centre) + w_west * (inner(padded, 0, -1) - centre)
    return result + w_north * (inner(padded, 1, 0) - centre) + w_south * (inner(padded, -1, 0) - centre)


def reference(adjoint_seed, face_flow, vert_diff, wet_mask, smooth_weights):
    wetness = wet_mask.astype(jnp.float32)
    cycle = ((1, 1), (1, 1))
    flow_pad = jnp.pad(face_flow, ((0, 0), (0, 0)) + cycle)
    wet_pad = jnp.pad(wetness, ((0, 0),) + cycle)
    adjoint = adjoint_seed * wetness[:, None]
    forcing = jnp.zeros(adjoint.shape[1:], jnp.float32)
    for step in range(2):
        solved = solve_levels(adjoint, vert_diff, wetness)
        forcing = forcing + solved[0]
        adjoint = adjoint_stencil(jnp.pad(solved, ((0, 0), (0, 0)) + cycle), flow_pad, wet_pad)
    levels = adjoint.shape[0]
    controls = jnp.concatenate([adjoint[:, 0:2].reshape(2 * levels, adjoint.shape[2], adjoint.shape[3]), forcing], 0)
    weight_pad = jnp.pad(smooth_weights, ((0, 0),) + cycle)
    for sweep in range(4):
        controls = smooth_once(jnp.pad(controls, ((0, 0),) + cycle), weight_pad)
    return adjoint, controls
```

```python
import functools

import jax
import jax.numpy as jnp
from jax import lax
from jax.experimental import pallas as pl
from jax.experimental.pallas import tpu as pltpu
from jax.sharding import PartitionSpec as P

F32 = jnp.float32
LEV = 64
ROWS = 16
LANES = 128
FLAT = LEV * ROWS
WET, UE, VN, VD = 4, 5, 6, 7
KAPPA = 0.15
MIB = 2**20

CHUNKS = ((0, 16), (16, 40), (40, 64))


def iota(shape, dim):
    return lax.broadcasted_iota(jnp.int32, shape, dim)


def rows_of(level):
    return pl.ds(pl.multiple_of(level * ROWS, ROWS), ROWS)


def east_of(tiles):
    last = iota(tiles[0].shape, 1) == LANES - 1
    turned = [pltpu.roll(t, LANES - 1, 1) for t in tiles]
    return [jnp.where(last, turned[(i + 1) % 3], turned[i]) for i in range(3)]


def west_of(tiles):
    first = iota(tiles[0].shape, 1) == 0
    turned = [pltpu.roll(t, 1, 1) for t in tiles]
    return [jnp.where(first, turned[(i + 2) % 3], turned[i]) for i in range(3)]


def call(kernel, outs, scratch=(), limit=8, alias=None, name=None, ins=None):
    def run(*args):
        specs = [pl.BlockSpec(memory_space=pltpu.SMEM)]
        for i in range(1, len(args)):
            space = pltpu.VMEM if ins is None else ins[i]
            specs.append(pl.BlockSpec(memory_space=space))
        return pl.pallas_call(
            kernel,
            out_shape=[jax.ShapeDtypeStruct(s, F32) for s, _ in outs],
            in_specs=specs,
            out_specs=[pl.BlockSpec(memory_space=m) for _, m in outs],
            scratch_shapes=list(scratch),
            input_output_aliases=alias or {},
            compiler_params=pltpu.CompilerParams(vmem_limit_bytes=limit * MIB),
            name=name,
        )(*args)

    return run


VM = pltpu.VMEM


def first_solve(ids, seed, flow, vd, wet, fld, pxa, pxb, ratio, pw, pe):
    lane = iota((ROWS, LANES), 1)
    zero = jnp.zeros((ROWS, LANES), F32)

    def block(b):
        return (lane >= 8 * b) & (lane < 8 * b + 8)

    def pack(b, tiles, west, east):
        sw, se = (8 * b) % LANES, (8 * b + 8) % LANES
        w = pltpu.roll(tiles[0], sw, 1) if sw else tiles[0]
        e = pltpu.roll(tiles[1], se, 1) if se else tiles[1]
        return jnp.where(block(b), w, west), jnp.where(block(b), e, east)

    carry = (
        [zero] * 2,
        [zero] * 2,
        [[zero] * 2 for _ in range(4)],
    )
    for half in range(2):

        def down(i, carry, half=half):
            low, rat, val = carry
            level = half * 32 + i
            at = rows_of(level)
            after = jnp.minimum(level + 1, LEV - 1)
            inside = jnp.where(level < LEV - 1, 1.0, 0.0).astype(F32)
            west = east = zero
            statics = [[], [], [], []]
            nlow, nrat, nval = [], [], [[], [], [], []]
            for t in range(2):
                cols = pl.ds(t * LANES, LANES)
                w = wet[level, :, cols].astype(F32)
                wn = wet[after, :, cols].astype(F32) * inside
                d = vd[level, :, cols]
                statics[0].append(w)
                statics[1].append(flow[0, level, :, cols])
                statics[2].append(flow[1, level, :, cols])
                statics[3].append(d)
                up = d * w * wn
                inv = 1.0 / (1.0 + low[t] + up - low[t] * rat[t])
                r = up * inv
                ratio[t, at, :] = r
                nlow.append(up)
                nrat.append(r)
                for v in range(4):
                    x = (seed[level, v, :, cols] * w + low[t] * val[v][t]) * inv
                    fld[v, t, at, :] = x
                    nval[v].append(x)
            for f in range(4):
                for t in range(2):
                    fld[4 + f, t, at, :] = statics[f][t]
                west, east = pack(8 * half + 4 + f, statics[f], west, east)
            if half == 0:
                pw[i] = west
                pe[i] = east
            else:
                pw[i] = pw[i] + west
                pe[i] = pe[i] + east
            return nlow, nrat, nval

        carry = lax.fori_loop(0, 32, down, carry)

    odd = lax.rem(ids[0], 2) == 1
    follow = [[zero] * 2 for _ in range(4)]
    for half in (1, 0):

        def up(n, follow, half=half):
            i = 31 - n
            at = rows_of(half * 32 + i)
            west = east = zero
            out = []
            r = [ratio[t, at, :] for t in range(2)]
            for v in range(4):
                y = [fld[v, t, at, :] + r[t] * follow[v][t] for t in range(2)]
                for t in range(2):
                    fld[v, t, at, :] = y[t]
                west, east = pack(8 * half + v, y, west, east)
                out.append(y)
            west = pw[i] + west
            east = pe[i] + east
            if half == 1:
                pw[i] = west
                pe[i] = east
            else:
                pxa[i] = jnp.where(odd, west, east)
                pxb[i] = jnp.where(odd, east, west)
            return out

        follow = lax.fori_loop(0, 32, up, follow)


ROWS_TS = 3 * 2 * LEV + 3 * 8
ROWS_UV = 2 * 2 * LEV + 2 * 8


def edge_pack(tiles8):
    lane = iota((8, LANES), 1)
    packed = jnp.zeros((8, LANES), F32)
    for g, t in enumerate(tiles8):
        turned = pltpu.roll(t, (16 * g + 8) % LANES, 1)
        packed = jnp.where((lane >= 16 * g) & (lane < 16 * g + 16), turned, packed)
    return packed


def edge_unpack(packed, g):
    return pltpu.roll(packed, (-(16 * g + 8)) % LANES, 1)


def put_edges(todd, pick, fields, oa, ob):
    for f in range(fields):
        for t in range(2):
            for g in range(8):
                n, s = pick(f, t, g)
                at = pl.ds((f * 2 + t) * LEV + 8 * g, 8)
                oa[at, :] = jnp.where(todd, s, n)
                ob[at, :] = jnp.where(todd, n, s)
        outer = [pick(f, 2, g) for g in range(8)]
        n = edge_pack([o[0] for o in outer])
        s = edge_pack([o[1] for o in outer])
        at = pl.ds(fields * 2 * LEV + 8 * f, 8)
        oa[at, :] = jnp.where(todd, s, n)
        ob[at, :] = jnp.where(todd, n, s)


def edge_rows(ref, g):
    north = ref[pl.ds(g * 8 * ROWS + ROWS - 1, 8, stride=ROWS), :]
    south = ref[pl.ds(g * 8 * ROWS, 8, stride=ROWS), :]
    return north, south


def outer_columns(ids, xa, xb, fld, w0, w1, w2, w3, fe, ya, yb, za, zb, wloc, pieces):
    face, tile = ids[0], ids[1]
    odd = lax.rem(face, 2) == 1
    todd = lax.rem(tile, 2) == 1
    lane = iota((ROWS, LANES), 1)
    on_east = (lane < 8) & (face < 3)
    on_west = (lane >= 120) & (face > 0)

    def unpack(i, carry):
        a, b = xa[i], xb[i]
        from_west = jnp.where(odd, a, b)
        from_east = jnp.where(odd, b, a)
        for half in range(2):
            at = rows_of(half * 32 + i)
            for f in range(8):
                k = 8 * half + f
                w = pltpu.roll(from_west, (120 - 8 * k) % LANES, 1)
                e = pltpu.roll(from_east, (-8 * k) % LANES, 1)
                fe[f, at, :] = jnp.where(on_east, e, jnp.where(on_west, w, 0.0))
        return carry

    lax.fori_loop(0, 32, unpack, 0)

    def source(f, t):
        return fe.at[f] if t == 2 else fld.at[f, t]

    def pick(f, t, g):
        if f < 2:
            return edge_rows(source(f, t), g)
        wn, ws = edge_rows(source(WET, t), g)
        vn, _ = edge_rows(source(VN, t), g)
        return wn * (KAPPA - 0.5 * vn), ws

    put_edges(todd, pick, 3, ya, yb)
    put_edges(todd, lambda f, t, g: edge_rows(source(2 + f, t), g), 2, za, zb)

    for k, w in enumerate((w0, w1, w2, w3)):
        pieces[k] = w[...]
    lane4 = iota((4, LANES), 1)
    for d in range(4):
        slot = jnp.bitwise_xor(face, d)
        for c in range(2):
            for t in range(3):
                at = pl.ds(4 * d, 4)
                if t < 2:
                    first = pl.multiple_of((2 * face + t) * LANES, LANES)
                    wloc[c, t, at, :] = pieces[slot, c, :, pl.ds(first, LANES)]
                    continue
                first = pl.multiple_of(jnp.minimum(2 * face + 2, 7) * LANES, LANES)
                e = pieces[slot, c, :, pl.ds(first, LANES)]
                first = pl.multiple_of(jnp.maximum(2 * face - 1, 0) * LANES, LANES)
                w = pieces[slot, c, :, pl.ds(first, LANES)]
                w = jnp.where((lane4 >= 120) & (face > 0), w, 0.0)
                wloc[c, t, at, :] = jnp.where((lane4 < 8) & (face < 3), e, w)
    for c in range(2):
        for t in range(3):
            n = wloc[c, t, 8:16, :]
            s = wloc[c, t, 0:8, :]
            at = pl.ds(ROWS_TS + 8 * (3 * c + t), 8)
            ya[at, :] = jnp.where(todd, s, n)
            yb[at, :] = jnp.where(todd, n, s)


def coefficients(ids, fld, fe, cf):
    row = iota((ROWS, LANES), 0)
    zero = jnp.zeros((ROWS, LANES), F32)

    def body(level, carry):
        low, rat = carry
        at = rows_of(level)
        after = rows_of(jnp.minimum(level + 1, LEV - 1))
        inside = jnp.where(level < LEV - 1, 1.0, 0.0).astype(F32)

        def get(f, where):
            return [fld[f, 0, where, :], fld[f, 1, where, :], fe[f, where, :]]

        wet, ue, vn, vd = (get(f, at) for f in (WET, UE, VN, VD))
        nxt = get(WET, after)
        wet_e = east_of(wet)
        qw_w = west_of([w * (KAPPA - 0.5 * u) for w, u in zip(wet, ue)])
        nlow, nrat = [], []
        for t in range(3):
            w = wet[t]
            ce = w * (KAPPA + 0.5 * ue[t]) * wet_e[t]
            cw = w * qw_w[t]
            wn = jnp.where(row == ROWS - 1, 1.0, pltpu.roll(w, ROWS - 1, 0))
            qs = jnp.where(row == 0, 1.0, pltpu.roll(w * (KAPPA - 0.5 * vn[t]), 1, 0))
            up = vd[t] * w * nxt[t] * inside
            inv = 1.0 / (1.0 + low[t] + up - low[t] * rat[t])
            r = up * inv
            cf[0, t, at, :] = ce
            cf[1, t, at, :] = cw
            cf[2, t, at, :] = w * (KAPPA + 0.5 * vn[t]) * wn
            cf[3, t, at, :] = w * qs
            cf[4, t, at, :] = w - ce - cw
            cf[5, t, at, :] = low[t]
            cf[6, t, at, :] = inv
            cf[7, t, at, :] = r
            nlow.append(up)
            nrat.append(r)
        return nlow, nrat

    lax.fori_loop(0, LEV, body, ([zero] * 3, [zero] * 3))


def take_edges(ids, ya, yb, hn, hs, fields, groups=(0, 8)):
    todd = lax.rem(ids[1], 2) == 1
    for f in range(fields):
        outer = pl.ds(fields * 2 * LEV + 8 * f, 8)
        oa, ob = ya[outer, :], yb[outer, :]
        on, os = jnp.where(todd, ob, oa), jnp.where(todd, oa, ob)
        for g in range(*groups):
            at = pl.ds(8 * g, 8)
            for t in range(2):
                src = pl.ds((f * 2 + t) * LEV + 8 * g, 8)
                a, b = ya[src, :], yb[src, :]
                hn[f, t, at, :] = jnp.where(todd, b, a)
                hs[f, t, at, :] = jnp.where(todd, a, b)
            hn[f, 2, at, :] = edge_unpack(on, g)
            hs[f, 2, at, :] = edge_unpack(os, g)


def stencil(y, coef, north_row, south_row, row):
    e, w = east_of(y), west_of(y)
    out = []
    for t in range(3):
        n = jnp.where(row == ROWS - 1, north_row[t], pltpu.roll(y[t], ROWS - 1, 0))
        s = jnp.where(row == 0, south_row[t], pltpu.roll(y[t], 1, 0))
        ce, cw, cn, cs, cc = coef[t]
        out.append(cc * y[t] + ce * e[t] + cw * w[t] + cn * n + cs * s)
    return out


def step(first, v0, ids, fld, fe, cfi, ya, yb, *refs):
    if first:
        cf, sol, oa, ob, fo, hn, hs = refs
    else:
        sol, oa, ob, fo, hn, hs = refs
        cf = cfi
    row = iota((ROWS, LANES), 0)
    zero = jnp.zeros((ROWS, LANES), F32)
    take_edges(ids, ya, yb, hn, hs, 3 if first else 2)

    def get(v, at):
        return [fld[v0 + v, 0, at, :], fld[v0 + v, 1, at, :], fe[v0 + v, at, :]]

    north_in = jnp.where(ids[1] < 31, 1.0, 0.0).astype(F32)
    south_in = jnp.where(ids[1] > 0, 1.0, 0.0).astype(F32)

    def down(level, prev):
        at = rows_of(level)
        one = pl.ds(level, 1)
        coef = []
        for t in range(3):
            ce, cw, cn, cs, cc = (cfi[k, t, at, :] for k in range(5))
            if first:
                cn = jnp.where(row == ROWS - 1, cn * (hn[2, t, one, :] * north_in), cn)
                cs = jnp.where(row == 0, cs * (hs[2, t, one, :] * south_in), cs)
                cc = cc - cn - cs
                cf[0, t, at, :] = ce
                cf[1, t, at, :] = cw
                cf[2, t, at, :] = cn
                cf[3, t, at, :] = cs
                cf[4, t, at, :] = cc
            coef.append((ce, cw, cn, cs, cc))
        out = []
        for v in range(2):
            y = get(v, at)
            n = [hn[v, t, one, :] for t in range(3)]
            s = [hs[v, t, one, :] for t in range(3)]
            adj = stencil(y, coef, n, s, row)
            new = []
            for t in range(3):
                x = (adj[t] + cfi[5, t, at, :] * prev[v][t]) * cfi[6, t, at, :]
                sol[v, t, at, :] = x
                new.append(x)
            out.append(new)
        return out

    lax.fori_loop(0, LEV, down, [[zero] * 3 for _ in range(2)])

    def up(n, follow):
        at = rows_of(LEV - 1 - n)
        out = [[], []]
        for t in range(3):
            r = cfi[7, t, at, :]
            for v in range(2):
                y = sol[v, t, at, :] + r * follow[v][t]
                sol[v, t, at, :] = y
                out[v].append(y)
        return out

    top = lax.fori_loop(0, LEV, up, [[zero] * 3 for _ in range(2)])
    for v in range(2):
        y = get(v, pl.ds(0, ROWS))
        for t in range(3):
            fo[v, t] = y[t] + top[v][t]
    todd = lax.rem(ids[1], 2) == 1
    put_edges(todd, lambda f, t, g: edge_rows(sol.at[f, t], g), 2, oa, ob)


def last_stencil(v0, l0, nl, extra, grads, *refs):
    ids, sol, cf, ya, yb = refs[:5]
    refs = refs[5:]
    fos = refs[:extra]
    refs = refs[extra:]
    if l0 or v0:
        refs = refs[1:]
    if grads:
        adj_out, g, ga, gb, hn, hs, en, es, buf, sem = refs
    else:
        adj_out, hn, hs, buf, sem = refs
    row = iota((ROWS, LANES), 0)
    low_half = iota((8, LANES), 0) < 4
    todd = lax.rem(ids[1], 2) == 1
    take_edges(ids, ya, yb, hn, hs, 2, (l0 // 8, (l0 + nl) // 8))

    def edges(u, ts, ss):
        for t in range(3):
            a, b = ts[t], ss[t]
            n = jnp.where(low_half, pltpu.roll(a[8:16], 4, 0), b[8:16])
            s = jnp.where(low_half, a[0:8], pltpu.roll(b[0:8], 4, 0))
            if t < 2:
                ga[2 * u + t] = jnp.where(todd, s, n)
                gb[2 * u + t] = jnp.where(todd, n, s)
            else:
                en[u] = n
                es[u] = s

    def body(u, carry):
        level = l0 + u
        at = rows_of(level)
        one = pl.ds(level, 1)
        coef = [tuple(cf[k, t, at, :] for k in range(5)) for t in range(3)]
        both = []
        for v in range(2):
            y = [sol[v, t, at, :] for t in range(3)]
            n = [hn[v, t, one, :] for t in range(3)]
            s = [hs[v, t, one, :] for t in range(3)]
            x = stencil(y, coef, n, s, row)
            buf[u, v, :, 0:LANES] = x[0]
            buf[u, v, :, LANES : 2 * LANES] = x[1]
            if grads:
                for t in range(3):
                    g[u, v, t] = x[t]
            both.append(x)
        if grads:
            edges(u, *both)
        return carry

    lax.fori_loop(0, nl, body, 0)
    copy = pltpu.make_async_copy(buf, adj_out.at[pl.ds(l0, nl), pl.ds(v0, 2)], sem)
    copy.start()
    if grads:
        for i, fo in enumerate(fos):
            pair = [[fo[v, t] for t in range(3)] for v in range(2)]
            for v in range(2):
                for t in range(3):
                    g[nl + i, v, t] = pair[v][t]
            edges(nl + i, *pair)
        units = nl + extra
        per = -(-units // 8)
        lane = iota((8, LANES), 1)
        for i in range(per):
            pn = ps = jnp.zeros((8, LANES), F32)
            for j in range(8):
                u = j * per + i
                if u < units:
                    mine = (lane >= 16 * j) & (lane < 16 * j + 16)
                    pn = jnp.where(mine, pltpu.roll(en[u], (16 * j + 8) % LANES, 1), pn)
                    ps = jnp.where(mine, pltpu.roll(es[u], (16 * j + 8) % LANES, 1), ps)
            ga[2 * units + i] = jnp.where(todd, ps, pn)
            gb[2 * units + i] = jnp.where(todd, pn, ps)
    copy.wait()


def smooth(units, ids, g, ga, gb, wloc, ya, yb, z0, z1, z2, z3, w5, hn, hs):
    zs = (z0, z1, z2, z3)
    face, tile = ids[0], ids[1]
    todd = lax.rem(tile, 2) == 1
    has_n, has_s = tile < 31, tile > 0
    sub = iota((8, LANES), 0)
    lane = iota((8, LANES), 1)
    low_half = sub < 4

    def stack3(lo, m0, m1, hi):
        r0, r1 = pltpu.roll(m0, 4, 0), pltpu.roll(m1, 4, 0)
        return [
            jnp.where(low_half, lo, r0),
            jnp.where(low_half, r0, r1),
            jnp.where(low_half, r1, hi),
        ]

    def north_of(k3):
        turned = [pltpu.roll(x, 7, 0) for x in k3]
        return [
            jnp.where(sub == 7, turned[1], turned[0]),
            jnp.where(sub == 7, turned[2], turned[1]),
            turned[2],
        ]

    def south_of(k3, below=None):
        turned = [pltpu.roll(x, 1, 0) for x in k3]
        return [
            turned[0] if below is None else jnp.where(sub == 0, below, turned[0]),
            jnp.where(sub == 0, turned[0], turned[1]),
            jnp.where(sub == 0, turned[1], turned[2]),
        ]

    we, wn, below = [], [], []
    for c, dest in ((0, we), (1, wn)):
        for t in range(3):
            at = pl.ds(ROWS_TS + 8 * (3 * c + t), 8)
            a, b = ya[at, :], yb[at, :]
            hi = jnp.where(has_n, jnp.where(todd, b, a), 0.0)
            lo = jnp.where(has_s, jnp.where(todd, a, b), 0.0)
            if c == 1:
                below.append(pltpu.roll(lo, 5, 0))
            dest.append(
                stack3(pltpu.roll(lo, 4, 0), wloc[c, t, 0:8, :], wloc[c, t, 8:16, :], pltpu.roll(hi, 4, 0))
            )
    for k in range(3):
        cw3 = west_of([we[t][k] for t in range(3)])
        for t in range(3):
            ok = jnp.ones((8, LANES), F32)
            if k == 0:
                ok = jnp.where(low_half & (tile == 0), 0.0, ok)
            if k == 2:
                ok = jnp.where((~low_half) & (tile == 31), 0.0, ok)
            if t == 2:
                inside = ((lane < 64) & (face < 3)) | ((lane >= 64) & (face > 0))
                ok = jnp.where(inside, ok, 0.0)
            ce = we[t][k] * ok
            cw = cw3[t] * ok
            cn = wn[t][k] * ok
            cs = south_of(wn[t], below[t])[k] * ok
            w5[0, t, k] = ce
            w5[1, t, k] = cw
            w5[2, t, k] = cn
            w5[3, t, k] = cs
            w5[4, t, k] = 1.0 - ce - cw - cn - cs

    per = -(-units // 8)
    for u in range(units):
        j, i = divmod(u, per)
        a, b = ga[2 * units + i], gb[2 * units + i]
        n = edge_unpack(jnp.where(todd, b, a), j)
        s = edge_unpack(jnp.where(todd, a, b), j)
        hn[u] = jnp.where(has_n, n, 0.0)
        hs[u] = jnp.where(has_s, s, 0.0)

    bit0 = lax.rem(face, 2) == 1
    bit1 = face >= 2

    def body(u, carry):
        hi, lo = [], []
        for t in range(2):
            a, b = ga[2 * u + t], gb[2 * u + t]
            hi.append(jnp.where(has_n, jnp.where(todd, b, a), 0.0))
            lo.append(jnp.where(has_s, jnp.where(todd, a, b), 0.0))
        hi.append(hn[u])
        lo.append(hs[u])
        for v in range(2):
            x = []
            for t in range(3):
                m = g[u, v, t]
                top = pltpu.roll(hi[t], 4, 0) if v == 0 else hi[t]
                bottom = lo[t] if v == 0 else pltpu.roll(lo[t], 4, 0)
                x.append(stack3(bottom, m[0:8], m[8:16], top))
            for _ in range(4):
                ns = [north_of(x[t]) for t in range(3)]
                ss = [south_of(x[t]) for t in range(3)]
                new = [[], [], []]
                for k in range(3):
                    at_k = [x[t][k] for t in range(3)]
                    e, w = east_of(at_k), west_of(at_k)
                    for t in range(3):
                        new[t].append(
                            w5[4, t, k] * x[t][k]
                            + w5[0, t, k] * e[t]
                            + w5[1, t, k] * w[t]
                            + w5[2, t, k] * ns[t][k]
                            + w5[3, t, k] * ss[t][k]
                        )
                x = new
            for t in range(2):
                p = [pltpu.roll(x[t][0], 4, 0), x[t][1], pltpu.roll(x[t][1], 4, 0), x[t][2]]
                p = [jnp.where(bit0, p[d ^ 1], p[d]) for d in range(4)]
                p = [jnp.where(bit1, p[d ^ 2], p[d]) for d in range(4)]
                for k in range(4):
                    zs[k][2 * u + v, :, t * LANES : (t + 1) * LANES] = p[k][0:4]
        return carry

    lax.fori_loop(0, units, body, 0)


def gather_rows(sizes, ids, *refs):
    face = ids[0]
    n = len(sizes)
    out, sem = refs[4 * n], refs[4 * n + 1]
    copies = []
    first = 0
    for c, size in enumerate(sizes):
        for k in range(4):
            cols = pl.multiple_of(jnp.bitwise_xor(face, k) * 256, 256)
            copies.append(
                pltpu.make_async_copy(
                    refs[4 * c + k],
                    out.at[pl.ds(first, size), :, pl.ds(cols, 256)],
                    sem.at[c, k],
                )
            )
        first += size
    for copy in copies:
        copy.start()
    for copy in copies:
        copy.wait()


def on_device(adjoint_seed, face_flow, vert_diff, wet_mask, smooth_weights):
    ids = jnp.stack([lax.axis_index("face"), lax.axis_index("tile")]).astype(jnp.int32)
    tiles = lax.axis_size("tile")
    pair_a = [(i, i ^ 1) for i in range(tiles)]
    pair_b = [(0, 0), (tiles - 1, tiles - 1)]
    for i in range(1, tiles - 1, 2):
        pair_b += [(i, i + 1), (i + 1, i)]
    side_a = [(0, 1), (1, 0), (2, 3), (3, 2)]
    side_b = [(0, 0), (1, 2), (2, 1), (3, 3)]

    def across(a, b):
        return lax.ppermute(a, "tile", pair_a), lax.ppermute(b, "tile", pair_b)

    def to_face(x, k):
        return lax.ppermute(x, "face", [(i, i ^ k) for i in range(4)])

    weights = [smooth_weights] + [to_face(smooth_weights, k) for k in (1, 2, 3)]
    edge = (ROWS, LANES)
    fld, pxa, pxb = call(
        first_solve,
        [((8, 2, FLAT, LANES), VM), ((32,) + edge, VM), ((32,) + edge, VM)],
        [VM((2, FLAT, LANES), F32), VM((32,) + edge, F32), VM((32,) + edge, F32)],
        limit=4,
        name="first_solve",
    )(ids, adjoint_seed, face_flow, vert_diff, wet_mask)
    xa = lax.ppermute(pxa, "face", side_a)
    xb = lax.ppermute(pxb, "face", side_b)
    rows_ts = ROWS_TS + 48
    fe, ya, yb, za, zb, wloc = call(
        outer_columns,
        [
            ((8, FLAT, LANES), VM),
            ((rows_ts, LANES), VM),
            ((rows_ts, LANES), VM),
            ((ROWS_UV, LANES), VM),
            ((ROWS_UV, LANES), VM),
            ((2, 3) + edge, VM),
        ],
        [VM((4, 2, 4, 1024), F32)],
        limit=4,
        name="outer_columns",
    )(ids, xa, xb, fld, *weights)
    ya, yb = across(ya, yb)
    za, zb = across(za, zb)
    (cf,) = call(coefficients, [((8, 3, FLAT, LANES), VM)], limit=4, name="coefficients")(ids, fld, fe)
    halo = VM((3, 3, LEV, LANES), F32)
    after = [
        ((2, 3, FLAT, LANES), VM),
        ((ROWS_UV, LANES), VM),
        ((ROWS_UV, LANES), VM),
        ((2, 3) + edge, VM),
    ]
    cf, sol_t, ta, tb, fo_t = call(
        functools.partial(step, True, 0),
        [((8, 3, FLAT, LANES), VM)] + after,
        [halo, halo],
        limit=4,
        alias={3: 0},
        name="step_ts",
    )(ids, fld, fe, cf, ya, yb)
    ta, tb = across(ta, tb)
    sol_u, ua, ub, fo_u = call(
        functools.partial(step, False, 2), after, [halo, halo], limit=4, name="step_uv"
    )(ids, fld, fe, cf, za, zb)
    ua, ub = across(ua, ub)

    adj_shape = adjoint_seed.shape
    adj = None
    sent = []
    sizes = []
    for l0, l1 in CHUNKS:
        nl = l1 - l0
        fos = [fo_t, fo_u] if l1 == LEV else []
        units = nl + len(fos)
        per = -(-units // 8)
        args = [ids, sol_t, cf, ta, tb] + fos
        spaces = [None] + [VM] * (len(args) - 1)
        alias = {}
        if adj is not None:
            alias = {len(args): 0}
            args.append(adj)
            spaces.append(pl.ANY)
        adj, g, ga, gb = call(
            functools.partial(last_stencil, 0, l0, nl, len(fos), True),
            [
                (adj_shape, pl.ANY),
                ((units, 2, 3) + edge, VM),
                ((2 * units + per, 8, LANES), VM),
                ((2 * units + per, 8, LANES), VM),
            ],
            [
                halo,
                halo,
                VM((units, 8, LANES), F32),
                VM((units, 8, LANES), F32),
                VM((nl, 2, ROWS, 256), F32),
                pltpu.SemaphoreType.DMA,
            ],
            limit=6,
            alias=alias,
            ins=spaces,
            name="last_ts_%d" % l0,
        )(*args)
        ga, gb = across(ga, gb)
        zs = call(
            functools.partial(smooth, units),
            [((2 * units, 4, 256), VM)] * 4,
            [
                VM((5, 3, 3, 8, LANES), F32),
                VM((units, 8, LANES), F32),
                VM((units, 8, LANES), F32),
            ],
            limit=4,
            name="smooth_%d" % l0,
        )(ids, g, ga, gb, wloc, ya, yb)
        sent.append([zs[0]] + [to_face(zs[k], k) for k in (1, 2, 3)])
        sizes.append(2 * units)
    (adj,) = call(
        functools.partial(last_stencil, 2, 0, LEV, 0, False),
        [(adj_shape, pl.ANY)],
        [halo, halo, VM((LEV, 2, ROWS, 256), F32), pltpu.SemaphoreType.DMA],
        limit=6,
        alias={5: 0},
        ins=[None] + [VM] * 4 + [pl.ANY],
        name="last_uv",
    )(ids, sol_u, cf, ua, ub, adj)
    flat = [x for group in sent for x in group]
    (controls,) = call(
        functools.partial(gather_rows, tuple(sizes)),
        [((sum(sizes), 4, 1024), pl.ANY)],
        [pltpu.SemaphoreType.DMA((len(sizes), 4))],
        ins=[None] + [pl.ANY] * len(flat),
        limit=4,
        name="gather_rows",
    )(ids, *flat)
    return adj, controls


def solution(mesh):
    placed = (
        P(None, None, "tile", "face"),
        P(None, None, "tile", "face"),
        P(None, "tile", "face"),
        P(None, "tile", "face"),
        P(None, ("tile", "face"), None),
    )
    return jax.shard_map(
        on_device,
        mesh=mesh,
        in_specs=placed,
        out_specs=(P(None, None, "tile", "face"), P(None, ("tile", "face"), None)),
        check_vma=False,
    )
```

```python
import functools

import jax
import jax.numpy as jnp
from jax import lax
from jax.experimental import pallas as pl
from jax.experimental.pallas import tpu as pltpu
from jax.sharding import PartitionSpec as P

F32 = jnp.float32
LEV = 64
ROWS = 16
LANES = 128
FLAT = LEV * ROWS
WET, UE, VN, VD = 4, 5, 6, 7
KAPPA = 0.15
MIB = 2**20
UNROLL_C = 4
UNROLL_S = 4
UNROLL_L = 4
UNROLL_M = 2

CHUNKS = ((0, 24), (24, 64))
PIECES = ((0, 0, 24), (1, 0, 22), (1, 22, 42))


def iota(shape, dim):
    return lax.broadcasted_iota(jnp.int32, shape, dim)


def rows_of(level):
    return pl.ds(pl.multiple_of(level * ROWS, ROWS), ROWS)


def east_of(tiles):
    last = iota(tiles[0].shape, 1) == LANES - 1
    turned = [pltpu.roll(t, LANES - 1, 1) for t in tiles]
    return [jnp.where(last, turned[(i + 1) % 3], turned[i]) for i in range(3)]


def west_of(tiles):
    first = iota(tiles[0].shape, 1) == 0
    turned = [pltpu.roll(t, 1, 1) for t in tiles]
    return [jnp.where(first, turned[(i + 2) % 3], turned[i]) for i in range(3)]


def call(kernel, outs, scratch=(), limit=8, alias=None, name=None, ins=None):
    def run(*args):
        args = list(args)
        specs = [pl.BlockSpec(memory_space=pltpu.SMEM)]
        for i in range(1, len(args)):
            if ins is not None and ins[i] is pltpu.HBM:
                args[i] = pltpu.with_memory_space_constraint(args[i], pltpu.HBM)
        for i in range(1, len(args)):
            space = pltpu.VMEM if ins is None else ins[i]
            specs.append(pl.BlockSpec(memory_space=space))
        return pl.pallas_call(
            kernel,
            out_shape=[jax.ShapeDtypeStruct(s, F32) for s, _ in outs],
            in_specs=specs,
            out_specs=[pl.BlockSpec(memory_space=m) for _, m in outs],
            scratch_shapes=list(scratch),
            input_output_aliases=alias or {},
            compiler_params=pltpu.CompilerParams(vmem_limit_bytes=limit * MIB),
            name=name,
        )(*args)

    return run


VM = pltpu.VMEM


HALF = LEV // 2


def pair_of(i):
    return rows_of(i), rows_of(LEV - 1 - i)


def thirds(tri, wet, vd, tiles, beside=None):
    zero = jnp.zeros((ROWS, LANES), F32)

    def body(i, carry):
        low, rat, low2, rat2 = ([], [], [], [])
        top, bottom = pair_of(i)
        for t in tiles:
            w = wet(t, i)
            up = vd(t, i) * w * wet(t, i + 1)
            p, q = carry[0][t - tiles[0]], carry[1][t - tiles[0]]
            inv = 1.0 / (1.0 + p + up - p * q)
            r = up * inv
            tri[0, t - tiles[0], top, :] = p
            tri[1, t - tiles[0], top, :] = inv
            tri[2, t - tiles[0], top, :] = r
            low.append(up)
            rat.append(r)
            j = LEV - 1 - i
            up = vd(t, j - 1) * wet(t, j - 1) * wet(t, j)
            p, q = carry[2][t - tiles[0]], carry[3][t - tiles[0]]
            inv = 1.0 / (1.0 + p + up - p * q)
            r = up * inv
            tri[0, t - tiles[0], bottom, :] = p
            tri[1, t - tiles[0], bottom, :] = inv
            tri[2, t - tiles[0], bottom, :] = r
            low2.append(up)
            rat2.append(r)
        if beside is not None:
            beside(i)
        return low, rat, low2, rat2

    n = len(tiles)
    lax.fori_loop(0, HALF, body, tuple([zero] * n for _ in range(4)))


def eliminate(rhs, put, get, tri, items, beside=None):
    zero = jnp.zeros((ROWS, LANES), F32)
    n = len(items)

    def inwards(i, carry):
        out = ([], [])
        for side, at in enumerate(pair_of(i)):
            for c, (key, t) in enumerate(items):
                x = (rhs(key, t, at) + tri(0, t, at) * carry[side][c]) * tri(1, t, at)
                put(key, t, at, x)
                out[side].append(x)
        return out

    ends = lax.fori_loop(0, HALF, inwards, ([zero] * n, [zero] * n))
    at, bt = pair_of(HALF - 1)
    start = ([], [])
    for c, (key, t) in enumerate(items):
        r, r2 = tri(2, t, at), tri(2, t, bt)
        y = (ends[0][c] + r * ends[1][c]) * (1.0 / (1.0 - r * r2))
        y2 = ends[1][c] + r2 * y
        put(key, t, at, y)
        put(key, t, bt, y2)
        start[0].append(y)
        start[1].append(y2)
    if beside is not None:
        beside(HALF - 1, start)

    def outwards(k, carry):
        out = ([], [])
        for side, at in enumerate(pair_of(HALF - 2 - k)):
            for c, (key, t) in enumerate(items):
                x = get(key, t, at) + tri(2, t, at) * carry[side][c]
                put(key, t, at, x)
                out[side].append(x)
        if beside is not None:
            beside(HALF - 2 - k, out)
        return out

    return lax.fori_loop(0, HALF - 1, outwards, start)


def first_solve(ids, seed, flow, vd, wet, fld, tri, pxa, pxb, wbuf, pw, pe, sems):
    def tile_copy(src, dst, k):
        copy = pltpu.make_async_copy(src, dst, sems.at[k])
        copy.start()
        return copy

    def place(f, t):
        return fld.at[f, t].reshape(LEV, ROWS, LANES)

    early, late = [], []
    for t in range(2):
        cols = pl.ds(t * LANES, LANES)
        early.append(tile_copy(wet.at[:, :, cols], wbuf.at[t], 8 * t))
        early.append(tile_copy(vd.at[:, :, cols], place(VD, t), 8 * t + 1))
        for v in range(2):
            early.append(tile_copy(flow.at[v, :, :, cols], place(UE + v, t), 8 * t + 2 + v))
    for t in range(2):
        cols = pl.ds(t * LANES, LANES)
        for v in range(4):
            late.append(tile_copy(seed.at[:, v, :, cols], place(v, t), 8 * t + 4 + v))
    for copy in early:
        copy.wait()

    def wet_to_float(i, carry):
        for k in range(8):
            for t in range(2):
                fld[WET, t, rows_of(8 * i + k), :] = wbuf[t, 8 * i + k].astype(F32)
        return carry

    lax.fori_loop(0, LEV // 8, wet_to_float, 0)
    lane = iota((ROWS, LANES), 1)
    zero = jnp.zeros((ROWS, LANES), F32)
    odd = lax.rem(ids[0], 2) == 1

    def pack(values):
        west = east = zero
        for b, x0, x1 in values:
            mine = (lane >= 8 * b) & (lane < 8 * b + 8)
            west = jnp.where(mine, pltpu.roll(x0, 8 * b, 1) if b else x0, west)
            s = (8 * b + 8) % LANES
            east = jnp.where(mine, pltpu.roll(x1, s, 1) if s else x1, east)
        return west, east

    def statics(i):
        values = []
        for half, at in enumerate(pair_of(i)):
            for f in range(4, 8):
                values.append((8 * half + f, fld[f, 0, at, :], fld[f, 1, at, :]))
        west, east = pack(values)
        pw[rows_of(i), :] = west
        pe[rows_of(i), :] = east

    thirds(
        tri,
        lambda t, level: fld[WET, t, rows_of(level), :],
        lambda t, level: fld[VD, t, rows_of(level), :],
        (0, 1),
        statics,
    )
    for copy in late:
        copy.wait()

    def put(v, t, at, x):
        fld[v, t, at, :] = x

    for pair in ((0, 1), (2, 3)):

        def solved(i, out, pair=pair):
            values = []
            for half in range(2):
                for c, v in enumerate(pair):
                    values.append((8 * half + v, out[half][2 * c], out[half][2 * c + 1]))
            west, east = pack(values)
            at = rows_of(i)
            west = pw[at, :] + west
            east = pe[at, :] + east
            if pair[0] == 0:
                pw[at, :] = west
                pe[at, :] = east
            else:
                pxa[at, :] = jnp.where(odd, west, east)
                pxb[at, :] = jnp.where(odd, east, west)

        eliminate(
            lambda v, t, at: fld[v, t, at, :] * fld[WET, t, at, :],
            put,
            lambda v, t, at: fld[v, t, at, :],
            lambda k, t, at: tri[k, t, at, :],
            [(v, t) for v in pair for t in range(2)],
            solved,
        )


OUTER = 5 * 2 * LEV
ROWS_1 = OUTER + LEV
ROWS_2 = 2 * 2 * LEV + 2 * 8
BLOCKS_2 = ROWS_2 // 8


def edge_pack(tiles8):
    lane = iota((8, LANES), 1)
    packed = jnp.zeros((8, LANES), F32)
    for g, t in enumerate(tiles8):
        turned = pltpu.roll(t, (16 * g + 8) % LANES, 1)
        packed = jnp.where((lane >= 16 * g) & (lane < 16 * g + 16), turned, packed)
    return packed


def edge_unpack(packed, g):
    return pltpu.roll(packed, (-(16 * g + 8)) % LANES, 1)


def put_edges(todd, pick, fields, oa, ob):
    for f in range(fields):
        for t in range(2):
            for g in range(8):
                n, s = pick(f, t, g)
                at = pl.ds((f * 2 + t) * LEV + 8 * g, 8)
                oa[at, :] = jnp.where(todd, s, n)
                ob[at, :] = jnp.where(todd, n, s)
        outer = [pick(f, 2, g) for g in range(8)]
        n = edge_pack([o[0] for o in outer])
        s = edge_pack([o[1] for o in outer])
        at = pl.ds(fields * 2 * LEV + 8 * f, 8)
        oa[at, :] = jnp.where(todd, s, n)
        ob[at, :] = jnp.where(todd, n, s)


def edge_rows(ref, g):
    north = ref[pl.ds(g * 8 * ROWS + ROWS - 1, 8, stride=ROWS), :]
    south = ref[pl.ds(g * 8 * ROWS, 8, stride=ROWS), :]
    return north, south


def main_edges(ids, fld, ya, yb):
    todd = lax.rem(ids[1], 2) == 1
    for k, f in enumerate((0, 1, WET, 2, 3)):
        for t in range(2):
            for g in range(8):
                n, s = edge_rows(fld.at[f, t], g)
                if f == WET:
                    n = n * (KAPPA - 0.5 * edge_rows(fld.at[VN, t], g)[0])
                at = pl.ds((2 * k + t) * LEV + 8 * g, 8)
                ya[at, :] = jnp.where(todd, s, n)
                yb[at, :] = jnp.where(todd, n, s)


def outer_edges(ids, xa, xb, ya_in, yb_in, ya, yb):
    face, tile = ids[0], ids[1]
    odd = lax.rem(face, 2) == 1
    todd = lax.rem(tile, 2) == 1
    for g in range(4):
        na, sa = edge_rows(xa, g)
        nb, sb = edge_rows(xb, g)
        west = (jnp.where(odd, na, nb), jnp.where(odd, sa, sb))
        east = (jnp.where(odd, nb, na), jnp.where(odd, sb, sa))
        for first, inside, (n, s) in ((0, face > 0, west), (HALF, face < 3, east)):
            n = jnp.where(inside, n, 0.0)
            s = jnp.where(inside, s, 0.0)
            at = pl.ds(OUTER + first + 8 * g, 8)
            ya[at, :] = jnp.where(todd, s, n)
            yb[at, :] = jnp.where(todd, n, s)


def local_weights(ids, w0, w1, w2, w3, wloc, pieces):
    face = ids[0]
    for k, w in enumerate((w0, w1, w2, w3)):
        pieces[k] = w[...]
    lane4 = iota((4, LANES), 1)
    for d in range(4):
        slot = jnp.bitwise_xor(face, d)
        for c in range(2):
            for t in range(3):
                at = pl.ds(4 * d, 4)
                if t < 2:
                    first = pl.multiple_of((2 * face + t) * LANES, LANES)
                    wloc[c, t, at, :] = pieces[slot, c, :, pl.ds(first, LANES)]
                    continue
                first = pl.multiple_of(jnp.minimum(2 * face + 2, 7) * LANES, LANES)
                e = pieces[slot, c, :, pl.ds(first, LANES)]
                first = pl.multiple_of(jnp.maximum(2 * face - 1, 0) * LANES, LANES)
                w = pieces[slot, c, :, pl.ds(first, LANES)]
                w = jnp.where((lane4 >= 120) & (face > 0), w, 0.0)
                wloc[c, t, at, :] = jnp.where((lane4 < 8) & (face < 3), e, w)


def coefficients(ids, fld, xa, xb, fe, cf, tri):
    row = iota((ROWS, LANES), 0)
    face = ids[0]
    odd = lax.rem(face, 2) == 1
    lane = iota((ROWS, LANES), 1)
    on_east = (lane < 8) & (face < 3)
    on_west = (lane >= 120) & (face > 0)

    def unpack(n, carry):
        for i in (2 * n, 2 * n + 1):
            a, b = xa[rows_of(i), :], xb[rows_of(i), :]
            from_west = jnp.where(odd, a, b)
            from_east = jnp.where(odd, b, a)
            for half, at in enumerate(pair_of(i)):
                for f in range(8):
                    k = 8 * half + f
                    w = pltpu.roll(from_west, (120 - 8 * k) % LANES, 1)
                    e = pltpu.roll(from_east, (-8 * k) % LANES, 1)
                    fe[f, at, :] = jnp.where(on_east, e, jnp.where(on_west, w, 0.0))
        return carry

    lax.fori_loop(0, HALF // 2, unpack, 0)
    thirds(
        tri,
        lambda t, level: fe[WET, rows_of(level), :],
        lambda t, level: fe[VD, rows_of(level), :],
        (2,),
    )

    def body(i, carry):
        for k in range(UNROLL_C):
            at = rows_of(UNROLL_C * i + k)

            def get(f):
                return [fld[f, 0, at, :], fld[f, 1, at, :], fe[f, at, :]]

            wet, ue, vn = (get(f) for f in (WET, UE, VN))
            wet_e = east_of(wet)
            qw_w = west_of([w * (KAPPA - 0.5 * u) for w, u in zip(wet, ue)])
            for t in range(3):
                w = wet[t]
                ce = w * (KAPPA + 0.5 * ue[t]) * wet_e[t]
                cw = w * qw_w[t]
                wn = jnp.where(row == ROWS - 1, 1.0, pltpu.roll(w, ROWS - 1, 0))
                qs = jnp.where(row == 0, 1.0, pltpu.roll(w * (KAPPA - 0.5 * vn[t]), 1, 0))
                cf[0, t, at, :] = ce
                cf[1, t, at, :] = cw
                cf[2, t, at, :] = w * (KAPPA + 0.5 * vn[t]) * wn
                cf[3, t, at, :] = w * qs
                cf[4, t, at, :] = w - ce - cw
        return carry

    lax.fori_loop(0, LEV // UNROLL_C, body, 0)


def slot_of(level):
    return jnp.where(level < HALF, level, LEV + HALF - 1 - level)


def take_first_edges(ids, ya, yb, hn, hs, first):
    todd = lax.rem(ids[1], 2) == 1
    lane = iota((8, LANES), 1)

    def both(at):
        a, b = ya[at, :], yb[at, :]
        return jnp.where(todd, b, a), jnp.where(todd, a, b)

    for f, k in enumerate((0, 1, 2) if first else (3, 4)):
        for t in range(2):
            for g in range(8):
                at = pl.ds(8 * g, 8)
                n, s = both(pl.ds((2 * k + t) * LEV + 8 * g, 8))
                hn[f, t, at, :] = n
                hs[f, t, at, :] = s
    for g in range(4):
        wests = both(pl.ds(OUTER + 8 * g, 8))
        easts = both(pl.ds(OUTER + HALF + 8 * g, 8))
        for half in range(2):

            def outer(side, f):
                b = 8 * half + f
                w = pltpu.roll(wests[side], (120 - 8 * b) % LANES, 1)
                e = pltpu.roll(easts[side], (-8 * b) % LANES, 1)
                return jnp.where(lane < 64, e, w)

            at = pl.ds(HALF * half + 8 * g, 8)
            for f, k in enumerate((0, 1) if first else (2, 3)):
                hn[f, 2, at, :] = outer(0, k)
                hs[f, 2, at, :] = outer(1, k)
            if first:
                hn[2, 2, at, :] = outer(0, WET)
                hs[2, 2, at, :] = outer(1, WET) * (KAPPA - 0.5 * outer(1, VN))


def take_edges(ids, load, hn, hs, groups=(0, 8)):
    todd = lax.rem(ids[1], 2) == 1
    for f in range(2):
        oa, ob = load(32 + f)
        on, os = jnp.where(todd, ob, oa), jnp.where(todd, oa, ob)
        for g in range(*groups):
            at = pl.ds(8 * g, 8)
            for t in range(2):
                a, b = load((f * 2 + t) * 8 + g)
                hn[f, t, at, :] = jnp.where(todd, b, a)
                hs[f, t, at, :] = jnp.where(todd, a, b)
            hn[f, 2, at, :] = edge_unpack(on, g)
            hs[f, 2, at, :] = edge_unpack(os, g)


def stencil(y, coef, north_row, south_row, row, tiles=3):
    e, w = east_of(y), west_of(y)
    out = []
    for t in range(tiles):
        n = jnp.where(row == ROWS - 1, north_row[t], pltpu.roll(y[t], ROWS - 1, 0))
        s = jnp.where(row == 0, south_row[t], pltpu.roll(y[t], 1, 0))
        ce, cw, cn, cs, cc = coef[t]
        out.append(cc * y[t] + ce * e[t] + cw * w[t] + cn * n + cs * s)
    return out


def step(first, v0, ids, fld, fe, cfi, trm, tre, ya, yb, *refs):
    if first:
        wloc, cf, sol, oa, ob, fo, hn, hs = refs
    else:
        sol, oa, ob, fo, hn, hs = refs
    row = iota((ROWS, LANES), 0)
    take_first_edges(ids, ya, yb, hn, hs, first)

    def get(v, at):
        return [fld[v0 + v, 0, at, :], fld[v0 + v, 1, at, :], fe[v0 + v, at, :]]

    north_in = jnp.where(ids[1] < 31, 1.0, 0.0).astype(F32)
    south_in = jnp.where(ids[1] > 0, 1.0, 0.0).astype(F32)

    def apply(i, carry):
        for k in range(UNROLL_S):
            level = UNROLL_S * i + k
            at = rows_of(level)
            ones = [pl.ds(level, 1), pl.ds(level, 1), pl.ds(slot_of(level), 1)]
            coef = []
            for t in range(3):
                ce, cw, cn, cs, cc = (cfi[c, t, at, :] for c in range(5))
                if first:
                    cn = jnp.where(row == ROWS - 1, cn * (hn[2, t, ones[t], :] * north_in), cn)
                    cs = jnp.where(row == 0, cs * (hs[2, t, ones[t], :] * south_in), cs)
                    cc = cc - cn - cs
                    cf[2, t, at, :] = cn
                    cf[3, t, at, :] = cs
                    cf[4, t, at, :] = cc
                coef.append((ce, cw, cn, cs, cc))
            for v in range(2):
                n = [hn[v, t, ones[t], :] for t in range(3)]
                s = [hs[v, t, ones[t], :] for t in range(3)]
                adj = stencil(get(v, at), coef, n, s, row)
                for t in range(3):
                    sol[v, t, at, :] = adj[t]
        return carry

    lax.fori_loop(0, LEV // UNROLL_S, apply, 0)

    def put(v, t, at, x):
        sol[v, t, at, :] = x

    def load(v, t, at):
        return sol[v, t, at, :]

    top = eliminate(
        load,
        put,
        load,
        lambda k, t, at: tre[k, 0, at, :] if t == 2 else trm[k, t, at, :],
        [(v, t) for v in range(2) for t in range(3)],
    )[0]
    for v in range(2):
        y = get(v, pl.ds(0, ROWS))
        for t in range(3):
            fo[v, t] = y[t] + top[3 * v + t]
    todd = lax.rem(ids[1], 2) == 1
    put_edges(todd, lambda f, t, g: edge_rows(sol.at[f, t], g), 2, oa, ob)
    if first:
        for c in range(2):
            for t in range(3):
                n = wloc[c, t, 8:16, :]
                s = wloc[c, t, 0:8, :]
                at = pl.ds(ROWS_2 + 8 * (3 * c + t), 8)
                oa[at, :] = jnp.where(todd, s, n)
                ob[at, :] = jnp.where(todd, n, s)


def last_stencil(v0, l0, nl, extra, carried, grads, *refs):
    ids, sol, cf, ya, yb = refs[:5]
    refs = refs[5:]
    fos = refs[:extra]
    refs = refs[extra:]
    if grads and carried:
        ua, ub = refs[:2]
        refs = refs[2:]
    if not grads:
        refs = refs[1:]
    if l0 or v0:
        refs = refs[1:]
    if grads:
        adj_out, g, ga, gb, hn, hs, en, es, buf, sem = refs
    else:
        adj_out, hn, hs, buf, sem = refs
    row = iota((ROWS, LANES), 0)
    low_half = iota((8, LANES), 0) < 4
    todd = lax.rem(ids[1], 2) == 1

    def load(block):
        if not grads:
            return ya[carried + block], yb[carried + block]
        at = pl.ds(8 * block, 8)
        return ya[at, :], yb[at, :]

    take_edges(ids, load, hn, hs, (l0 // 8, (l0 + nl) // 8))

    def edges(u, ts, ss):
        for t in range(3):
            a, b = ts[t], ss[t]
            n = jnp.where(low_half, pltpu.roll(a[8:16], 4, 0), b[8:16])
            s = jnp.where(low_half, a[0:8], pltpu.roll(b[0:8], 4, 0))
            if t < 2:
                ga[2 * u + t] = jnp.where(todd, s, n)
                gb[2 * u + t] = jnp.where(todd, n, s)
            else:
                en[u] = n
                es[u] = s

    def body(i, carry):
        for k in range(UNROLL_L):
            u = UNROLL_L * i + k
            level = l0 + u
            at = rows_of(level)
            one = pl.ds(level, 1)
            coef = [tuple(cf[c, t, at, :] for c in range(5)) for t in range(3)]
            both = []
            for v in range(2):
                y = [sol[v, t, at, :] for t in range(3)]
                n = [hn[v, t, one, :] for t in range(3)]
                s = [hs[v, t, one, :] for t in range(3)]
                x = stencil(y, coef, n, s, row, 3 if grads else 2)
                buf[u, v, :, 0:LANES] = x[0]
                buf[u, v, :, LANES : 2 * LANES] = x[1]
                if grads:
                    for t in range(3):
                        g[u, v, t] = x[t]
                both.append(x)
            if grads:
                edges(u, *both)
        return carry

    lax.fori_loop(0, nl // UNROLL_L, body, 0)
    copy = pltpu.make_async_copy(buf, adj_out.at[pl.ds(l0, nl), pl.ds(v0, 2)], sem)
    copy.start()
    if grads:
        for i, fo in enumerate(fos):
            pair = [[fo[v, t] for t in range(3)] for v in range(2)]
            for v in range(2):
                for t in range(3):
                    g[nl + i, v, t] = pair[v][t]
            edges(nl + i, *pair)
        units = nl + extra
        per = -(-units // 8)
        lane = iota((8, LANES), 1)
        for i in range(per):
            pn = ps = jnp.zeros((8, LANES), F32)
            for j in range(8):
                u = j * per + i
                if u < units:
                    mine = (lane >= 16 * j) & (lane < 16 * j + 16)
                    pn = jnp.where(mine, pltpu.roll(en[u], (16 * j + 8) % LANES, 1), pn)
                    ps = jnp.where(mine, pltpu.roll(es[u], (16 * j + 8) % LANES, 1), ps)
            ga[2 * units + i] = jnp.where(todd, ps, pn)
            gb[2 * units + i] = jnp.where(todd, pn, ps)
        if carried:
            for i in range(BLOCKS_2):
                ga[2 * units + per + i] = ua[pl.ds(8 * i, 8), :]
                gb[2 * units + per + i] = ub[pl.ds(8 * i, 8), :]
    copy.wait()


def smooth(units, u0, u1, ids, g, ga, gb, wloc, ya, yb, after, z0, z1, z2, z3, w5, hn, hs):
    del after
    zs = (z0, z1, z2, z3)
    face, tile = ids[0], ids[1]
    todd = lax.rem(tile, 2) == 1
    has_n, has_s = tile < 31, tile > 0
    sub = iota((8, LANES), 0)
    lane = iota((8, LANES), 1)
    low_half = sub < 4

    def stack3(lo, m0, m1, hi):
        r0, r1 = pltpu.roll(m0, 4, 0), pltpu.roll(m1, 4, 0)
        return [
            jnp.where(low_half, lo, r0),
            jnp.where(low_half, r0, r1),
            jnp.where(low_half, r1, hi),
        ]

    def north_of(k3):
        turned = [pltpu.roll(x, 7, 0) for x in k3]
        return [
            jnp.where(sub == 7, turned[1], turned[0]),
            jnp.where(sub == 7, turned[2], turned[1]),
            turned[2],
        ]

    def south_of(k3, below=None):
        turned = [pltpu.roll(x, 1, 0) for x in k3]
        return [
            turned[0] if below is None else jnp.where(sub == 0, below, turned[0]),
            jnp.where(sub == 0, turned[0], turned[1]),
            jnp.where(sub == 0, turned[1], turned[2]),
        ]

    we, wn, below = [], [], []
    for c, dest in ((0, we), (1, wn)):
        for t in range(3):
            at = pl.ds(ROWS_2 + 8 * (3 * c + t), 8)
            a, b = ya[at, :], yb[at, :]
            hi = jnp.where(has_n, jnp.where(todd, b, a), 0.0)
            lo = jnp.where(has_s, jnp.where(todd, a, b), 0.0)
            if c == 1:
                below.append(pltpu.roll(lo, 5, 0))
            dest.append(
                stack3(pltpu.roll(lo, 4, 0), wloc[c, t, 0:8, :], wloc[c, t, 8:16, :], pltpu.roll(hi, 4, 0))
            )
    for k in range(3):
        cw3 = west_of([we[t][k] for t in range(3)])
        for t in range(3):
            ok = jnp.ones((8, LANES), F32)
            if k == 0:
                ok = jnp.where(low_half & (tile == 0), 0.0, ok)
            if k == 2:
                ok = jnp.where((~low_half) & (tile == 31), 0.0, ok)
            if t == 2:
                inside = ((lane < 64) & (face < 3)) | ((lane >= 64) & (face > 0))
                ok = jnp.where(inside, ok, 0.0)
            ce = we[t][k] * ok
            cw = cw3[t] * ok
            cn = wn[t][k] * ok
            cs = south_of(wn[t], below[t])[k] * ok
            w5[0, t, k] = ce
            w5[1, t, k] = cw
            w5[2, t, k] = cn
            w5[3, t, k] = cs
            w5[4, t, k] = 1.0 - ce - cw - cn - cs

    per = -(-units // 8)
    for u in range(u0, u1):
        j, i = divmod(u, per)
        a, b = ga[2 * units + i], gb[2 * units + i]
        n = edge_unpack(jnp.where(todd, b, a), j)
        s = edge_unpack(jnp.where(todd, a, b), j)
        u -= u0
        hn[u] = jnp.where(has_n, n, 0.0)
        hs[u] = jnp.where(has_s, s, 0.0)

    bit0 = lax.rem(face, 2) == 1
    bit1 = face >= 2

    def body(i, carry):
        fields = []
        for u in [UNROLL_M * i + k for k in range(UNROLL_M)]:
            hi, lo = [], []
            for t in range(2):
                a, b = ga[2 * (u0 + u) + t], gb[2 * (u0 + u) + t]
                hi.append(jnp.where(has_n, jnp.where(todd, b, a), 0.0))
                lo.append(jnp.where(has_s, jnp.where(todd, a, b), 0.0))
            hi.append(hn[u])
            lo.append(hs[u])
            for v in range(2):
                x = []
                for t in range(3):
                    m = g[u0 + u, v, t]
                    top = pltpu.roll(hi[t], 4, 0) if v == 0 else hi[t]
                    bottom = lo[t] if v == 0 else pltpu.roll(lo[t], 4, 0)
                    x.append(stack3(bottom, m[0:8], m[8:16], top))
                fields.append(x)
        for _ in range(4):
            coefs = [[[w5[c, t, k] for c in range(5)] for k in range(3)] for t in range(3)]
            swept = []
            for x in fields:
                ns = [north_of(x[t]) for t in range(3)]
                ss = [south_of(x[t]) for t in range(3)]
                new = [[], [], []]
                for k in range(3):
                    at_k = [x[t][k] for t in range(3)]
                    e, w = east_of(at_k), west_of(at_k)
                    for t in range(3):
                        ce, cw, cn, cs, cc = coefs[t][k]
                        new[t].append(
                            cc * x[t][k] + ce * e[t] + cw * w[t] + cn * ns[t][k] + cs * ss[t][k]
                        )
                swept.append(new)
            fields = swept
        for c, x in enumerate(fields):
            u = UNROLL_M * i + c // 2
            for t in range(2):
                p = [pltpu.roll(x[t][0], 4, 0), x[t][1], pltpu.roll(x[t][1], 4, 0), x[t][2]]
                p = [jnp.where(bit0, p[d ^ 1], p[d]) for d in range(4)]
                p = [jnp.where(bit1, p[d ^ 2], p[d]) for d in range(4)]
                for k in range(4):
                    zs[k][2 * u + c % 2, :, t * LANES : (t + 1) * LANES] = p[k][0:4]
        return carry

    lax.fori_loop(0, (u1 - u0) // UNROLL_M, body, 0)


def gather_rows(first, size, ids, z0, z1, z2, z3, *refs):
    out, sem = refs[-2:]
    copies = []
    for k, z in enumerate((z0, z1, z2, z3)):
        cols = pl.multiple_of(jnp.bitwise_xor(ids[0], k) * 256, 256)
        dst = out.at[pl.ds(first, size), :, pl.ds(cols, 256)]
        copies.append(pltpu.make_async_copy(z, dst, sem.at[k]))
    for copy in copies:
        copy.start()
    for copy in copies:
        copy.wait()


def on_device(adjoint_seed, face_flow, vert_diff, wet_mask, smooth_weights):
    ids = jnp.stack([lax.axis_index("face"), lax.axis_index("tile")]).astype(jnp.int32)
    tiles = lax.axis_size("tile")
    pair_a = [(i, i ^ 1) for i in range(tiles)]
    pair_b = [(0, 0), (tiles - 1, tiles - 1)]
    for i in range(1, tiles - 1, 2):
        pair_b += [(i, i + 1), (i + 1, i)]
    side_a = [(0, 1), (1, 0), (2, 3), (3, 2)]
    side_b = [(0, 0), (1, 2), (2, 1), (3, 3)]
    hbm, any_space = pltpu.HBM, pl.ANY

    def across(a, b):
        return lax.ppermute(a, "tile", pair_a), lax.ppermute(b, "tile", pair_b)

    def to_face(x, k):
        return lax.ppermute(x, "face", [(i, i ^ k) for i in range(4)])

    edge = (ROWS, LANES)
    packed = (HALF * ROWS, LANES)
    fld, tri, pxa, pxb = call(
        first_solve,
        [((8, 2, FLAT, LANES), VM), ((3, 2, FLAT, LANES), VM), (packed, VM), (packed, VM)],
        [
            VM((2, LEV) + edge, jnp.int32),
            VM(packed, F32),
            VM(packed, F32),
            pltpu.SemaphoreType.DMA((16,)),
        ],
        limit=5,
        ins=[None] + [hbm] * 4,
        name="first_solve",
    )(ids, adjoint_seed, face_flow, vert_diff, wet_mask)
    xa = lax.ppermute(pxa, "face", side_a)
    xb = lax.ppermute(pxb, "face", side_b)
    rows_1 = ((ROWS_1, LANES), VM)
    ya, yb = call(main_edges, [rows_1, rows_1], limit=4, name="main_edges")(ids, fld)
    ya, yb = call(
        outer_edges, [rows_1, rows_1], limit=4, alias={3: 0, 4: 1}, name="outer_edges"
    )(ids, xa, xb, ya, yb)
    later, _ = lax.optimization_barrier((smooth_weights, ya))
    ya, yb = across(ya, yb)
    fe, cf, tre = call(
        coefficients,
        [((8, FLAT, LANES), VM), ((5, 3, FLAT, LANES), VM), ((3, 1, FLAT, LANES), VM)],
        limit=4,
        name="coefficients",
    )(ids, fld, xa, xb)
    weights = [later] + [to_face(later, k) for k in (1, 2, 3)]
    (wloc,) = call(
        local_weights,
        [((2, 3) + edge, VM)],
        [VM((4, 2, 4, 1024), F32)],
        limit=4,
        name="local_weights",
    )(ids, *weights)
    halo = VM((3, 3, LEV, LANES), F32)
    sol_shape = ((2, 3, FLAT, LANES), VM)
    fo_shape = ((2, 3) + edge, VM)
    rows_w = ((ROWS_2 + 48, LANES), VM)
    rows_2 = ((ROWS_2, LANES), VM)
    cf, sol_t, ta, tb, fo_t = call(
        functools.partial(step, True, 0),
        [((5, 3, FLAT, LANES), VM), sol_shape, rows_w, rows_w, fo_shape],
        [halo, halo],
        limit=4,
        alias={3: 0},
        name="step_ts",
    )(ids, fld, fe, cf, tri, tre, ya, yb, wloc)
    ta, tb = across(ta, tb)
    sol_u, ua, ub, fo_u = call(
        functools.partial(step, False, 2),
        [sol_shape, rows_2, rows_2, fo_shape],
        [halo, halo],
        limit=4,
        name="step_uv",
    )(ids, fld, fe, cf, tri, tre, ya, yb)

    adj_shape = adjoint_seed.shape
    adj = None
    chunks = []
    for l0, l1 in CHUNKS:
        nl = l1 - l0
        fos = [fo_t, fo_u] if l1 == LEV else []
        units = nl + len(fos)
        per = -(-units // 8)
        args = [ids, sol_t, cf, ta, tb] + fos
        blocks = 2 * units + per
        carried = 0
        if l0 == 0:
            args += [ua, ub]
            carried = blocks
            blocks += BLOCKS_2
        spaces = [None] + [VM] * (len(args) - 1)
        alias = {}
        if adj is not None:
            alias = {len(args): 0}
            args.append(adj)
            spaces.append(any_space)
        adj, g, ga, gb = call(
            functools.partial(last_stencil, 0, l0, nl, len(fos), carried, True),
            [
                (adj_shape, any_space),
                ((units, 2, 3) + edge, VM),
                ((blocks, 8, LANES), VM),
                ((blocks, 8, LANES), VM),
            ],
            [
                halo,
                halo,
                VM((units, 8, LANES), F32),
                VM((units, 8, LANES), F32),
                VM((nl, 2, ROWS, 256), F32),
                pltpu.SemaphoreType.DMA,
            ],
            limit=6,
            alias=alias,
            ins=spaces,
            name="last_ts_%d" % l0,
        )(*args)
        ga, gb = across(ga, gb)
        chunks.append((units, g, ga, gb))
        if l0 == 0:
            uv_rows = (carried, ga, gb)

    controls = None
    after = chunks[-1][1]
    sent = []
    first = 0

    def gather(controls, first, size, parts):
        args = [ids] + parts
        alias = {}
        if controls is not None:
            alias = {len(args): 0}
            args.append(controls)
        (controls,) = call(
            functools.partial(gather_rows, first, size),
            [((2 * (LEV + 2), 4, 1024), any_space)],
            [pltpu.SemaphoreType.DMA((4,))],
            ins=[None] + [any_space] * (len(args) - 1),
            limit=4,
            alias=alias,
            name="gather_%d" % first,
        )(*args)
        return controls

    for c, u0, u1 in PIECES:
        units, g, ga, gb = chunks[c]
        n = u1 - u0
        zs = call(
            functools.partial(smooth, units, u0, u1),
            [((2 * n, 4, 256), VM)] * 4,
            [
                VM((5, 3, 3, 8, LANES), F32),
                VM((n, 8, LANES), F32),
                VM((n, 8, LANES), F32),
            ],
            ins=[None] + [VM] * 6 + [any_space],
            limit=4,
            name="smooth_%d_%d" % (c, u0),
        )(ids, g, ga, gb, wloc, ta, tb, after)
        after = zs[0]
        sent.append((first, 2 * n, [zs[0]] + [to_face(zs[k], k) for k in (1, 2, 3)]))
        first += 2 * n
    carried, ga, gb = uv_rows
    (adj,) = call(
        functools.partial(last_stencil, 2, 0, LEV, 0, carried, False),
        [(adj_shape, any_space)],
        [halo, halo, VM((LEV, 2, ROWS, 256), F32), pltpu.SemaphoreType.DMA],
        limit=6,
        alias={6: 0},
        ins=[None] + [VM] * 4 + [any_space] * 2,
        name="last_uv",
    )(ids, sol_u, cf, ga, gb, after, adj)
    for start, size, parts in sent:
        controls = gather(controls, start, size, parts)
    return adj, controls


def solution(mesh):
    placed = (
        P(None, None, "tile", "face"),
        P(None, None, "tile", "face"),
        P(None, "tile", "face"),
        P(None, "tile", "face"),
        P(None, ("tile", "face"), None),
    )
    return jax.shard_map(
        on_device,
        mesh=mesh,
        in_specs=placed,
        out_specs=(P(None, None, "tile", "face"), P(None, ("tile", "face"), None)),
        check_vma=False,
    )
```

```python
import functools

import jax
import jax.numpy as jnp
from jax import lax
from jax.experimental import pallas as pl
from jax.experimental.pallas import tpu as pltpu
from jax.sharding import PartitionSpec as P

F32 = jnp.float32
LEV = 64
ROWS = 16
LANES = 128
FLAT = LEV * ROWS
WET, UE, VN, VD = 4, 5, 6, 7
KAPPA = 0.15
MIB = 2**20
UNROLL_S = 4
UNROLL_L = 4
UNROLL_M = 2

CHUNKS = ((0, 24), (24, 64))
PIECES = ((0, 0, 24), (1, 0, 22), (1, 22, 42))


def iota(shape, dim):
    return lax.broadcasted_iota(jnp.int32, shape, dim)


def rows_of(level):
    return pl.ds(pl.multiple_of(level * ROWS, ROWS), ROWS)


def east_of(tiles):
    last = iota(tiles[0].shape, 1) == LANES - 1
    turned = [pltpu.roll(t, LANES - 1, 1) for t in tiles]
    return [jnp.where(last, turned[(i + 1) % 3], turned[i]) for i in range(3)]


def west_of(tiles):
    first = iota(tiles[0].shape, 1) == 0
    turned = [pltpu.roll(t, 1, 1) for t in tiles]
    return [jnp.where(first, turned[(i + 2) % 3], turned[i]) for i in range(3)]


def call(kernel, outs, scratch=(), limit=8, alias=None, name=None, ins=None):
    def run(*args):
        args = list(args)
        specs = [pl.BlockSpec(memory_space=pltpu.SMEM)]
        for i in range(1, len(args)):
            if ins is not None and ins[i] is pltpu.HBM:
                args[i] = pltpu.with_memory_space_constraint(args[i], pltpu.HBM)
        for i in range(1, len(args)):
            space = pltpu.VMEM if ins is None else ins[i]
            specs.append(pl.BlockSpec(memory_space=space))
        return pl.pallas_call(
            kernel,
            out_shape=[jax.ShapeDtypeStruct(s, F32) for s, _ in outs],
            in_specs=specs,
            out_specs=[pl.BlockSpec(memory_space=m) for _, m in outs],
            scratch_shapes=list(scratch),
            input_output_aliases=alias or {},
            compiler_params=pltpu.CompilerParams(vmem_limit_bytes=limit * MIB),
            name=name,
        )(*args)

    return run


VM = pltpu.VMEM


HALF = LEV // 2


def pair_of(i):
    return rows_of(i), rows_of(LEV - 1 - i)


def thirds(tri, wet, vd, tiles, beside=None):
    zero = jnp.zeros((ROWS, LANES), F32)

    def body(i, carry):
        low, rat, low2, rat2 = ([], [], [], [])
        top, bottom = pair_of(i)
        for t in tiles:
            w = wet(t, i)
            up = vd(t, i) * w * wet(t, i + 1)
            p, q = carry[0][t - tiles[0]], carry[1][t - tiles[0]]
            inv = 1.0 / (1.0 + p + up - p * q)
            r = up * inv
            tri[0, t - tiles[0], top, :] = p
            tri[1, t - tiles[0], top, :] = inv
            tri[2, t - tiles[0], top, :] = r
            low.append(up)
            rat.append(r)
            j = LEV - 1 - i
            up = vd(t, j - 1) * wet(t, j - 1) * wet(t, j)
            p, q = carry[2][t - tiles[0]], carry[3][t - tiles[0]]
            inv = 1.0 / (1.0 + p + up - p * q)
            r = up * inv
            tri[0, t - tiles[0], bottom, :] = p
            tri[1, t - tiles[0], bottom, :] = inv
            tri[2, t - tiles[0], bottom, :] = r
            low2.append(up)
            rat2.append(r)
        if beside is not None:
            beside(i)
        return low, rat, low2, rat2

    n = len(tiles)
    lax.fori_loop(0, HALF, body, tuple([zero] * n for _ in range(4)))


def eliminate(rhs, put, get, tri, items, beside=None):
    zero = jnp.zeros((ROWS, LANES), F32)
    n = len(items)

    def inwards(i, carry):
        out = ([], [])
        for side, at in enumerate(pair_of(i)):
            for c, (key, t) in enumerate(items):
                x = (rhs(key, t, at) + tri(0, t, at) * carry[side][c]) * tri(1, t, at)
                put(key, t, at, x)
                out[side].append(x)
        return out

    ends = lax.fori_loop(0, HALF, inwards, ([zero] * n, [zero] * n))
    at, bt = pair_of(HALF - 1)
    start = ([], [])
    for c, (key, t) in enumerate(items):
        r, r2 = tri(2, t, at), tri(2, t, bt)
        y = (ends[0][c] + r * ends[1][c]) * (1.0 / (1.0 - r * r2))
        y2 = ends[1][c] + r2 * y
        put(key, t, at, y)
        put(key, t, bt, y2)
        start[0].append(y)
        start[1].append(y2)
    if beside is not None:
        beside(HALF - 1, start)

    def outwards(k, carry):
        out = ([], [])
        for side, at in enumerate(pair_of(HALF - 2 - k)):
            for c, (key, t) in enumerate(items):
                x = get(key, t, at) + tri(2, t, at) * carry[side][c]
                put(key, t, at, x)
                out[side].append(x)
        if beside is not None:
            beside(HALF - 2 - k, out)
        return out

    return lax.fori_loop(0, HALF - 1, outwards, start)


def first_solve(ids, seed, flow, vd, wet, fld, tri, pxa, pxb, wbuf, pw, sems):
    def tile_copy(src, dst, k):
        copy = pltpu.make_async_copy(src, dst, sems.at[k])
        copy.start()
        return copy

    def place(f, t):
        return fld.at[f, t].reshape(LEV, ROWS, LANES)

    early, late = [], []
    for t in range(2):
        cols = pl.ds(t * LANES, LANES)
        early.append(tile_copy(wet.at[:, :, cols], wbuf.at[t], 8 * t))
        early.append(tile_copy(vd.at[:, :, cols], place(VD, t), 8 * t + 1))
        for v in range(2):
            early.append(tile_copy(flow.at[v, :, :, cols], place(UE + v, t), 8 * t + 2 + v))
    for t in range(2):
        cols = pl.ds(t * LANES, LANES)
        for v in range(4):
            late.append(tile_copy(seed.at[:, v, :, cols], place(v, t), 8 * t + 4 + v))
    for copy in early:
        copy.wait()

    def wet_to_float(i, carry):
        for k in range(8):
            for t in range(2):
                fld[WET, t, rows_of(8 * i + k), :] = wbuf[t, 8 * i + k].astype(F32)
        return carry

    lax.fori_loop(0, LEV // 8, wet_to_float, 0)
    lane = iota((ROWS, LANES), 1)
    first8 = lane < 8
    odd = lax.rem(ids[0], 2) == 1

    def pack(at, fields):
        out = jnp.zeros((ROWS, LANES), F32)
        for f in fields:
            edge = jnp.where(first8, fld[f, 0, at, :], fld[f, 1, at, :])
            mine = (lane >= 16 * f) & (lane < 16 * f + 16)
            by = (16 * f + 8) % LANES
            out = jnp.where(mine, pltpu.roll(edge, by, 1) if by else edge, out)
        return out

    def statics(i):
        top, bottom = pair_of(i)
        pw[top, :] = pack(top, range(4, 8))
        pw[bottom, :] = pack(bottom, range(4, 8))

    thirds(
        tri,
        lambda t, level: fld[WET, t, rows_of(level), :],
        lambda t, level: fld[VD, t, rows_of(level), :],
        (0, 1),
        statics,
    )
    for copy in late:
        copy.wait()

    def put(v, t, at, x):
        fld[v, t, at, :] = x

    for pair in ((0, 1), (2, 3)):
        eliminate(
            lambda v, t, at: fld[v, t, at, :] * fld[WET, t, at, :],
            put,
            lambda v, t, at: fld[v, t, at, :],
            lambda k, t, at: tri[k, t, at, :],
            [(v, t) for v in pair for t in range(2)],
        )

    low = lax.rem(lane, 16) < 8

    def states(n, carry):
        for i in [4 * n + k for k in range(4)]:
            top, bottom = pair_of(i)
            a = pw[top, :] + pack(top, range(4))
            b = pw[bottom, :] + pack(bottom, range(4))
            east = jnp.where(low, a, pltpu.roll(b, 8, 1))
            west = jnp.where(low, pltpu.roll(a, LANES - 8, 1), b)
            at = rows_of(i)
            pxa[at, :] = jnp.where(odd, west, east)
            pxb[at, :] = jnp.where(odd, east, west)
        return carry

    lax.fori_loop(0, HALF // 4, states, 0)


def spread(west, east, half, low):
    if half == 0:
        return jnp.where(low, west, pltpu.roll(east, 8, 1))
    return jnp.where(low, pltpu.roll(west, LANES - 8, 1), east)


def outer_of(both, f):
    by = (120 - 16 * f) % LANES
    return pltpu.roll(both, by, 1) if by else both


OUTER = 5 * 2 * LEV
ROWS_1 = OUTER + LEV
ROWS_2 = 2 * 2 * LEV + 2 * 8
BLOCKS_2 = ROWS_2 // 8


def edge_pack(tiles8):
    lane = iota((8, LANES), 1)
    packed = jnp.zeros((8, LANES), F32)
    for g, t in enumerate(tiles8):
        turned = pltpu.roll(t, (16 * g + 8) % LANES, 1)
        packed = jnp.where((lane >= 16 * g) & (lane < 16 * g + 16), turned, packed)
    return packed


def edge_unpack(packed, g):
    return pltpu.roll(packed, (-(16 * g + 8)) % LANES, 1)


def odd_tile(ids):
    return lax.rem(ids[1], 2) == 1


def turn(todd, x, y):
    return jnp.where(todd, y, x), jnp.where(todd, x, y)


def put_edges(todd, pick, fields, oa, ob):
    for f in range(fields):
        for t in range(2):
            for g in range(8):
                n, s = pick(f, t, g)
                at = pl.ds((f * 2 + t) * LEV + 8 * g, 8)
                oa[at, :], ob[at, :] = turn(todd, n, s)
        outer = [pick(f, 2, g) for g in range(8)]
        n = edge_pack([o[0] for o in outer])
        s = edge_pack([o[1] for o in outer])
        at = pl.ds(fields * 2 * LEV + 8 * f, 8)
        oa[at, :], ob[at, :] = turn(todd, n, s)


def edge_rows(ref, g):
    north = ref[pl.ds(g * 8 * ROWS + ROWS - 1, 8, stride=ROWS), :]
    south = ref[pl.ds(g * 8 * ROWS, 8, stride=ROWS), :]
    return north, south


def main_edges(ids, fld, ya, yb):
    todd = odd_tile(ids)
    for k, f in enumerate((0, 1, WET, 2, 3)):
        for t in range(2):
            for g in range(8):
                n, s = edge_rows(fld.at[f, t], g)
                if f == WET:
                    n = n * (KAPPA - 0.5 * edge_rows(fld.at[VN, t], g)[0])
                at = pl.ds((2 * k + t) * LEV + 8 * g, 8)
                ya[at, :], yb[at, :] = turn(todd, n, s)


def outer_edges(ids, xa, xb, ya_in, yb_in, ya, yb):
    face, tile = ids[0], ids[1]
    odd = lax.rem(face, 2) == 1
    todd = odd_tile(ids)
    for g in range(4):
        na, sa = edge_rows(xa, g)
        nb, sb = edge_rows(xb, g)
        west = (jnp.where(odd, na, nb), jnp.where(odd, sa, sb))
        east = (jnp.where(odd, nb, na), jnp.where(odd, sb, sa))
        for first, inside, (n, s) in ((0, face > 0, west), (HALF, face < 3, east)):
            n = jnp.where(inside, n, 0.0)
            s = jnp.where(inside, s, 0.0)
            at = pl.ds(OUTER + first + 8 * g, 8)
            ya[at, :], yb[at, :] = turn(todd, n, s)


def local_weights(ids, w0, w1, w2, w3, wloc, pieces):
    face = ids[0]
    for k, w in enumerate((w0, w1, w2, w3)):
        pieces[k] = w[...]
    lane4 = iota((4, LANES), 1)
    for d in range(4):
        slot = jnp.bitwise_xor(face, d)
        for c in range(2):
            for t in range(3):
                at = pl.ds(4 * d, 4)
                if t < 2:
                    first = pl.multiple_of((2 * face + t) * LANES, LANES)
                    wloc[c, t, at, :] = pieces[slot, c, :, pl.ds(first, LANES)]
                    continue
                first = pl.multiple_of(jnp.minimum(2 * face + 2, 7) * LANES, LANES)
                e = pieces[slot, c, :, pl.ds(first, LANES)]
                first = pl.multiple_of(jnp.maximum(2 * face - 1, 0) * LANES, LANES)
                w = pieces[slot, c, :, pl.ds(first, LANES)]
                w = jnp.where((lane4 >= 120) & (face > 0), w, 0.0)
                wloc[c, t, at, :] = jnp.where((lane4 < 8) & (face < 3), e, w)


def coefficients(ids, fld, xa, xb, fe, cf, tri):
    row = iota((ROWS, LANES), 0)
    face = ids[0]
    odd = lax.rem(face, 2) == 1
    lane = iota((ROWS, LANES), 1)
    on_east = (lane < 8) & (face < 3)
    on_west = (lane >= 120) & (face > 0)

    outside = on_east | on_west
    low = lax.rem(lane, 16) < 8

    def unpack(n, carry):
        for i in [4 * n + k for k in range(4)]:
            a, b = xa[rows_of(i), :], xb[rows_of(i), :]
            from_west = jnp.where(odd, a, b)
            from_east = jnp.where(odd, b, a)
            for half, at in enumerate(pair_of(i)):
                both = spread(from_west, from_east, half, low)
                for f in range(8):
                    fe[f, at, :] = jnp.where(outside, outer_of(both, f), 0.0)
        return carry

    lax.fori_loop(0, HALF // 4, unpack, 0)
    def body(i):
        for at in pair_of(i):

            def get(f):
                return [fld[f, 0, at, :], fld[f, 1, at, :], fe[f, at, :]]

            wet, ue, vn = (get(f) for f in (WET, UE, VN))
            wet_e = east_of(wet)
            qw_w = west_of([w * (KAPPA - 0.5 * u) for w, u in zip(wet, ue)])
            for t in range(3):
                w = wet[t]
                ce = w * (KAPPA + 0.5 * ue[t]) * wet_e[t]
                cw = w * qw_w[t]
                wn = jnp.where(row == ROWS - 1, 1.0, pltpu.roll(w, ROWS - 1, 0))
                qs = jnp.where(row == 0, 1.0, pltpu.roll(w * (KAPPA - 0.5 * vn[t]), 1, 0))
                cf[0, t, at, :] = ce
                cf[1, t, at, :] = cw
                cf[2, t, at, :] = w * (KAPPA + 0.5 * vn[t]) * wn
                cf[3, t, at, :] = w * qs
                cf[4, t, at, :] = w - ce - cw

    thirds(
        tri,
        lambda t, level: fe[WET, rows_of(level), :],
        lambda t, level: fe[VD, rows_of(level), :],
        (2,),
        body,
    )


def slot_of(level):
    return jnp.where(level < HALF, level, LEV + HALF - 1 - level)


def take_first_edges(ids, ya, yb, hn, hs, first):
    todd = odd_tile(ids)
    lane = iota((8, LANES), 1)

    def both(at):
        a, b = ya[at, :], yb[at, :]
        return turn(todd, a, b)

    for f, k in enumerate((0, 1, 2) if first else (3, 4)):
        for t in range(2):
            for g in range(8):
                at = pl.ds(8 * g, 8)
                n, s = both(pl.ds((2 * k + t) * LEV + 8 * g, 8))
                hn[f, t, at, :] = n
                hs[f, t, at, :] = s
    low = lax.rem(lane, 16) < 8
    for g in range(4):
        wests = both(pl.ds(OUTER + 8 * g, 8))
        easts = both(pl.ds(OUTER + HALF + 8 * g, 8))
        for half in range(2):
            spreads = [spread(w, e, half, low) for w, e in zip(wests, easts)]

            def outer(side, f):
                return outer_of(spreads[side], f)

            at = pl.ds(HALF * half + 8 * g, 8)
            for f, k in enumerate((0, 1) if first else (2, 3)):
                hn[f, 2, at, :] = outer(0, k)
                hs[f, 2, at, :] = outer(1, k)
            if first:
                hn[2, 2, at, :] = outer(0, WET)
                hs[2, 2, at, :] = outer(1, WET) * (KAPPA - 0.5 * outer(1, VN))


def take_edges(ids, load, hn, hs, groups=(0, 8)):
    todd = odd_tile(ids)
    for f in range(2):
        oa, ob = load(32 + f)
        on, os = turn(todd, oa, ob)
        for g in range(*groups):
            at = pl.ds(8 * g, 8)
            for t in range(2):
                a, b = load((f * 2 + t) * 8 + g)
                hn[f, t, at, :], hs[f, t, at, :] = turn(todd, a, b)
            hn[f, 2, at, :] = edge_unpack(on, g)
            hs[f, 2, at, :] = edge_unpack(os, g)


def stencil(y, ref, level, coef, north_row, south_row, tiles=3):
    e, w = east_of(y), west_of(y)
    sub = iota((8, LANES), 0)
    base = pl.multiple_of(level * ROWS, ROWS)
    out = []
    for t in range(tiles):
        n = jnp.concatenate(
            [
                ref(t)[pl.ds(base + 1, 8), :],
                jnp.where(sub == 7, north_row[t], pltpu.roll(y[t][8:16], 7, 0)),
            ],
            0,
        )
        s = jnp.concatenate(
            [
                jnp.where(sub == 0, south_row[t], pltpu.roll(y[t][0:8], 1, 0)),
                ref(t)[pl.ds(base + 7, 8), :],
            ],
            0,
        )
        ce, cw, cn, cs, cc = coef[t]
        out.append(cc * y[t] + ce * e[t] + cw * w[t] + cn * n + cs * s)
    return out


def step(first, v0, ids, fld, fe, cfi, trm, tre, ya, yb, *refs):
    if first:
        wloc, cf, sol, oa, ob, fo, hn, hs = refs
    else:
        sol, oa, ob, fo, hn, hs = refs
    todd = odd_tile(ids)
    row = iota((ROWS, LANES), 0)
    take_first_edges(ids, ya, yb, hn, hs, first)

    def get(v, at):
        return [fld[v0 + v, 0, at, :], fld[v0 + v, 1, at, :], fe[v0 + v, at, :]]

    north_in = jnp.where(ids[1] < 31, 1.0, 0.0).astype(F32)
    south_in = jnp.where(ids[1] > 0, 1.0, 0.0).astype(F32)

    def apply(i, carry):
        for k in range(UNROLL_S):
            level = UNROLL_S * i + k
            at = rows_of(level)
            ones = [pl.ds(level, 1), pl.ds(level, 1), pl.ds(slot_of(level), 1)]
            coef = []
            for t in range(3):
                ce, cw, cn, cs, cc = (cfi[c, t, at, :] for c in range(5))
                if first:
                    cn = jnp.where(row == ROWS - 1, cn * (hn[2, t, ones[t], :] * north_in), cn)
                    cs = jnp.where(row == 0, cs * (hs[2, t, ones[t], :] * south_in), cs)
                    cc = cc - cn - cs
                    cf[2, t, at, :] = cn
                    cf[3, t, at, :] = cs
                    cf[4, t, at, :] = cc
                coef.append((ce, cw, cn, cs, cc))
            for v in range(2):
                n = [hn[v, t, ones[t], :] for t in range(3)]
                s = [hs[v, t, ones[t], :] for t in range(3)]
                f = v0 + v
                adj = stencil(
                    get(v, at), lambda t: fe.at[f] if t == 2 else fld.at[f, t], level, coef, n, s
                )
                for t in range(3):
                    sol[v, t, at, :] = adj[t]
        return carry

    lax.fori_loop(0, LEV // UNROLL_S, apply, 0)

    def put(v, t, at, x):
        sol[v, t, at, :] = x

    def load(v, t, at):
        return sol[v, t, at, :]

    top = eliminate(
        load,
        put,
        load,
        lambda k, t, at: tre[k, 0, at, :] if t == 2 else trm[k, t, at, :],
        [(v, t) for v in range(2) for t in range(3)],
    )[0]
    for v in range(2):
        y = get(v, pl.ds(0, ROWS))
        for t in range(3):
            fo[v, t] = y[t] + top[3 * v + t]
    put_edges(todd, lambda f, t, g: edge_rows(sol.at[f, t], g), 2, oa, ob)
    if first:
        for c in range(2):
            for t in range(3):
                n = wloc[c, t, 8:16, :]
                s = wloc[c, t, 0:8, :]
                at = pl.ds(ROWS_2 + 8 * (3 * c + t), 8)
                oa[at, :], ob[at, :] = turn(todd, n, s)


def last_stencil(v0, l0, nl, extra, carried, grads, *refs):
    ids, sol, cf, ya, yb = refs[:5]
    refs = refs[5:]
    fos = refs[:extra]
    refs = refs[extra:]
    if grads and carried:
        ua, ub = refs[:2]
        refs = refs[2:]
    if not grads:
        refs = refs[1:]
    if l0 or v0:
        refs = refs[1:]
    if grads:
        adj_out, g, ga, gb, hn, hs, en, es, buf, sem = refs
    else:
        adj_out, hn, hs, buf, sem = refs
    row = iota((ROWS, LANES), 0)
    todd = odd_tile(ids)
    low_half = iota((8, LANES), 0) < 4

    def load(block):
        if not grads:
            return ya[carried + block], yb[carried + block]
        at = pl.ds(8 * block, 8)
        return ya[at, :], yb[at, :]

    take_edges(ids, load, hn, hs, (l0 // 8, (l0 + nl) // 8))

    def edges(u, ts, ss):
        for t in range(3):
            a, b = ts[t], ss[t]
            n = jnp.where(low_half, pltpu.roll(a[8:16], 4, 0), b[8:16])
            s = jnp.where(low_half, a[0:8], pltpu.roll(b[0:8], 4, 0))
            if t < 2:
                ga[2 * u + t], gb[2 * u + t] = turn(todd, n, s)
            else:
                en[u] = n
                es[u] = s

    def body(i, carry):
        for k in range(UNROLL_L):
            u = UNROLL_L * i + k
            level = l0 + u
            at = rows_of(level)
            one = pl.ds(level, 1)
            coef = [tuple(cf[c, t, at, :] for c in range(5)) for t in range(3)]
            both = []
            for v in range(2):
                y = [sol[v, t, at, :] for t in range(3)]
                n = [hn[v, t, one, :] for t in range(3)]
                s = [hs[v, t, one, :] for t in range(3)]
                x = stencil(y, lambda t: sol.at[v, t], level, coef, n, s, 3 if grads else 2)
                buf[u, v, :, 0:LANES] = x[0]
                buf[u, v, :, LANES : 2 * LANES] = x[1]
                if grads:
                    for t in range(3):
                        g[u, v, t] = x[t]
                both.append(x)
            if grads:
                edges(u, *both)
        return carry

    lax.fori_loop(0, nl // UNROLL_L, body, 0)
    copy = pltpu.make_async_copy(buf, adj_out.at[pl.ds(l0, nl), pl.ds(v0, 2)], sem)
    copy.start()
    if grads:
        for i, fo in enumerate(fos):
            pair = [[fo[v, t] for t in range(3)] for v in range(2)]
            for v in range(2):
                for t in range(3):
                    g[nl + i, v, t] = pair[v][t]
            edges(nl + i, *pair)
        units = nl + extra
        per = -(-units // 8)
        lane = iota((8, LANES), 1)
        for i in range(per):
            pn = ps = jnp.zeros((8, LANES), F32)
            for j in range(8):
                u = j * per + i
                if u < units:
                    mine = (lane >= 16 * j) & (lane < 16 * j + 16)
                    pn = jnp.where(mine, pltpu.roll(en[u], (16 * j + 8) % LANES, 1), pn)
                    ps = jnp.where(mine, pltpu.roll(es[u], (16 * j + 8) % LANES, 1), ps)
            ga[2 * units + i], gb[2 * units + i] = turn(todd, pn, ps)
        if carried:
            for i in range(BLOCKS_2):
                ga[2 * units + per + i] = ua[pl.ds(8 * i, 8), :]
                gb[2 * units + per + i] = ub[pl.ds(8 * i, 8), :]
    copy.wait()


def smooth(units, u0, u1, ids, g, ga, gb, wloc, ya, yb, after, z0, z1, z2, z3, w5, hn, hs):
    del after
    zs = (z0, z1, z2, z3)
    face, tile = ids[0], ids[1]
    todd = odd_tile(ids)
    has_n, has_s = tile < 31, tile > 0
    sub = iota((8, LANES), 0)
    lane = iota((8, LANES), 1)
    low_half = sub < 4

    def stack3(lo, m0, m1, hi):
        r0, r1 = pltpu.roll(m0, 4, 0), pltpu.roll(m1, 4, 0)
        return [
            jnp.where(low_half, lo, r0),
            jnp.where(low_half, r0, r1),
            jnp.where(low_half, r1, hi),
        ]

    def north_of(k3):
        turned = [pltpu.roll(x, 7, 0) for x in k3]
        return [
            jnp.where(sub == 7, turned[1], turned[0]),
            jnp.where(sub == 7, turned[2], turned[1]),
            turned[2],
        ]

    def south_of(k3, below=None):
        turned = [pltpu.roll(x, 1, 0) for x in k3]
        return [
            turned[0] if below is None else jnp.where(sub == 0, below, turned[0]),
            jnp.where(sub == 0, turned[0], turned[1]),
            jnp.where(sub == 0, turned[1], turned[2]),
        ]

    we, wn, below = [], [], []
    for c, dest in ((0, we), (1, wn)):
        for t in range(3):
            at = pl.ds(ROWS_2 + 8 * (3 * c + t), 8)
            a, b = ya[at, :], yb[at, :]
            a, b = turn(todd, a, b)
            hi = jnp.where(has_n, a, 0.0)
            lo = jnp.where(has_s, b, 0.0)
            if c == 1:
                below.append(pltpu.roll(lo, 5, 0))
            dest.append(
                stack3(pltpu.roll(lo, 4, 0), wloc[c, t, 0:8, :], wloc[c, t, 8:16, :], pltpu.roll(hi, 4, 0))
            )
    for k in range(3):
        cw3 = west_of([we[t][k] for t in range(3)])
        for t in range(3):
            ok = jnp.ones((8, LANES), F32)
            if k == 0:
                ok = jnp.where(low_half & (tile == 0), 0.0, ok)
            if k == 2:
                ok = jnp.where((~low_half) & (tile == 31), 0.0, ok)
            if t == 2:
                inside = ((lane < 64) & (face < 3)) | ((lane >= 64) & (face > 0))
                ok = jnp.where(inside, ok, 0.0)
            ce = we[t][k] * ok
            cw = cw3[t] * ok
            cn = wn[t][k] * ok
            cs = south_of(wn[t], below[t])[k] * ok
            w5[0, t, k] = ce
            w5[1, t, k] = cw
            w5[2, t, k] = cn
            w5[3, t, k] = cs
            w5[4, t, k] = 1.0 - ce - cw - cn - cs

    per = -(-units // 8)
    for u in range(u0, u1):
        j, i = divmod(u, per)
        a, b = ga[2 * units + i], gb[2 * units + i]
        a, b = turn(todd, a, b)
        n = edge_unpack(a, j)
        s = edge_unpack(b, j)
        u -= u0
        hn[u] = jnp.where(has_n, n, 0.0)
        hs[u] = jnp.where(has_s, s, 0.0)

    bit0 = lax.rem(face, 2) == 1
    bit1 = face >= 2

    def body(i, carry):
        fields = []
        for u in [UNROLL_M * i + k for k in range(UNROLL_M)]:
            hi, lo = [], []
            for t in range(2):
                a, b = ga[2 * (u0 + u) + t], gb[2 * (u0 + u) + t]
                a, b = turn(todd, a, b)
                hi.append(jnp.where(has_n, a, 0.0))
                lo.append(jnp.where(has_s, b, 0.0))
            hi.append(hn[u])
            lo.append(hs[u])
            for v in range(2):
                x = []
                for t in range(3):
                    m = g[u0 + u, v, t]
                    top = pltpu.roll(hi[t], 4, 0) if v == 0 else hi[t]
                    bottom = lo[t] if v == 0 else pltpu.roll(lo[t], 4, 0)
                    x.append(stack3(bottom, m[0:8], m[8:16], top))
                fields.append(x)
        for sweep in range(4):
            kept = 3 if sweep < 3 else 2
            coefs = [[[w5[c, t, k] for c in range(5)] for k in range(3)] for t in range(3)]
            swept = []
            for x in fields:
                ns = [north_of(x[t]) for t in range(kept)]
                ss = [south_of(x[t]) for t in range(kept)]
                new = [[], [], []]
                for k in range(3):
                    at_k = [x[t][k] for t in range(3)]
                    e, w = east_of(at_k), west_of(at_k)
                    for t in range(kept):
                        ce, cw, cn, cs, cc = coefs[t][k]
                        new[t].append(
                            cc * x[t][k] + ce * e[t] + cw * w[t] + cn * ns[t][k] + cs * ss[t][k]
                        )
                swept.append(new)
            fields = swept
        for c, x in enumerate(fields):
            u = UNROLL_M * i + c // 2
            for t in range(2):
                p = [pltpu.roll(x[t][0], 4, 0), x[t][1], pltpu.roll(x[t][1], 4, 0), x[t][2]]
                p = [jnp.where(bit0, p[d ^ 1], p[d]) for d in range(4)]
                p = [jnp.where(bit1, p[d ^ 2], p[d]) for d in range(4)]
                for k in range(4):
                    zs[k][2 * u + c % 2, :, t * LANES : (t + 1) * LANES] = p[k][0:4]
        return carry

    lax.fori_loop(0, (u1 - u0) // UNROLL_M, body, 0)


def gather_rows(first, size, ids, z0, z1, z2, z3, *refs):
    out, sem = refs[-2:]
    copies = []
    for k, z in enumerate((z0, z1, z2, z3)):
        cols = pl.multiple_of(jnp.bitwise_xor(ids[0], k) * 256, 256)
        dst = out.at[pl.ds(first, size), :, pl.ds(cols, 256)]
        copies.append(pltpu.make_async_copy(z, dst, sem.at[k]))
    for copy in copies:
        copy.start()
    for copy in copies:
        copy.wait()


def on_device(adjoint_seed, face_flow, vert_diff, wet_mask, smooth_weights):
    ids = jnp.stack([lax.axis_index("face"), lax.axis_index("tile")]).astype(jnp.int32)
    tiles = lax.axis_size("tile")
    pair_a = [(i, i ^ 1) for i in range(tiles)]
    pair_b = [(i, (i + (1 if i % 2 else -1)) % tiles) for i in range(tiles)]
    side_a = [(0, 1), (1, 0), (2, 3), (3, 2)]
    side_b = [(0, 0), (1, 2), (2, 1), (3, 3)]
    hbm, any_space = pltpu.HBM, pl.ANY

    def across(a, b):
        return lax.ppermute(a, "tile", pair_a), lax.ppermute(b, "tile", pair_b)

    def to_face(x, k):
        return lax.ppermute(x, "face", [(i, i ^ k) for i in range(4)])

    edge = (ROWS, LANES)
    packed = (HALF * ROWS, LANES)
    fld, tri, pxa, pxb = call(
        first_solve,
        [((8, 2, FLAT, LANES), VM), ((3, 2, FLAT, LANES), VM), (packed, VM), (packed, VM)],
        [
            VM((2, LEV) + edge, jnp.int32),
            VM((FLAT, LANES), F32),
            pltpu.SemaphoreType.DMA((16,)),
        ],
        limit=5,
        ins=[None] + [hbm] * 4,
        name="first_solve",
    )(ids, adjoint_seed, face_flow, vert_diff, wet_mask)
    weights = [smooth_weights] + [to_face(smooth_weights, k) for k in (1, 2, 3)]
    (wloc,) = call(
        local_weights,
        [((2, 3) + edge, VM)],
        [VM((4, 2, 4, 1024), F32)],
        limit=4,
        name="local_weights",
    )(ids, *weights)
    pxa, pxb, wloc = lax.optimization_barrier((pxa, pxb, wloc))
    xa = lax.ppermute(pxa, "face", side_a)
    xb = lax.ppermute(pxb, "face", side_b)
    rows_1 = ((ROWS_1, LANES), VM)
    ya, yb = call(main_edges, [rows_1, rows_1], limit=4, name="main_edges")(ids, fld)
    ya, yb = call(
        outer_edges, [rows_1, rows_1], limit=4, alias={3: 0, 4: 1}, name="outer_edges"
    )(ids, xa, xb, ya, yb)
    ya, yb = across(ya, yb)
    fe, cf, tre = call(
        coefficients,
        [((8, FLAT, LANES), VM), ((5, 3, FLAT, LANES), VM), ((3, 1, FLAT, LANES), VM)],
        limit=4,
        name="coefficients",
    )(ids, fld, xa, xb)
    halo = VM((3, 3, LEV, LANES), F32)
    sol_shape = ((2, 3, FLAT, LANES), VM)
    fo_shape = ((2, 3) + edge, VM)
    rows_w = ((ROWS_2 + 48, LANES), VM)
    rows_2 = ((ROWS_2, LANES), VM)
    cf, sol_t, ta, tb, fo_t = call(
        functools.partial(step, True, 0),
        [((5, 3, FLAT, LANES), VM), sol_shape, rows_w, rows_w, fo_shape],
        [halo, halo],
        limit=4,
        alias={3: 0},
        name="step_ts",
    )(ids, fld, fe, cf, tri, tre, ya, yb, wloc)
    ta, tb = across(ta, tb)
    sol_u, ua, ub, fo_u = call(
        functools.partial(step, False, 2),
        [sol_shape, rows_2, rows_2, fo_shape],
        [halo, halo],
        limit=4,
        name="step_uv",
    )(ids, fld, fe, cf, tri, tre, ya, yb)

    adj_shape = adjoint_seed.shape
    adj = None
    chunks = []
    for l0, l1 in CHUNKS:
        nl = l1 - l0
        fos = [fo_t, fo_u] if l1 == LEV else []
        units = nl + len(fos)
        per = -(-units // 8)
        args = [ids, sol_t, cf, ta, tb] + fos
        blocks = 2 * units + per
        carried = 0
        if l0 == 0:
            args += [ua, ub]
            carried = blocks
            blocks += BLOCKS_2
        spaces = [None] + [VM] * (len(args) - 1)
        alias = {}
        if adj is not None:
            alias = {len(args): 0}
            args.append(adj)
            spaces.append(any_space)
        adj, g, ga, gb = call(
            functools.partial(last_stencil, 0, l0, nl, len(fos), carried, True),
            [
                (adj_shape, any_space),
                ((units, 2, 3) + edge, VM),
                ((blocks, 8, LANES), VM),
                ((blocks, 8, LANES), VM),
            ],
            [
                halo,
                halo,
                VM((units, 8, LANES), F32),
                VM((units, 8, LANES), F32),
                VM((nl, 2, ROWS, 256), F32),
                pltpu.SemaphoreType.DMA,
            ],
            limit=6,
            alias=alias,
            ins=spaces,
            name="last_ts_%d" % l0,
        )(*args)
        ga, gb = across(ga, gb)
        chunks.append((units, g, ga, gb))
        if l0 == 0:
            uv_rows = (carried, ga, gb)

    controls = None
    after = chunks[-1][1]
    sent = []
    first = 0

    def gather(controls, first, size, parts):
        args = [ids] + parts
        alias = {}
        if controls is not None:
            alias = {len(args): 0}
            args.append(controls)
        (controls,) = call(
            functools.partial(gather_rows, first, size),
            [((2 * (LEV + 2), 4, 1024), any_space)],
            [pltpu.SemaphoreType.DMA((4,))],
            ins=[None] + [any_space] * (len(args) - 1),
            limit=4,
            alias=alias,
            name="gather_%d" % first,
        )(*args)
        return controls

    for c, u0, u1 in PIECES:
        units, g, ga, gb = chunks[c]
        n = u1 - u0
        zs = call(
            functools.partial(smooth, units, u0, u1),
            [((2 * n, 4, 256), VM)] * 4,
            [
                VM((5, 3, 3, 8, LANES), F32),
                VM((n, 8, LANES), F32),
                VM((n, 8, LANES), F32),
            ],
            ins=[None] + [VM] * 6 + [any_space],
            limit=4,
            name="smooth_%d_%d" % (c, u0),
        )(ids, g, ga, gb, wloc, ta, tb, after)
        after = zs[0]
        sent.append((first, 2 * n, [zs[0]] + [to_face(zs[k], k) for k in (1, 2, 3)]))
        first += 2 * n
    carried, ga, gb = uv_rows
    (adj,) = call(
        functools.partial(last_stencil, 2, 0, LEV, 0, carried, False),
        [(adj_shape, any_space)],
        [halo, halo, VM((LEV, 2, ROWS, 256), F32), pltpu.SemaphoreType.DMA],
        limit=6,
        alias={6: 0},
        ins=[None] + [VM] * 4 + [any_space] * 2,
        name="last_uv",
    )(ids, sol_u, cf, ga, gb, after, adj)
    for start, size, parts in sent:
        controls = gather(controls, start, size, parts)
    return adj, controls


def solution(mesh):
    placed = (
        P(None, None, "tile", "face"),
        P(None, None, "tile", "face"),
        P(None, "tile", "face"),
        P(None, "tile", "face"),
        P(None, ("tile", "face"), None),
    )
    return jax.shard_map(
        on_device,
        mesh=mesh,
        in_specs=placed,
        out_specs=(P(None, None, "tile", "face"), P(None, ("tile", "face"), None)),
        check_vma=False,
    )
```

```python
import functools

import jax
import jax.numpy as jnp
from jax import lax
from jax.experimental import pallas as pl
from jax.experimental.pallas import tpu as pltpu
from jax.sharding import PartitionSpec as P

F32 = jnp.float32
LEV = 64
ROWS = 16
LANES = 128
FLAT = LEV * ROWS
WET, UE, VN, VD = 4, 5, 6, 7
KAPPA = 0.15
MIB = 2**20
UNROLL_S = 8
UNROLL_L = 8
UNROLL_M = 2

CHUNKS = ((0, 24), (24, 64))
PIECES = ((0, 0, 24), (1, 0, 22), (1, 22, 42))
CARRIER = 0


def iota(shape, dim):
    return lax.broadcasted_iota(jnp.int32, shape, dim)


def rows_of(level):
    return pl.ds(pl.multiple_of(level * ROWS, ROWS), ROWS)


def east_of(tiles):
    last = iota(tiles[0].shape, 1) == LANES - 1
    turned = [pltpu.roll(t, LANES - 1, 1) for t in tiles]
    return [jnp.where(last, turned[(i + 1) % 3], turned[i]) for i in range(3)]


def west_of(tiles):
    first = iota(tiles[0].shape, 1) == 0
    turned = [pltpu.roll(t, 1, 1) for t in tiles]
    return [jnp.where(first, turned[(i + 2) % 3], turned[i]) for i in range(3)]


def call(kernel, outs, scratch=(), limit=8, alias=None, name=None, ins=None):
    def run(*args):
        args = list(args)
        specs = [pl.BlockSpec(memory_space=pltpu.SMEM)]
        for i in range(1, len(args)):
            if ins is not None and ins[i] is pltpu.HBM:
                args[i] = pltpu.with_memory_space_constraint(args[i], pltpu.HBM)
        for i in range(1, len(args)):
            space = pltpu.VMEM if ins is None else ins[i]
            specs.append(pl.BlockSpec(memory_space=space))
        return pl.pallas_call(
            kernel,
            out_shape=[jax.ShapeDtypeStruct(s, F32) for s, _ in outs],
            in_specs=specs,
            out_specs=[pl.BlockSpec(memory_space=m) for _, m in outs],
            scratch_shapes=list(scratch),
            input_output_aliases=alias or {},
            compiler_params=pltpu.CompilerParams(vmem_limit_bytes=limit * MIB),
            name=name,
        )(*args)

    return run


VM = pltpu.VMEM


HALF = LEV // 2


def pair_of(i):
    return rows_of(i), rows_of(LEV - 1 - i)


def thirds(tri, wet, vd, tiles, beside=None):
    zero = jnp.zeros((ROWS, LANES), F32)

    def one(i, carry):
        low, rat, low2, rat2 = ([], [], [], [])
        top, bottom = pair_of(i)
        for t in tiles:
            w = wet(t, i)
            up = vd(t, i) * w * wet(t, i + 1)
            p, q = carry[0][t - tiles[0]], carry[1][t - tiles[0]]
            inv = 1.0 / (1.0 + p + up - p * q)
            r = up * inv
            tri[0, t - tiles[0], top, :] = p
            tri[1, t - tiles[0], top, :] = inv
            tri[2, t - tiles[0], top, :] = r
            low.append(up)
            rat.append(r)
            j = LEV - 1 - i
            up = vd(t, j - 1) * wet(t, j - 1) * wet(t, j)
            p, q = carry[2][t - tiles[0]], carry[3][t - tiles[0]]
            inv = 1.0 / (1.0 + p + up - p * q)
            r = up * inv
            tri[0, t - tiles[0], bottom, :] = p
            tri[1, t - tiles[0], bottom, :] = inv
            tri[2, t - tiles[0], bottom, :] = r
            low2.append(up)
            rat2.append(r)
        if beside is not None:
            beside(i)
        return low, rat, low2, rat2

    def body(m, carry):
        return one(2 * m + 1, one(2 * m, carry))

    n = len(tiles)
    lax.fori_loop(0, HALF // 2, body, tuple([zero] * n for _ in range(4)))


def eliminate(rhs, put, get, tri, items, beside=None):
    zero = jnp.zeros((ROWS, LANES), F32)
    n = len(items)

    def inwards(i, carry):
        out = ([], [])
        for side, at in enumerate(pair_of(i)):
            for c, (key, t) in enumerate(items):
                x = (rhs(key, t, at) + tri(0, t, at) * carry[side][c]) * tri(1, t, at)
                put(key, t, at, x)
                out[side].append(x)
        return out

    ends = lax.fori_loop(0, HALF, inwards, ([zero] * n, [zero] * n))
    at, bt = pair_of(HALF - 1)
    start = ([], [])
    for c, (key, t) in enumerate(items):
        r, r2 = tri(2, t, at), tri(2, t, bt)
        y = (ends[0][c] + r * ends[1][c]) * (1.0 / (1.0 - r * r2))
        y2 = ends[1][c] + r2 * y
        put(key, t, at, y)
        put(key, t, bt, y2)
        start[0].append(y)
        start[1].append(y2)
    if beside is not None:
        beside(HALF - 1, start)

    def outwards(k, carry):
        out = ([], [])
        for side, at in enumerate(pair_of(HALF - 2 - k)):
            for c, (key, t) in enumerate(items):
                x = get(key, t, at) + tri(2, t, at) * carry[side][c]
                put(key, t, at, x)
                out[side].append(x)
        if beside is not None:
            beside(HALF - 2 - k, out)
        return out

    return lax.fori_loop(0, HALF - 1, outwards, start)


def first_solve(ids, seed, flow, vd, wet, fld, tri, pxa, pxb, wbuf, pw, sems):
    def tile_copy(src, dst, k):
        copy = pltpu.make_async_copy(src, dst, sems.at[k])
        copy.start()
        return copy

    def place(f, t):
        return fld.at[f, t].reshape(LEV, ROWS, LANES)

    early, late = [], []
    for t in range(2):
        cols = pl.ds(t * LANES, LANES)
        early.append(tile_copy(wet.at[:, :, cols], wbuf.at[t], 8 * t))
        early.append(tile_copy(vd.at[:, :, cols], place(VD, t), 8 * t + 1))
        for v in range(2):
            early.append(tile_copy(flow.at[v, :, :, cols], place(UE + v, t), 8 * t + 2 + v))
    for t in range(2):
        cols = pl.ds(t * LANES, LANES)
        for v in range(4):
            late.append(tile_copy(seed.at[:, v, :, cols], place(v, t), 8 * t + 4 + v))
    for copy in early:
        copy.wait()

    def wet_to_float(i, carry):
        for k in range(8):
            for t in range(2):
                fld[WET, t, rows_of(8 * i + k), :] = wbuf[t, 8 * i + k].astype(F32)
        return carry

    lax.fori_loop(0, LEV // 8, wet_to_float, 0)
    lane = iota((ROWS, LANES), 1)
    first8 = lane < 8
    odd = lax.rem(ids[0], 2) == 1

    def pack(at, fields):
        out = jnp.zeros((ROWS, LANES), F32)
        for f in fields:
            edge = jnp.where(first8, fld[f, 0, at, :], fld[f, 1, at, :])
            mine = (lane >= 16 * f) & (lane < 16 * f + 16)
            by = (16 * f + 8) % LANES
            out = jnp.where(mine, pltpu.roll(edge, by, 1) if by else edge, out)
        return out

    def statics(i):
        top, bottom = pair_of(i)
        pw[top, :] = pack(top, range(4, 8))
        pw[bottom, :] = pack(bottom, range(4, 8))

    thirds(
        tri,
        lambda t, level: fld[WET, t, rows_of(level), :],
        lambda t, level: fld[VD, t, rows_of(level), :],
        (0, 1),
        statics,
    )
    for copy in late:
        copy.wait()

    def put(v, t, at, x):
        fld[v, t, at, :] = x

    for pair in ((0, 1), (2, 3)):
        eliminate(
            lambda v, t, at: fld[v, t, at, :] * fld[WET, t, at, :],
            put,
            lambda v, t, at: fld[v, t, at, :],
            lambda k, t, at: tri[k, t, at, :],
            [(v, t) for v in pair for t in range(2)],
        )

    low = lax.rem(lane, 16) < 8

    def states(n, carry):
        for i in [4 * n + k for k in range(4)]:
            top, bottom = pair_of(i)
            a = pw[top, :] + pack(top, range(4))
            b = pw[bottom, :] + pack(bottom, range(4))
            east = jnp.where(low, a, pltpu.roll(b, 8, 1))
            west = jnp.where(low, pltpu.roll(a, LANES - 8, 1), b)
            at = rows_of(i)
            pxa[at, :] = jnp.where(odd, west, east)
            pxb[at, :] = jnp.where(odd, east, west)
        return carry

    lax.fori_loop(0, HALF // 4, states, 0)


def spread(west, east, half, low):
    if half == 0:
        return jnp.where(low, west, pltpu.roll(east, 8, 1))
    return jnp.where(low, pltpu.roll(west, LANES - 8, 1), east)


def outer_of(both, f):
    by = (120 - 16 * f) % LANES
    return pltpu.roll(both, by, 1) if by else both


OUTER = 5 * 2 * LEV
ROWS_1 = OUTER + LEV
ROWS_2 = 2 * 2 * LEV + 2 * 8
BLOCKS_2 = ROWS_2 // 8


def edge_pack(tiles8):
    lane = iota((8, LANES), 1)
    packed = jnp.zeros((8, LANES), F32)
    for g, t in enumerate(tiles8):
        turned = pltpu.roll(t, (16 * g + 8) % LANES, 1)
        packed = jnp.where((lane >= 16 * g) & (lane < 16 * g + 16), turned, packed)
    return packed


def edge_unpack(packed, g):
    return pltpu.roll(packed, (-(16 * g + 8)) % LANES, 1)


def even_tile(ids):
    return lax.rem(ids[1], 2) == 0


def turn(even, x, y):
    return jnp.where(even, y, x), jnp.where(even, x, y)


def put_edges(even, pick, fields, oa, ob):
    for f in range(fields):
        for t in range(2):
            for g in range(8):
                n, s = pick(f, t, g)
                at = pl.ds((f * 2 + t) * LEV + 8 * g, 8)
                oa[at, :], ob[at, :] = turn(even, n, s)
        outer = [pick(f, 2, g) for g in range(8)]
        n = edge_pack([o[0] for o in outer])
        s = edge_pack([o[1] for o in outer])
        at = pl.ds(fields * 2 * LEV + 8 * f, 8)
        oa[at, :], ob[at, :] = turn(even, n, s)


def edge_rows(ref, g):
    north = ref[pl.ds(g * 8 * ROWS + ROWS - 1, 8, stride=ROWS), :]
    south = ref[pl.ds(g * 8 * ROWS, 8, stride=ROWS), :]
    return north, south


def main_edges(ids, fld, ya, yb):
    even = even_tile(ids)
    for k, f in enumerate((0, 1, WET, 2, 3)):
        for t in range(2):
            for g in range(8):
                n, s = edge_rows(fld.at[f, t], g)
                if f == WET:
                    n = n * (KAPPA - 0.5 * edge_rows(fld.at[VN, t], g)[0])
                at = pl.ds((2 * k + t) * LEV + 8 * g, 8)
                ya[at, :], yb[at, :] = turn(even, n, s)


def outer_edges(ids, xa, xb, ya_in, yb_in, ya, yb):
    face, tile = ids[0], ids[1]
    odd = lax.rem(face, 2) == 1
    even = even_tile(ids)
    for g in range(4):
        na, sa = edge_rows(xa, g)
        nb, sb = edge_rows(xb, g)
        west = (jnp.where(odd, na, nb), jnp.where(odd, sa, sb))
        east = (jnp.where(odd, nb, na), jnp.where(odd, sb, sa))
        for first, inside, (n, s) in ((0, face > 0, west), (HALF, face < 3, east)):
            n = jnp.where(inside, n, 0.0)
            s = jnp.where(inside, s, 0.0)
            at = pl.ds(OUTER + first + 8 * g, 8)
            ya[at, :], yb[at, :] = turn(even, n, s)


def local_weights(ids, w0, w1, w2, w3, wloc, pieces):
    face = ids[0]
    for k, w in enumerate((w0, w1, w2, w3)):
        pieces[k] = w[...]
    lane4 = iota((4, LANES), 1)
    for d in range(4):
        slot = jnp.bitwise_xor(face, d)
        for c in range(2):
            for t in range(3):
                at = pl.ds(4 * d, 4)
                if t < 2:
                    first = pl.multiple_of((2 * face + t) * LANES, LANES)
                    wloc[c, t, at, :] = pieces[slot, c, :, pl.ds(first, LANES)]
                    continue
                first = pl.multiple_of(jnp.minimum(2 * face + 2, 7) * LANES, LANES)
                e = pieces[slot, c, :, pl.ds(first, LANES)]
                first = pl.multiple_of(jnp.maximum(2 * face - 1, 0) * LANES, LANES)
                w = pieces[slot, c, :, pl.ds(first, LANES)]
                w = jnp.where((lane4 >= 120) & (face > 0), w, 0.0)
                wloc[c, t, at, :] = jnp.where((lane4 < 8) & (face < 3), e, w)


def coefficients(ids, fld, xa, xb, fe, cf, tri):
    row = iota((ROWS, LANES), 0)
    face = ids[0]
    odd = lax.rem(face, 2) == 1
    lane = iota((ROWS, LANES), 1)
    on_east = (lane < 8) & (face < 3)
    on_west = (lane >= 120) & (face > 0)

    outside = on_east | on_west
    low = lax.rem(lane, 16) < 8

    def unpack(n, carry):
        for i in [4 * n + k for k in range(4)]:
            a, b = xa[rows_of(i), :], xb[rows_of(i), :]
            from_west = jnp.where(odd, a, b)
            from_east = jnp.where(odd, b, a)
            for half, at in enumerate(pair_of(i)):
                both = spread(from_west, from_east, half, low)
                for f in range(8):
                    fe[f, at, :] = jnp.where(outside, outer_of(both, f), 0.0)
        return carry

    lax.fori_loop(0, HALF // 4, unpack, 0)
    def body(i):
        for at in pair_of(i):

            def get(f):
                return [fld[f, 0, at, :], fld[f, 1, at, :], fe[f, at, :]]

            wet, ue, vn = (get(f) for f in (WET, UE, VN))
            wet_e = east_of(wet)
            qw_w = west_of([w * (KAPPA - 0.5 * u) for w, u in zip(wet, ue)])
            for t in range(3):
                w = wet[t]
                ce = w * (KAPPA + 0.5 * ue[t]) * wet_e[t]
                cw = w * qw_w[t]
                wn = jnp.where(row == ROWS - 1, 1.0, pltpu.roll(w, ROWS - 1, 0))
                qs = jnp.where(row == 0, 1.0, pltpu.roll(w * (KAPPA - 0.5 * vn[t]), 1, 0))
                cf[0, t, at, :] = ce
                cf[1, t, at, :] = cw
                cf[2, t, at, :] = w * (KAPPA + 0.5 * vn[t]) * wn
                cf[3, t, at, :] = w * qs
                cf[4, t, at, :] = w - ce - cw

    thirds(
        tri,
        lambda t, level: fe[WET, rows_of(level), :],
        lambda t, level: fe[VD, rows_of(level), :],
        (2,),
        body,
    )


def slot_of(level):
    return jnp.where(level < HALF, level, LEV + HALF - 1 - level)


def take_first_edges(ids, ya, yb, hn, hs, first):
    even = even_tile(ids)
    lane = iota((8, LANES), 1)

    def both(at):
        a, b = ya[at, :], yb[at, :]
        return turn(even, a, b)

    for f, k in enumerate((0, 1, 2) if first else (3, 4)):
        for t in range(2):
            for g in range(8):
                at = pl.ds(8 * g, 8)
                n, s = both(pl.ds((2 * k + t) * LEV + 8 * g, 8))
                hn[f, t, at, :] = n
                hs[f, t, at, :] = s
    low = lax.rem(lane, 16) < 8
    for g in range(4):
        wests = both(pl.ds(OUTER + 8 * g, 8))
        easts = both(pl.ds(OUTER + HALF + 8 * g, 8))
        for half in range(2):
            spreads = [spread(w, e, half, low) for w, e in zip(wests, easts)]

            def outer(side, f):
                return outer_of(spreads[side], f)

            at = pl.ds(HALF * half + 8 * g, 8)
            for f, k in enumerate((0, 1) if first else (2, 3)):
                hn[f, 2, at, :] = outer(0, k)
                hs[f, 2, at, :] = outer(1, k)
            if first:
                hn[2, 2, at, :] = outer(0, WET)
                hs[2, 2, at, :] = outer(1, WET) * (KAPPA - 0.5 * outer(1, VN))


def take_edges(ids, load, hn, hs, groups=(0, 8)):
    even = even_tile(ids)
    for f in range(2):
        oa, ob = load(32 + f)
        on, os = turn(even, oa, ob)
        for g in range(*groups):
            at = pl.ds(8 * g, 8)
            for t in range(2):
                a, b = load((f * 2 + t) * 8 + g)
                hn[f, t, at, :], hs[f, t, at, :] = turn(even, a, b)
            hn[f, 2, at, :] = edge_unpack(on, g)
            hs[f, 2, at, :] = edge_unpack(os, g)


def stencil(y, ref, level, coef, north_row, south_row, tiles=3):
    e, w = east_of(y), west_of(y)
    sub = iota((8, LANES), 0)
    base = pl.multiple_of(level * ROWS, ROWS)
    out = []
    for t in range(tiles):
        n = jnp.concatenate(
            [
                ref(t)[pl.ds(base + 1, 8), :],
                jnp.where(sub == 7, north_row[t], pltpu.roll(y[t][8:16], 7, 0)),
            ],
            0,
        )
        s = jnp.concatenate(
            [
                jnp.where(sub == 0, south_row[t], pltpu.roll(y[t][0:8], 1, 0)),
                ref(t)[pl.ds(base + 7, 8), :],
            ],
            0,
        )
        ce, cw, cn, cs, cc = coef[t]
        out.append(cc * y[t] + ce * e[t] + cw * w[t] + cn * n + cs * s)
    return out


def step(first, v0, ids, fld, fe, cfi, trm, tre, ya, yb, *refs):
    if first:
        wloc, cf, sol, oa, ob, fo, hn, hs = refs
    else:
        sol, oa, ob, fo, hn, hs = refs
    even = even_tile(ids)
    row = iota((ROWS, LANES), 0)
    take_first_edges(ids, ya, yb, hn, hs, first)

    def get(v, at):
        return [fld[v0 + v, 0, at, :], fld[v0 + v, 1, at, :], fe[v0 + v, at, :]]

    north_in = jnp.where(ids[1] < 31, 1.0, 0.0).astype(F32)
    south_in = jnp.where(ids[1] > 0, 1.0, 0.0).astype(F32)

    def apply(i, carry):
        for k in range(UNROLL_S):
            level = UNROLL_S * i + k
            at = rows_of(level)
            ones = [pl.ds(level, 1), pl.ds(level, 1), pl.ds(slot_of(level), 1)]
            coef = []
            for t in range(3):
                ce, cw, cn, cs, cc = (cfi[c, t, at, :] for c in range(5))
                if first:
                    cn = jnp.where(row == ROWS - 1, cn * (hn[2, t, ones[t], :] * north_in), cn)
                    cs = jnp.where(row == 0, cs * (hs[2, t, ones[t], :] * south_in), cs)
                    cc = cc - cn - cs
                    cf[2, t, at, :] = cn
                    cf[3, t, at, :] = cs
                    cf[4, t, at, :] = cc
                coef.append((ce, cw, cn, cs, cc))
            for v in range(2):
                n = [hn[v, t, ones[t], :] for t in range(3)]
                s = [hs[v, t, ones[t], :] for t in range(3)]
                f = v0 + v
                adj = stencil(
                    get(v, at), lambda t: fe.at[f] if t == 2 else fld.at[f, t], level, coef, n, s
                )
                for t in range(3):
                    sol[v, t, at, :] = adj[t]
        return carry

    lax.fori_loop(0, LEV // UNROLL_S, apply, 0)

    def put(v, t, at, x):
        sol[v, t, at, :] = x

    def load(v, t, at):
        return sol[v, t, at, :]

    top = eliminate(
        load,
        put,
        load,
        lambda k, t, at: tre[k, 0, at, :] if t == 2 else trm[k, t, at, :],
        [(v, t) for v in range(2) for t in range(3)],
    )[0]
    for v in range(2):
        y = get(v, pl.ds(0, ROWS))
        for t in range(3):
            fo[v, t] = y[t] + top[3 * v + t]
    put_edges(even, lambda f, t, g: edge_rows(sol.at[f, t], g), 2, oa, ob)
    if first:
        for c in range(2):
            for t in range(3):
                n = wloc[c, t, 8:16, :]
                s = wloc[c, t, 0:8, :]
                at = pl.ds(ROWS_2 + 8 * (3 * c + t), 8)
                oa[at, :], ob[at, :] = turn(even, n, s)


def last_stencil(v0, l0, nl, extra, carried, grads, *refs):
    ids, sol, cf, ya, yb = refs[:5]
    refs = refs[5:]
    fos = refs[:extra]
    refs = refs[extra:]
    if grads and carried:
        ua, ub = refs[:2]
        refs = refs[2:]
    if not grads:
        refs = refs[1:]
    if l0 or v0:
        refs = refs[1:]
    if grads:
        adj_out, g, ga, gb, hn, hs, en, es, buf, sem = refs
    else:
        adj_out, hn, hs, buf, sem = refs
    row = iota((ROWS, LANES), 0)
    even = even_tile(ids)
    low_half = iota((8, LANES), 0) < 4

    def load(block):
        if not grads:
            return ya[carried + block], yb[carried + block]
        at = pl.ds(8 * block, 8)
        return ya[at, :], yb[at, :]

    take_edges(ids, load, hn, hs, (l0 // 8, (l0 + nl) // 8))

    def edges(u, ts, ss):
        for t in range(3):
            a, b = ts[t], ss[t]
            n = jnp.where(low_half, pltpu.roll(a[8:16], 4, 0), b[8:16])
            s = jnp.where(low_half, a[0:8], pltpu.roll(b[0:8], 4, 0))
            if t < 2:
                ga[2 * u + t], gb[2 * u + t] = turn(even, n, s)
            else:
                en[u] = n
                es[u] = s

    def body(i, carry):
        for k in range(UNROLL_L):
            u = UNROLL_L * i + k
            level = l0 + u
            at = rows_of(level)
            one = pl.ds(level, 1)
            coef = [tuple(cf[c, t, at, :] for c in range(5)) for t in range(3)]
            both = []
            for v in range(2):
                y = [sol[v, t, at, :] for t in range(3)]
                n = [hn[v, t, one, :] for t in range(3)]
                s = [hs[v, t, one, :] for t in range(3)]
                x = stencil(y, lambda t: sol.at[v, t], level, coef, n, s, 3 if grads else 2)
                buf[u, v, :, 0:LANES] = x[0]
                buf[u, v, :, LANES : 2 * LANES] = x[1]
                if grads:
                    for t in range(3):
                        g[u, v, t] = x[t]
                both.append(x)
            if grads:
                edges(u, *both)
        return carry

    lax.fori_loop(0, nl // UNROLL_L, body, 0)
    copy = pltpu.make_async_copy(buf, adj_out.at[pl.ds(l0, nl), pl.ds(v0, 2)], sem)
    copy.start()
    if grads:
        for i, fo in enumerate(fos):
            pair = [[fo[v, t] for t in range(3)] for v in range(2)]
            for v in range(2):
                for t in range(3):
                    g[nl + i, v, t] = pair[v][t]
            edges(nl + i, *pair)
        units = nl + extra
        per = -(-units // 8)
        lane = iota((8, LANES), 1)
        for i in range(per):
            pn = ps = jnp.zeros((8, LANES), F32)
            for j in range(8):
                u = j * per + i
                if u < units:
                    mine = (lane >= 16 * j) & (lane < 16 * j + 16)
                    pn = jnp.where(mine, pltpu.roll(en[u], (16 * j + 8) % LANES, 1), pn)
                    ps = jnp.where(mine, pltpu.roll(es[u], (16 * j + 8) % LANES, 1), ps)
            ga[2 * units + i], gb[2 * units + i] = turn(even, pn, ps)
        if carried:
            for i in range(BLOCKS_2):
                ga[2 * units + per + i] = ua[pl.ds(8 * i, 8), :]
                gb[2 * units + per + i] = ub[pl.ds(8 * i, 8), :]
    copy.wait()


def smooth(units, u0, u1, ids, g, ga, gb, wloc, ya, yb, after, z0, z1, z2, z3, w5, hn, hs):
    del after
    zs = (z0, z1, z2, z3)
    face, tile = ids[0], ids[1]
    even = even_tile(ids)
    has_n, has_s = tile < 31, tile > 0
    sub = iota((8, LANES), 0)
    lane = iota((8, LANES), 1)
    low_half = sub < 4

    def stack3(lo, m0, m1, hi):
        r0, r1 = pltpu.roll(m0, 4, 0), pltpu.roll(m1, 4, 0)
        return [
            jnp.where(low_half, lo, r0),
            jnp.where(low_half, r0, r1),
            jnp.where(low_half, r1, hi),
        ]

    def north_of(k3):
        turned = [pltpu.roll(x, 7, 0) for x in k3]
        return [
            jnp.where(sub == 7, turned[1], turned[0]),
            jnp.where(sub == 7, turned[2], turned[1]),
            turned[2],
        ]

    def south_of(k3, below=None):
        turned = [pltpu.roll(x, 1, 0) for x in k3]
        return [
            turned[0] if below is None else jnp.where(sub == 0, below, turned[0]),
            jnp.where(sub == 0, turned[0], turned[1]),
            jnp.where(sub == 0, turned[1], turned[2]),
        ]

    we, wn, below = [], [], []
    for c, dest in ((0, we), (1, wn)):
        for t in range(3):
            at = pl.ds(ROWS_2 + 8 * (3 * c + t), 8)
            a, b = ya[at, :], yb[at, :]
            a, b = turn(even, a, b)
            hi = jnp.where(has_n, a, 0.0)
            lo = jnp.where(has_s, b, 0.0)
            if c == 1:
                below.append(pltpu.roll(lo, 5, 0))
            dest.append(
                stack3(pltpu.roll(lo, 4, 0), wloc[c, t, 0:8, :], wloc[c, t, 8:16, :], pltpu.roll(hi, 4, 0))
            )
    for k in range(3):
        cw3 = west_of([we[t][k] for t in range(3)])
        for t in range(3):
            ok = jnp.ones((8, LANES), F32)
            if k == 0:
                ok = jnp.where(low_half & (tile == 0), 0.0, ok)
            if k == 2:
                ok = jnp.where((~low_half) & (tile == 31), 0.0, ok)
            if t == 2:
                inside = ((lane < 64) & (face < 3)) | ((lane >= 64) & (face > 0))
                ok = jnp.where(inside, ok, 0.0)
            ce = we[t][k] * ok
            cw = cw3[t] * ok
            cn = wn[t][k] * ok
            cs = south_of(wn[t], below[t])[k] * ok
            w5[0, t, k] = ce
            w5[1, t, k] = cw
            w5[2, t, k] = cn
            w5[3, t, k] = cs
            w5[4, t, k] = 1.0 - ce - cw - cn - cs

    per = -(-units // 8)
    for u in range(u0, u1):
        j, i = divmod(u, per)
        a, b = ga[2 * units + i], gb[2 * units + i]
        a, b = turn(even, a, b)
        n = edge_unpack(a, j)
        s = edge_unpack(b, j)
        u -= u0
        hn[u] = jnp.where(has_n, n, 0.0)
        hs[u] = jnp.where(has_s, s, 0.0)

    bit0 = lax.rem(face, 2) == 1
    bit1 = face >= 2

    def body(i, carry):
        fields = []
        for u in [UNROLL_M * i + k for k in range(UNROLL_M)]:
            hi, lo = [], []
            for t in range(2):
                a, b = ga[2 * (u0 + u) + t], gb[2 * (u0 + u) + t]
                a, b = turn(even, a, b)
                hi.append(jnp.where(has_n, a, 0.0))
                lo.append(jnp.where(has_s, b, 0.0))
            hi.append(hn[u])
            lo.append(hs[u])
            for v in range(2):
                x = []
                for t in range(3):
                    m = g[u0 + u, v, t]
                    top = pltpu.roll(hi[t], 4, 0) if v == 0 else hi[t]
                    bottom = lo[t] if v == 0 else pltpu.roll(lo[t], 4, 0)
                    x.append(stack3(bottom, m[0:8], m[8:16], top))
                fields.append(x)
        for sweep in range(4):
            kept = 3 if sweep < 3 else 2
            coefs = [[[w5[c, t, k] for c in range(5)] for k in range(3)] for t in range(3)]
            swept = []
            for x in fields:
                ns = [north_of(x[t]) for t in range(kept)]
                ss = [south_of(x[t]) for t in range(kept)]
                new = [[], [], []]
                for k in range(3):
                    at_k = [x[t][k] for t in range(3)]
                    e, w = east_of(at_k), west_of(at_k)
                    for t in range(kept):
                        ce, cw, cn, cs, cc = coefs[t][k]
                        new[t].append(
                            cc * x[t][k] + ce * e[t] + cw * w[t] + cn * ns[t][k] + cs * ss[t][k]
                        )
                swept.append(new)
            fields = swept
        for c, x in enumerate(fields):
            u = UNROLL_M * i + c // 2
            for t in range(2):
                p = [pltpu.roll(x[t][0], 4, 0), x[t][1], pltpu.roll(x[t][1], 4, 0), x[t][2]]
                p = [jnp.where(bit0, p[d ^ 1], p[d]) for d in range(4)]
                p = [jnp.where(bit1, p[d ^ 2], p[d]) for d in range(4)]
                for k in range(4):
                    zs[k][2 * u + c % 2, :, t * LANES : (t + 1) * LANES] = p[k][0:4]
        return carry

    lax.fori_loop(0, (u1 - u0) // UNROLL_M, body, 0)


def gather_rows(first, size, ids, z0, z1, z2, z3, *refs):
    out, sem = refs[-2:]
    copies = []
    for k, z in enumerate((z0, z1, z2, z3)):
        cols = pl.multiple_of(jnp.bitwise_xor(ids[0], k) * 256, 256)
        dst = out.at[pl.ds(first, size), :, pl.ds(cols, 256)]
        copies.append(pltpu.make_async_copy(z, dst, sem.at[k]))
    for copy in copies:
        copy.start()
    for copy in copies:
        copy.wait()


def on_device(adjoint_seed, face_flow, vert_diff, wet_mask, smooth_weights):
    ids = jnp.stack([lax.axis_index("face"), lax.axis_index("tile")]).astype(jnp.int32)
    tiles = lax.axis_size("tile")
    pair_a = [(i, i ^ 1) for i in range(tiles)]
    pair_b = [(i, (i + (1 if i % 2 else -1)) % tiles) for i in range(tiles)]
    side_a = [(0, 1), (1, 0), (2, 3), (3, 2)]
    side_b = [(0, 0), (1, 2), (2, 1), (3, 3)]
    hbm, any_space = pltpu.HBM, pl.ANY

    def across(a, b):
        return lax.ppermute(a, "tile", pair_b), lax.ppermute(b, "tile", pair_a)

    def to_face(x, k):
        return lax.ppermute(x, "face", [(i, i ^ k) for i in range(4)])

    edge = (ROWS, LANES)
    packed = (HALF * ROWS, LANES)
    fld, tri, pxa, pxb = call(
        first_solve,
        [((8, 2, FLAT, LANES), VM), ((3, 2, FLAT, LANES), VM), (packed, VM), (packed, VM)],
        [
            VM((2, LEV) + edge, jnp.int32),
            VM((FLAT, LANES), F32),
            pltpu.SemaphoreType.DMA((16,)),
        ],
        limit=5,
        ins=[None] + [hbm] * 4,
        name="first_solve",
    )(ids, adjoint_seed, face_flow, vert_diff, wet_mask)
    weights = [smooth_weights] + [to_face(smooth_weights, k) for k in (1, 2, 3)]
    (wloc,) = call(
        local_weights,
        [((2, 3) + edge, VM)],
        [VM((4, 2, 4, 1024), F32)],
        limit=4,
        name="local_weights",
    )(ids, *weights)
    pxa, pxb, wloc = lax.optimization_barrier((pxa, pxb, wloc))
    xa = lax.ppermute(pxa, "face", side_a)
    xb = lax.ppermute(pxb, "face", side_b)
    rows_1 = ((ROWS_1, LANES), VM)
    ya, yb = call(main_edges, [rows_1, rows_1], limit=4, name="main_edges")(ids, fld)
    ya, yb = call(
        outer_edges, [rows_1, rows_1], limit=4, alias={3: 0, 4: 1}, name="outer_edges"
    )(ids, xa, xb, ya, yb)
    ya, yb = across(ya, yb)
    fe, cf, tre = call(
        coefficients,
        [((8, FLAT, LANES), VM), ((5, 3, FLAT, LANES), VM), ((3, 1, FLAT, LANES), VM)],
        limit=4,
        name="coefficients",
    )(ids, fld, xa, xb)
    halo = VM((3, 3, LEV, LANES), F32)
    sol_shape = ((2, 3, FLAT, LANES), VM)
    fo_shape = ((2, 3) + edge, VM)
    rows_w = ((ROWS_2 + 48, LANES), VM)
    rows_2 = ((ROWS_2, LANES), VM)
    cf, sol_t, ta, tb, fo_t = call(
        functools.partial(step, True, 0),
        [((5, 3, FLAT, LANES), VM), sol_shape, rows_w, rows_w, fo_shape],
        [halo, halo],
        limit=4,
        alias={3: 0},
        name="step_ts",
    )(ids, fld, fe, cf, tri, tre, ya, yb, wloc)
    ta, tb = across(ta, tb)
    sol_u, ua, ub, fo_u = call(
        functools.partial(step, False, 2),
        [sol_shape, rows_2, rows_2, fo_shape],
        [halo, halo],
        limit=4,
        name="step_uv",
    )(ids, fld, fe, cf, tri, tre, ya, yb)

    adj_shape = adjoint_seed.shape
    adj = None
    chunks = []
    for l0, l1 in CHUNKS:
        nl = l1 - l0
        fos = [fo_t, fo_u] if l1 == LEV else []
        units = nl + len(fos)
        per = -(-units // 8)
        args = [ids, sol_t, cf, ta, tb] + fos
        blocks = 2 * units + per
        carried = 0
        if len(chunks) == CARRIER:
            args += [ua, ub]
            carried = blocks
            blocks += BLOCKS_2
        spaces = [None] + [VM] * (len(args) - 1)
        alias = {}
        if adj is not None:
            alias = {len(args): 0}
            args.append(adj)
            spaces.append(any_space)
        adj, g, ga, gb = call(
            functools.partial(last_stencil, 0, l0, nl, len(fos), carried, True),
            [
                (adj_shape, any_space),
                ((units, 2, 3) + edge, VM),
                ((blocks, 8, LANES), VM),
                ((blocks, 8, LANES), VM),
            ],
            [
                halo,
                halo,
                VM((units, 8, LANES), F32),
                VM((units, 8, LANES), F32),
                VM((nl, 2, ROWS, 256), F32),
                pltpu.SemaphoreType.DMA,
            ],
            limit=6,
            alias=alias,
            ins=spaces,
            name="last_ts_%d" % l0,
        )(*args)
        ga, gb = across(ga, gb)
        chunks.append((units, g, ga, gb, carried))

    controls = None
    after = chunks[-1][1]
    sent = []
    first = 0

    def gather(controls, first, size, parts):
        args = [ids] + parts
        alias = {}
        if controls is not None:
            alias = {len(args): 0}
            args.append(controls)
        (controls,) = call(
            functools.partial(gather_rows, first, size),
            [((2 * (LEV + 2), 4, 1024), any_space)],
            [pltpu.SemaphoreType.DMA((4,))],
            ins=[None] + [any_space] * (len(args) - 1),
            limit=4,
            alias=alias,
            name="gather_%d" % first,
        )(*args)
        return controls

    for c, u0, u1 in PIECES:
        units, g, ga, gb, _ = chunks[c]
        n = u1 - u0
        zs = call(
            functools.partial(smooth, units, u0, u1),
            [((2 * n, 4, 256), VM)] * 4,
            [
                VM((5, 3, 3, 8, LANES), F32),
                VM((n, 8, LANES), F32),
                VM((n, 8, LANES), F32),
            ],
            ins=[None] + [VM] * 6 + [any_space],
            limit=4,
            name="smooth_%d_%d" % (c, u0),
        )(ids, g, ga, gb, wloc, ta, tb, after)
        after = zs[0]
        sent.append((first, 2 * n, [zs[0]] + [to_face(zs[k], k) for k in (1, 2, 3)]))
        first += 2 * n
    _, _, ga, gb, carried = chunks[CARRIER]
    (adj,) = call(
        functools.partial(last_stencil, 2, 0, LEV, 0, carried, False),
        [(adj_shape, any_space)],
        [halo, halo, VM((LEV, 2, ROWS, 256), F32), pltpu.SemaphoreType.DMA],
        limit=6,
        alias={6: 0},
        ins=[None] + [VM] * 4 + [any_space] * 2,
        name="last_uv",
    )(ids, sol_u, cf, ga, gb, after, adj)
    for start, size, parts in sent:
        controls = gather(controls, start, size, parts)
    return adj, controls


def solution(mesh):
    placed = (
        P(None, None, "tile", "face"),
        P(None, None, "tile", "face"),
        P(None, "tile", "face"),
        P(None, "tile", "face"),
        P(None, ("tile", "face"), None),
    )
    return jax.shard_map(
        on_device,
        mesh=mesh,
        in_specs=placed,
        out_specs=(P(None, None, "tile", "face"), P(None, ("tile", "face"), None)),
        check_vma=False,
    )
```

```python
import functools

import jax
import jax.numpy as jnp
from jax import lax
from jax.experimental import pallas as pl
from jax.experimental.pallas import tpu as pltpu
from jax.sharding import PartitionSpec as P

F32 = jnp.float32
LEV = 64
ROWS = 16
LANES = 128
FLAT = LEV * ROWS
WET, UE, VN, VD = 4, 5, 6, 7
KAPPA = 0.15
MIB = 2**20
UNROLL_S = 8
UNROLL_L = 8
UNROLL_M = 2

CHUNKS = ((0, 24), (24, 64))
PIECES = ((0, 0, 24), (1, 0, 22), (1, 22, 42))
CARRIER = 0


def iota(shape, dim):
    return lax.broadcasted_iota(jnp.int32, shape, dim)


def rows_of(level):
    return pl.ds(pl.multiple_of(level * ROWS, ROWS), ROWS)


def east_of(tiles):
    last = iota(tiles[0].shape, 1) == LANES - 1
    turned = [pltpu.roll(t, LANES - 1, 1) for t in tiles]
    return [jnp.where(last, turned[(i + 1) % 3], turned[i]) for i in range(3)]


def west_of(tiles):
    first = iota(tiles[0].shape, 1) == 0
    turned = [pltpu.roll(t, 1, 1) for t in tiles]
    return [jnp.where(first, turned[(i + 2) % 3], turned[i]) for i in range(3)]


def call(kernel, outs, scratch=(), limit=8, alias=None, name=None, ins=None):
    def run(*args):
        args = list(args)
        specs = [pl.BlockSpec(memory_space=pltpu.SMEM)]
        for i in range(1, len(args)):
            if ins is not None and ins[i] is pltpu.HBM:
                args[i] = pltpu.with_memory_space_constraint(args[i], pltpu.HBM)
        for i in range(1, len(args)):
            space = pltpu.VMEM if ins is None else ins[i]
            specs.append(pl.BlockSpec(memory_space=space))
        return pl.pallas_call(
            kernel,
            out_shape=[jax.ShapeDtypeStruct(s, F32) for s, _ in outs],
            in_specs=specs,
            out_specs=[pl.BlockSpec(memory_space=m) for _, m in outs],
            scratch_shapes=list(scratch),
            input_output_aliases=alias or {},
            compiler_params=pltpu.CompilerParams(vmem_limit_bytes=limit * MIB),
            name=name,
        )(*args)

    return run


VM = pltpu.VMEM


HALF = LEV // 2


def pair_of(i):
    return rows_of(i), rows_of(LEV - 1 - i)


def thirds(tri, wet, vd, tiles, beside=None):
    zero = jnp.zeros((ROWS, LANES), F32)

    def one(i, carry):
        low, rat, low2, rat2 = ([], [], [], [])
        top, bottom = pair_of(i)
        for t in tiles:
            w = wet(t, i)
            up = vd(t, i) * w * wet(t, i + 1)
            p, q = carry[0][t - tiles[0]], carry[1][t - tiles[0]]
            inv = 1.0 / (1.0 + p + up - p * q)
            r = up * inv
            tri[0, t - tiles[0], top, :] = p
            tri[1, t - tiles[0], top, :] = inv
            tri[2, t - tiles[0], top, :] = r
            low.append(up)
            rat.append(r)
            j = LEV - 1 - i
            up = vd(t, j - 1) * wet(t, j - 1) * wet(t, j)
            p, q = carry[2][t - tiles[0]], carry[3][t - tiles[0]]
            inv = 1.0 / (1.0 + p + up - p * q)
            r = up * inv
            tri[0, t - tiles[0], bottom, :] = p
            tri[1, t - tiles[0], bottom, :] = inv
            tri[2, t - tiles[0], bottom, :] = r
            low2.append(up)
            rat2.append(r)
        if beside is not None:
            beside(i)
        return low, rat, low2, rat2

    def body(m, carry):
        return one(2 * m + 1, one(2 * m, carry))

    n = len(tiles)
    lax.fori_loop(0, HALF // 2, body, tuple([zero] * n for _ in range(4)))


def eliminate(rhs, put, get, tri, items, beside=None):
    zero = jnp.zeros((ROWS, LANES), F32)
    n = len(items)

    def inwards(i, carry):
        out = ([], [])
        for side, at in enumerate(pair_of(i)):
            for c, (key, t) in enumerate(items):
                x = (rhs(key, t, at) + tri(0, t, at) * carry[side][c]) * tri(1, t, at)
                put(key, t, at, x)
                out[side].append(x)
        return out

    ends = lax.fori_loop(0, HALF, inwards, ([zero] * n, [zero] * n))
    at, bt = pair_of(HALF - 1)
    start = ([], [])
    for c, (key, t) in enumerate(items):
        r, r2 = tri(2, t, at), tri(2, t, bt)
        y = (ends[0][c] + r * ends[1][c]) * (1.0 / (1.0 - r * r2))
        y2 = ends[1][c] + r2 * y
        put(key, t, at, y)
        put(key, t, bt, y2)
        start[0].append(y)
        start[1].append(y2)
    if beside is not None:
        beside(HALF - 1, start)

    def outwards(k, carry):
        out = ([], [])
        for side, at in enumerate(pair_of(HALF - 2 - k)):
            for c, (key, t) in enumerate(items):
                x = get(key, t, at) + tri(2, t, at) * carry[side][c]
                put(key, t, at, x)
                out[side].append(x)
        if beside is not None:
            beside(HALF - 2 - k, out)
        return out

    return lax.fori_loop(0, HALF - 1, outwards, start)


def first_solve(ids, seed, flow, vd, wet, fld, tri, pxa, pxb, wbuf, pw, sems):
    def tile_copy(src, dst, k):
        copy = pltpu.make_async_copy(src, dst, sems.at[k])
        copy.start()
        return copy

    def place(f, t):
        return fld.at[f, t].reshape(LEV, ROWS, LANES)

    early, late = [], []
    for t in range(2):
        cols = pl.ds(t * LANES, LANES)
        early.append(tile_copy(wet.at[:, :, cols], wbuf.at[t], 8 * t))
        early.append(tile_copy(vd.at[:, :, cols], place(VD, t), 8 * t + 1))
        for v in range(2):
            early.append(tile_copy(flow.at[v, :, :, cols], place(UE + v, t), 8 * t + 2 + v))
    for t in range(2):
        cols = pl.ds(t * LANES, LANES)
        for v in range(4):
            late.append(tile_copy(seed.at[:, v, :, cols], place(v, t), 8 * t + 4 + v))
    for copy in early:
        copy.wait()

    def wet_to_float(i, carry):
        for k in range(8):
            for t in range(2):
                fld[WET, t, rows_of(8 * i + k), :] = wbuf[t, 8 * i + k].astype(F32)
        return carry

    lax.fori_loop(0, LEV // 8, wet_to_float, 0)
    lane = iota((ROWS, LANES), 1)
    first8 = lane < 8
    odd = lax.rem(ids[0], 2) == 1

    def pack(at, fields):
        out = jnp.zeros((ROWS, LANES), F32)
        for f in fields:
            edge = jnp.where(first8, fld[f, 0, at, :], fld[f, 1, at, :])
            mine = (lane >= 16 * f) & (lane < 16 * f + 16)
            by = (16 * f + 8) % LANES
            out = jnp.where(mine, pltpu.roll(edge, by, 1) if by else edge, out)
        return out

    def statics(i):
        top, bottom = pair_of(i)
        pw[top, :] = pack(top, range(4, 8))
        pw[bottom, :] = pack(bottom, range(4, 8))

    thirds(
        tri,
        lambda t, level: fld[WET, t, rows_of(level), :],
        lambda t, level: fld[VD, t, rows_of(level), :],
        (0, 1),
        statics,
    )
    for copy in late:
        copy.wait()

    def put(v, t, at, x):
        fld[v, t, at, :] = x

    for pair in ((0, 1), (2, 3)):
        eliminate(
            lambda v, t, at: fld[v, t, at, :] * fld[WET, t, at, :],
            put,
            lambda v, t, at: fld[v, t, at, :],
            lambda k, t, at: tri[k, t, at, :],
            [(v, t) for v in pair for t in range(2)],
        )

    low = lax.rem(lane, 16) < 8

    def states(n, carry):
        for i in [4 * n + k for k in range(4)]:
            top, bottom = pair_of(i)
            a = pw[top, :] + pack(top, range(4))
            b = pw[bottom, :] + pack(bottom, range(4))
            east = jnp.where(low, a, pltpu.roll(b, 8, 1))
            west = jnp.where(low, pltpu.roll(a, LANES - 8, 1), b)
            at = rows_of(i)
            pxa[at, :] = jnp.where(odd, west, east)
            pxb[at, :] = jnp.where(odd, east, west)
        return carry

    lax.fori_loop(0, HALF // 4, states, 0)


def spread(west, east, half, low):
    if half == 0:
        return jnp.where(low, west, pltpu.roll(east, 8, 1))
    return jnp.where(low, pltpu.roll(west, LANES - 8, 1), east)


def outer_of(both, f):
    by = (120 - 16 * f) % LANES
    return pltpu.roll(both, by, 1) if by else both


OUTER = 5 * 2 * LEV
ROWS_1 = OUTER + LEV
ROWS_2 = 2 * 2 * LEV + 2 * 8
BLOCKS_2 = ROWS_2 // 8


def edge_pack(tiles8):
    lane = iota((8, LANES), 1)
    packed = jnp.zeros((8, LANES), F32)
    for g, t in enumerate(tiles8):
        turned = pltpu.roll(t, (16 * g + 8) % LANES, 1)
        packed = jnp.where((lane >= 16 * g) & (lane < 16 * g + 16), turned, packed)
    return packed


def edge_unpack(packed, g):
    return pltpu.roll(packed, (-(16 * g + 8)) % LANES, 1)


def even_tile(ids):
    return lax.rem(ids[1], 2) == 0


def turn(even, x, y):
    return jnp.where(even, y, x), jnp.where(even, x, y)


def put_edges(even, pick, fields, oa, ob):
    for f in range(fields):
        for t in range(2):
            for g in range(8):
                n, s = pick(f, t, g)
                at = pl.ds((f * 2 + t) * LEV + 8 * g, 8)
                oa[at, :], ob[at, :] = turn(even, n, s)
        outer = [pick(f, 2, g) for g in range(8)]
        n = edge_pack([o[0] for o in outer])
        s = edge_pack([o[1] for o in outer])
        at = pl.ds(fields * 2 * LEV + 8 * f, 8)
        oa[at, :], ob[at, :] = turn(even, n, s)


def edge_rows(ref, g):
    north = ref[pl.ds(g * 8 * ROWS + ROWS - 1, 8, stride=ROWS), :]
    south = ref[pl.ds(g * 8 * ROWS, 8, stride=ROWS), :]
    return north, south


def main_edges(ids, fld, ya, yb):
    even = even_tile(ids)
    for k, f in enumerate((0, 1, WET, 2, 3)):
        for t in range(2):
            for g in range(8):
                n, s = edge_rows(fld.at[f, t], g)
                if f == WET:
                    n = n * (KAPPA - 0.5 * edge_rows(fld.at[VN, t], g)[0])
                at = pl.ds((2 * k + t) * LEV + 8 * g, 8)
                ya[at, :], yb[at, :] = turn(even, n, s)


def outer_edges(ids, xa, xb, ya_in, yb_in, ya, yb):
    face, tile = ids[0], ids[1]
    odd = lax.rem(face, 2) == 1
    even = even_tile(ids)
    for g in range(4):
        na, sa = edge_rows(xa, g)
        nb, sb = edge_rows(xb, g)
        west = (jnp.where(odd, na, nb), jnp.where(odd, sa, sb))
        east = (jnp.where(odd, nb, na), jnp.where(odd, sb, sa))
        for first, inside, (n, s) in ((0, face > 0, west), (HALF, face < 3, east)):
            n = jnp.where(inside, n, 0.0)
            s = jnp.where(inside, s, 0.0)
            at = pl.ds(OUTER + first + 8 * g, 8)
            ya[at, :], yb[at, :] = turn(even, n, s)


def local_weights(ids, w0, w1, w2, w3, wloc, pieces):
    face = ids[0]
    for k, w in enumerate((w0, w1, w2, w3)):
        pieces[k] = w[...]
    lane4 = iota((4, LANES), 1)
    for d in range(4):
        slot = jnp.bitwise_xor(face, d)
        for c in range(2):
            for t in range(3):
                at = pl.ds(4 * d, 4)
                if t < 2:
                    first = pl.multiple_of((2 * face + t) * LANES, LANES)
                    wloc[c, t, at, :] = pieces[slot, c, :, pl.ds(first, LANES)]
                    continue
                first = pl.multiple_of(jnp.minimum(2 * face + 2, 7) * LANES, LANES)
                e = pieces[slot, c, :, pl.ds(first, LANES)]
                first = pl.multiple_of(jnp.maximum(2 * face - 1, 0) * LANES, LANES)
                w = pieces[slot, c, :, pl.ds(first, LANES)]
                w = jnp.where((lane4 >= 120) & (face > 0), w, 0.0)
                wloc[c, t, at, :] = jnp.where((lane4 < 8) & (face < 3), e, w)


def coefficients(ids, fld, xa, xb, fe, cf, tri):
    row = iota((ROWS, LANES), 0)
    face = ids[0]
    odd = lax.rem(face, 2) == 1
    lane = iota((ROWS, LANES), 1)
    on_east = (lane < 8) & (face < 3)
    on_west = (lane >= 120) & (face > 0)

    outside = on_east | on_west
    low = lax.rem(lane, 16) < 8

    def unpack(n, carry):
        for i in [4 * n + k for k in range(4)]:
            a, b = xa[rows_of(i), :], xb[rows_of(i), :]
            from_west = jnp.where(odd, a, b)
            from_east = jnp.where(odd, b, a)
            for half, at in enumerate(pair_of(i)):
                both = spread(from_west, from_east, half, low)
                for f in range(8):
                    fe[f, at, :] = jnp.where(outside, outer_of(both, f), 0.0)
        return carry

    lax.fori_loop(0, HALF // 4, unpack, 0)
    def body(i):
        for at in pair_of(i):

            def get(f):
                return [fld[f, 0, at, :], fld[f, 1, at, :], fe[f, at, :]]

            wet, ue, vn = (get(f) for f in (WET, UE, VN))
            wet_e = east_of(wet)
            qw_w = west_of([w * (KAPPA - 0.5 * u) for w, u in zip(wet, ue)])
            for t in range(3):
                w = wet[t]
                ce = w * (KAPPA + 0.5 * ue[t]) * wet_e[t]
                cw = w * qw_w[t]
                wn = jnp.where(row == ROWS - 1, 1.0, pltpu.roll(w, ROWS - 1, 0))
                qs = jnp.where(row == 0, 1.0, pltpu.roll(w * (KAPPA - 0.5 * vn[t]), 1, 0))
                cf[0, t, at, :] = ce
                cf[1, t, at, :] = cw
                cf[2, t, at, :] = w * (KAPPA + 0.5 * vn[t]) * wn
                cf[3, t, at, :] = w * qs
                cf[4, t, at, :] = w - ce - cw

    thirds(
        tri,
        lambda t, level: fe[WET, rows_of(level), :],
        lambda t, level: fe[VD, rows_of(level), :],
        (2,),
        body,
    )


def slot_of(level):
    return jnp.where(level < HALF, level, LEV + HALF - 1 - level)


def take_first_edges(ids, ya, yb, hn, hs, first):
    even = even_tile(ids)
    lane = iota((8, LANES), 1)

    def both(at):
        a, b = ya[at, :], yb[at, :]
        return turn(even, a, b)

    for f, k in enumerate((0, 1, 2) if first else (3, 4)):
        for t in range(2):
            for g in range(8):
                at = pl.ds(8 * g, 8)
                n, s = both(pl.ds((2 * k + t) * LEV + 8 * g, 8))
                hn[f, t, at, :] = n
                hs[f, t, at, :] = s
    low = lax.rem(lane, 16) < 8
    for g in range(4):
        wests = both(pl.ds(OUTER + 8 * g, 8))
        easts = both(pl.ds(OUTER + HALF + 8 * g, 8))
        for half in range(2):
            spreads = [spread(w, e, half, low) for w, e in zip(wests, easts)]

            def outer(side, f):
                return outer_of(spreads[side], f)

            at = pl.ds(HALF * half + 8 * g, 8)
            for f, k in enumerate((0, 1) if first else (2, 3)):
                hn[f, 2, at, :] = outer(0, k)
                hs[f, 2, at, :] = outer(1, k)
            if first:
                hn[2, 2, at, :] = outer(0, WET)
                hs[2, 2, at, :] = outer(1, WET) * (KAPPA - 0.5 * outer(1, VN))


def take_edges(ids, load, hn, hs, groups=(0, 8)):
    even = even_tile(ids)
    for f in range(2):
        oa, ob = load(32 + f)
        on, os = turn(even, oa, ob)
        for g in range(*groups):
            at = pl.ds(8 * g, 8)
            for t in range(2):
                a, b = load((f * 2 + t) * 8 + g)
                hn[f, t, at, :], hs[f, t, at, :] = turn(even, a, b)
            hn[f, 2, at, :] = edge_unpack(on, g)
            hs[f, 2, at, :] = edge_unpack(os, g)


def stencil(y, ref, level, coef, north_row, south_row, tiles=3):
    e, w = east_of(y), west_of(y)
    sub = iota((8, LANES), 0)
    base = pl.multiple_of(level * ROWS, ROWS)
    out = []
    for t in range(tiles):
        n = jnp.concatenate(
            [
                ref(t)[pl.ds(base + 1, 8), :],
                jnp.where(sub == 7, north_row[t], pltpu.roll(y[t][8:16], 7, 0)),
            ],
            0,
        )
        s = jnp.concatenate(
            [
                jnp.where(sub == 0, south_row[t], pltpu.roll(y[t][0:8], 1, 0)),
                ref(t)[pl.ds(base + 7, 8), :],
            ],
            0,
        )
        ce, cw, cn, cs, cc = coef[t]
        out.append(cc * y[t] + ce * e[t] + cw * w[t] + cn * n + cs * s)
    return out


def step(first, v0, ids, fld, fe, cfi, trm, tre, ya, yb, *refs):
    if first:
        wloc, cf, sol, oa, ob, fo, hn, hs = refs
    else:
        sol, oa, ob, fo, hn, hs = refs
    even = even_tile(ids)
    row = iota((ROWS, LANES), 0)
    take_first_edges(ids, ya, yb, hn, hs, first)

    def get(v, at):
        return [fld[v0 + v, 0, at, :], fld[v0 + v, 1, at, :], fe[v0 + v, at, :]]

    north_in = jnp.where(ids[1] < 31, 1.0, 0.0).astype(F32)
    south_in = jnp.where(ids[1] > 0, 1.0, 0.0).astype(F32)

    def apply(i, carry):
        for k in range(UNROLL_S):
            level = UNROLL_S * i + k
            at = rows_of(level)
            ones = [pl.ds(level, 1), pl.ds(level, 1), pl.ds(slot_of(level), 1)]
            coef = []
            for t in range(3):
                ce, cw, cn, cs, cc = (cfi[c, t, at, :] for c in range(5))
                if first:
                    cn = jnp.where(row == ROWS - 1, cn * (hn[2, t, ones[t], :] * north_in), cn)
                    cs = jnp.where(row == 0, cs * (hs[2, t, ones[t], :] * south_in), cs)
                    cc = cc - cn - cs
                    cf[2, t, at, :] = cn
                    cf[3, t, at, :] = cs
                    cf[4, t, at, :] = cc
                coef.append((ce, cw, cn, cs, cc))
            for v in range(2):
                n = [hn[v, t, ones[t], :] for t in range(3)]
                s = [hs[v, t, ones[t], :] for t in range(3)]
                f = v0 + v
                adj = stencil(
                    get(v, at), lambda t: fe.at[f] if t == 2 else fld.at[f, t], level, coef, n, s
                )
                for t in range(3):
                    sol[v, t, at, :] = adj[t]
        return carry

    lax.fori_loop(0, LEV // UNROLL_S, apply, 0)

    def put(v, t, at, x):
        sol[v, t, at, :] = x

    def load(v, t, at):
        return sol[v, t, at, :]

    top = eliminate(
        load,
        put,
        load,
        lambda k, t, at: tre[k, 0, at, :] if t == 2 else trm[k, t, at, :],
        [(v, t) for v in range(2) for t in range(3)],
    )[0]
    for v in range(2):
        y = get(v, pl.ds(0, ROWS))
        for t in range(3):
            fo[v, t] = y[t] + top[3 * v + t]
    put_edges(even, lambda f, t, g: edge_rows(sol.at[f, t], g), 2, oa, ob)
    if first:
        for c in range(2):
            for t in range(3):
                n = wloc[c, t, 8:16, :]
                s = wloc[c, t, 0:8, :]
                at = pl.ds(ROWS_2 + 8 * (3 * c + t), 8)
                oa[at, :], ob[at, :] = turn(even, n, s)


def last_stencil(v0, l0, nl, extra, carried, grads, *refs):
    ids, sol, cf, ya, yb = refs[:5]
    refs = refs[5:]
    fos = refs[:extra]
    refs = refs[extra:]
    if grads and carried:
        ua, ub = refs[:2]
        refs = refs[2:]
    if not grads:
        refs = refs[1:]
    if l0 or v0:
        refs = refs[1:]
    if grads:
        adj_out, g, ga, gb, hn, hs, en, es, buf, sem = refs
    else:
        adj_out, hn, hs, buf, sem = refs
    row = iota((ROWS, LANES), 0)
    even = even_tile(ids)
    low_half = iota((8, LANES), 0) < 4

    def load(block):
        if not grads:
            return ya[carried + block], yb[carried + block]
        at = pl.ds(8 * block, 8)
        return ya[at, :], yb[at, :]

    take_edges(ids, load, hn, hs, (l0 // 8, (l0 + nl) // 8))

    def edges(u, ts, ss):
        for t in range(3):
            a, b = ts[t], ss[t]
            n = jnp.where(low_half, pltpu.roll(a[8:16], 4, 0), b[8:16])
            s = jnp.where(low_half, a[0:8], pltpu.roll(b[0:8], 4, 0))
            if t < 2:
                ga[2 * u + t], gb[2 * u + t] = turn(even, n, s)
            else:
                en[u] = n
                es[u] = s

    def body(i, carry):
        for k in range(UNROLL_L):
            u = UNROLL_L * i + k
            level = l0 + u
            at = rows_of(level)
            one = pl.ds(level, 1)
            coef = [tuple(cf[c, t, at, :] for c in range(5)) for t in range(3)]
            both = []
            for v in range(2):
                y = [sol[v, t, at, :] for t in range(3)]
                n = [hn[v, t, one, :] for t in range(3)]
                s = [hs[v, t, one, :] for t in range(3)]
                x = stencil(y, lambda t: sol.at[v, t], level, coef, n, s, 3 if grads else 2)
                buf[u, v, :, 0:LANES] = x[0]
                buf[u, v, :, LANES : 2 * LANES] = x[1]
                if grads:
                    for t in range(3):
                        g[u, v, t] = x[t]
                both.append(x)
            if grads:
                edges(u, *both)
        return carry

    lax.fori_loop(0, nl // UNROLL_L, body, 0)
    copy = pltpu.make_async_copy(buf, adj_out.at[pl.ds(l0, nl), pl.ds(v0, 2)], sem)
    copy.start()
    if grads:
        for i, fo in enumerate(fos):
            pair = [[fo[v, t] for t in range(3)] for v in range(2)]
            for v in range(2):
                for t in range(3):
                    g[nl + i, v, t] = pair[v][t]
            edges(nl + i, *pair)
        units = nl + extra
        per = -(-units // 8)
        lane = iota((8, LANES), 1)
        for i in range(per):
            pn = ps = jnp.zeros((8, LANES), F32)
            for j in range(8):
                u = j * per + i
                if u < units:
                    mine = (lane >= 16 * j) & (lane < 16 * j + 16)
                    pn = jnp.where(mine, pltpu.roll(en[u], (16 * j + 8) % LANES, 1), pn)
                    ps = jnp.where(mine, pltpu.roll(es[u], (16 * j + 8) % LANES, 1), ps)
            ga[2 * units + i], gb[2 * units + i] = turn(even, pn, ps)
        if carried:
            for i in range(BLOCKS_2):
                ga[2 * units + per + i] = ua[pl.ds(8 * i, 8), :]
                gb[2 * units + per + i] = ub[pl.ds(8 * i, 8), :]
    copy.wait()


def smooth(units, u0, u1, ids, g, ga, gb, wloc, ya, yb, after, z0, z1, z2, z3, w5, hn, hs):
    del after
    zs = (z0, z1, z2, z3)
    face, tile = ids[0], ids[1]
    even = even_tile(ids)
    has_n, has_s = tile < 31, tile > 0
    sub = iota((8, LANES), 0)
    lane = iota((8, LANES), 1)
    low_half = sub < 4

    def stack3(lo, m0, m1, hi):
        r0, r1 = pltpu.roll(m0, 4, 0), pltpu.roll(m1, 4, 0)
        return [
            jnp.where(low_half, lo, r0),
            jnp.where(low_half, r0, r1),
            jnp.where(low_half, r1, hi),
        ]

    def north_of(k3):
        turned = [pltpu.roll(x, 7, 0) for x in k3]
        return [
            jnp.where(sub == 7, turned[1], turned[0]),
            jnp.where(sub == 7, turned[2], turned[1]),
            turned[2],
        ]

    def south_of(k3, below=None):
        turned = [pltpu.roll(x, 1, 0) for x in k3]
        return [
            turned[0] if below is None else jnp.where(sub == 0, below, turned[0]),
            jnp.where(sub == 0, turned[0], turned[1]),
            jnp.where(sub == 0, turned[1], turned[2]),
        ]

    we, wn, below = [], [], []
    for c, dest in ((0, we), (1, wn)):
        for t in range(3):
            at = pl.ds(ROWS_2 + 8 * (3 * c + t), 8)
            a, b = ya[at, :], yb[at, :]
            a, b = turn(even, a, b)
            hi = jnp.where(has_n, a, 0.0)
            lo = jnp.where(has_s, b, 0.0)
            if c == 1:
                below.append(pltpu.roll(lo, 5, 0))
            dest.append(
                stack3(pltpu.roll(lo, 4, 0), wloc[c, t, 0:8, :], wloc[c, t, 8:16, :], pltpu.roll(hi, 4, 0))
            )
    for k in range(3):
        cw3 = west_of([we[t][k] for t in range(3)])
        for t in range(3):
            ok = jnp.ones((8, LANES), F32)
            if k == 0:
                ok = jnp.where(low_half & (tile == 0), 0.0, ok)
            if k == 2:
                ok = jnp.where((~low_half) & (tile == 31), 0.0, ok)
            if t == 2:
                inside = ((lane < 64) & (face < 3)) | ((lane >= 64) & (face > 0))
                ok = jnp.where(inside, ok, 0.0)
            ce = we[t][k] * ok
            cw = cw3[t] * ok
            cn = wn[t][k] * ok
            cs = south_of(wn[t], below[t])[k] * ok
            w5[0, t, k] = ce
            w5[1, t, k] = cw
            w5[2, t, k] = cn
            w5[3, t, k] = cs
            w5[4, t, k] = 1.0 - ce - cw - cn - cs

    per = -(-units // 8)
    for u in range(u0, u1):
        j, i = divmod(u, per)
        a, b = ga[2 * units + i], gb[2 * units + i]
        a, b = turn(even, a, b)
        n = edge_unpack(a, j)
        s = edge_unpack(b, j)
        u -= u0
        hn[u] = jnp.where(has_n, n, 0.0)
        hs[u] = jnp.where(has_s, s, 0.0)

    bit0 = lax.rem(face, 2) == 1
    bit1 = face >= 2

    def body(i, carry):
        fields = []
        for u in [UNROLL_M * i + k for k in range(UNROLL_M)]:
            hi, lo = [], []
            for t in range(2):
                a, b = ga[2 * (u0 + u) + t], gb[2 * (u0 + u) + t]
                a, b = turn(even, a, b)
                hi.append(jnp.where(has_n, a, 0.0))
                lo.append(jnp.where(has_s, b, 0.0))
            hi.append(hn[u])
            lo.append(hs[u])
            for v in range(2):
                x = []
                for t in range(3):
                    m = g[u0 + u, v, t]
                    top = pltpu.roll(hi[t], 4, 0) if v == 0 else hi[t]
                    bottom = lo[t] if v == 0 else pltpu.roll(lo[t], 4, 0)
                    x.append(stack3(bottom, m[0:8], m[8:16], top))
                fields.append(x)
        for sweep in range(4):
            kept = 3 if sweep < 3 else 2
            coefs = [[[w5[c, t, k] for c in range(5)] for k in range(3)] for t in range(3)]
            swept = []
            for x in fields:
                ns = [north_of(x[t]) for t in range(kept)]
                ss = [south_of(x[t]) for t in range(kept)]
                new = [[], [], []]
                for k in range(3):
                    at_k = [x[t][k] for t in range(3)]
                    e, w = east_of(at_k), west_of(at_k)
                    for t in range(kept):
                        ce, cw, cn, cs, cc = coefs[t][k]
                        new[t].append(
                            cc * x[t][k] + ce * e[t] + cw * w[t] + cn * ns[t][k] + cs * ss[t][k]
                        )
                swept.append(new)
            fields = swept
        for c, x in enumerate(fields):
            u = UNROLL_M * i + c // 2
            for t in range(2):
                p = [pltpu.roll(x[t][0], 4, 0), x[t][1], pltpu.roll(x[t][1], 4, 0), x[t][2]]
                p = [jnp.where(bit0, p[d ^ 1], p[d]) for d in range(4)]
                p = [jnp.where(bit1, p[d ^ 2], p[d]) for d in range(4)]
                for k in range(4):
                    zs[k][2 * u + c % 2, :, t * LANES : (t + 1) * LANES] = p[k][0:4]
        return carry

    lax.fori_loop(0, (u1 - u0) // UNROLL_M, body, 0)


def gather_rows(first, size, ids, z0, z1, z2, z3, *refs):
    out, sem = refs[-2:]
    copies = []
    for k, z in enumerate((z0, z1, z2, z3)):
        cols = pl.multiple_of(jnp.bitwise_xor(ids[0], k) * 256, 256)
        dst = out.at[pl.ds(first, size), :, pl.ds(cols, 256)]
        copies.append(pltpu.make_async_copy(z, dst, sem.at[k]))
    for copy in copies:
        copy.start()
    for copy in copies:
        copy.wait()


def on_device(adjoint_seed, face_flow, vert_diff, wet_mask, smooth_weights):
    ids = jnp.stack([lax.axis_index("face"), lax.axis_index("tile")]).astype(jnp.int32)
    tiles = lax.axis_size("tile")
    pair_a = [(i, i ^ 1) for i in range(tiles)]
    pair_b = []
    for t in range(tiles):
        for f in range(4):
            if t in (0, tiles - 1):
                partner = 4 * t + (f ^ 1)
            else:
                partner = 4 * (t + 1 if t % 2 else t - 1) + f
            pair_b.append((4 * t + f, partner))
    side_a = [(0, 1), (1, 0), (2, 3), (3, 2)]
    side_b = [(0, 0), (1, 2), (2, 1), (3, 3)]
    hbm, any_space = pltpu.HBM, pl.ANY

    def across(a, b):
        return lax.ppermute(a, ("tile", "face"), pair_b), lax.ppermute(b, "tile", pair_a)

    def to_face(x, k):
        return lax.ppermute(x, "face", [(i, i ^ k) for i in range(4)])

    edge = (ROWS, LANES)
    packed = (HALF * ROWS, LANES)
    fld, tri, pxa, pxb = call(
        first_solve,
        [((8, 2, FLAT, LANES), VM), ((3, 2, FLAT, LANES), VM), (packed, VM), (packed, VM)],
        [
            VM((2, LEV) + edge, jnp.int32),
            VM((FLAT, LANES), F32),
            pltpu.SemaphoreType.DMA((16,)),
        ],
        limit=5,
        ins=[None] + [hbm] * 4,
        name="first_solve",
    )(ids, adjoint_seed, face_flow, vert_diff, wet_mask)
    weights = [smooth_weights] + [to_face(smooth_weights, k) for k in (1, 2, 3)]
    (wloc,) = call(
        local_weights,
        [((2, 3) + edge, VM)],
        [VM((4, 2, 4, 1024), F32)],
        limit=4,
        name="local_weights",
    )(ids, *weights)
    pxa, pxb, wloc = lax.optimization_barrier((pxa, pxb, wloc))
    xa = lax.ppermute(pxa, "face", side_a)
    xb = lax.ppermute(pxb, "face", side_b)
    rows_1 = ((ROWS_1, LANES), VM)
    ya, yb = call(main_edges, [rows_1, rows_1], limit=4, name="main_edges")(ids, fld)
    ya, yb = call(
        outer_edges, [rows_1, rows_1], limit=4, alias={3: 0, 4: 1}, name="outer_edges"
    )(ids, xa, xb, ya, yb)
    ya, yb = across(ya, yb)
    fe, cf, tre = call(
        coefficients,
        [((8, FLAT, LANES), VM), ((5, 3, FLAT, LANES), VM), ((3, 1, FLAT, LANES), VM)],
        limit=4,
        name="coefficients",
    )(ids, fld, xa, xb)
    halo = VM((3, 3, LEV, LANES), F32)
    sol_shape = ((2, 3, FLAT, LANES), VM)
    fo_shape = ((2, 3) + edge, VM)
    rows_w = ((ROWS_2 + 48, LANES), VM)
    rows_2 = ((ROWS_2, LANES), VM)
    cf, sol_t, ta, tb, fo_t = call(
        functools.partial(step, True, 0),
        [((5, 3, FLAT, LANES), VM), sol_shape, rows_w, rows_w, fo_shape],
        [halo, halo],
        limit=4,
        alias={3: 0},
        name="step_ts",
    )(ids, fld, fe, cf, tri, tre, ya, yb, wloc)
    ta, tb = across(ta, tb)
    sol_u, ua, ub, fo_u = call(
        functools.partial(step, False, 2),
        [sol_shape, rows_2, rows_2, fo_shape],
        [halo, halo],
        limit=4,
        name="step_uv",
    )(ids, fld, fe, cf, tri, tre, ya, yb)

    adj_shape = adjoint_seed.shape
    adj = None
    chunks = []
    for l0, l1 in CHUNKS:
        nl = l1 - l0
        fos = [fo_t, fo_u] if l1 == LEV else []
        units = nl + len(fos)
        per = -(-units // 8)
        args = [ids, sol_t, cf, ta, tb] + fos
        blocks = 2 * units + per
        carried = 0
        if len(chunks) == CARRIER:
            args += [ua, ub]
            carried = blocks
            blocks += BLOCKS_2
        spaces = [None] + [VM] * (len(args) - 1)
        alias = {}
        if adj is not None:
            alias = {len(args): 0}
            args.append(adj)
            spaces.append(any_space)
        adj, g, ga, gb = call(
            functools.partial(last_stencil, 0, l0, nl, len(fos), carried, True),
            [
                (adj_shape, any_space),
                ((units, 2, 3) + edge, VM),
                ((blocks, 8, LANES), VM),
                ((blocks, 8, LANES), VM),
            ],
            [
                halo,
                halo,
                VM((units, 8, LANES), F32),
                VM((units, 8, LANES), F32),
                VM((nl, 2, ROWS, 256), F32),
                pltpu.SemaphoreType.DMA,
            ],
            limit=6,
            alias=alias,
            ins=spaces,
            name="last_ts_%d" % l0,
        )(*args)
        ga, gb = across(ga, gb)
        chunks.append((units, g, ga, gb, carried))

    controls = None
    after = chunks[-1][1]
    sent = []
    first = 0

    def gather(controls, first, size, parts):
        args = [ids] + parts
        alias = {}
        if controls is not None:
            alias = {len(args): 0}
            args.append(controls)
        (controls,) = call(
            functools.partial(gather_rows, first, size),
            [((2 * (LEV + 2), 4, 1024), any_space)],
            [pltpu.SemaphoreType.DMA((4,))],
            ins=[None] + [any_space] * (len(args) - 1),
            limit=4,
            alias=alias,
            name="gather_%d" % first,
        )(*args)
        return controls

    for c, u0, u1 in PIECES:
        units, g, ga, gb, _ = chunks[c]
        n = u1 - u0
        zs = call(
            functools.partial(smooth, units, u0, u1),
            [((2 * n, 4, 256), VM)] * 4,
            [
                VM((5, 3, 3, 8, LANES), F32),
                VM((n, 8, LANES), F32),
                VM((n, 8, LANES), F32),
            ],
            ins=[None] + [VM] * 6 + [any_space],
            limit=4,
            name="smooth_%d_%d" % (c, u0),
        )(ids, g, ga, gb, wloc, ta, tb, after)
        after = zs[0]
        sent.append((first, 2 * n, [zs[0]] + [to_face(zs[k], k) for k in (1, 2, 3)]))
        first += 2 * n
    _, _, ga, gb, carried = chunks[CARRIER]
    (adj,) = call(
        functools.partial(last_stencil, 2, 0, LEV, 0, carried, False),
        [(adj_shape, any_space)],
        [halo, halo, VM((LEV, 2, ROWS, 256), F32), pltpu.SemaphoreType.DMA],
        limit=6,
        alias={6: 0},
        ins=[None] + [VM] * 4 + [any_space] * 2,
        name="last_uv",
    )(ids, sol_u, cf, ga, gb, after, adj)
    for start, size, parts in sent:
        controls = gather(controls, start, size, parts)
    return adj, controls


def solution(mesh):
    placed = (
        P(None, None, "tile", "face"),
        P(None, None, "tile", "face"),
        P(None, "tile", "face"),
        P(None, "tile", "face"),
        P(None, ("tile", "face"), None),
    )
    return jax.shard_map(
        on_device,
        mesh=mesh,
        in_specs=placed,
        out_specs=(P(None, None, "tile", "face"), P(None, ("tile", "face"), None)),
        check_vma=False,
    )
```

```python
import functools

import jax
import jax.numpy as jnp
from jax import lax
from jax.experimental import pallas as pl
from jax.experimental.pallas import tpu as pltpu
from jax.sharding import PartitionSpec as P

F32 = jnp.float32
LEV = 64
ROWS = 16
LANES = 128
FLAT = LEV * ROWS
WET, UE, VN, VD = 4, 5, 6, 7
KAPPA = 0.15
MIB = 2**20
UNROLL_S = 8
UNROLL_L = 8
UNROLL_M = 3

CHUNKS = ((0, 24), (24, 64))
PIECES = ((0, 0, 24), (1, 0, 24), (1, 24, 42))
CARRIER = 0


def iota(shape, dim):
    return lax.broadcasted_iota(jnp.int32, shape, dim)


def rows_of(level):
    return pl.ds(pl.multiple_of(level * ROWS, ROWS), ROWS)


def east_of(tiles):
    last = iota(tiles[0].shape, 1) == LANES - 1
    turned = [pltpu.roll(t, LANES - 1, 1) for t in tiles]
    return [jnp.where(last, turned[(i + 1) % 3], turned[i]) for i in range(3)]


def west_of(tiles):
    first = iota(tiles[0].shape, 1) == 0
    turned = [pltpu.roll(t, 1, 1) for t in tiles]
    return [jnp.where(first, turned[(i + 2) % 3], turned[i]) for i in range(3)]


def call(kernel, outs, scratch=(), limit=8, alias=None, name=None, ins=None, cost=None):
    def run(*args):
        args = list(args)
        specs = [pl.BlockSpec(memory_space=pltpu.SMEM)]
        for i in range(1, len(args)):
            if ins is not None and ins[i] is pltpu.HBM:
                args[i] = pltpu.with_memory_space_constraint(args[i], pltpu.HBM)
        for i in range(1, len(args)):
            space = pltpu.VMEM if ins is None else ins[i]
            specs.append(pl.BlockSpec(memory_space=space))
        return pl.pallas_call(
            kernel,
            out_shape=[jax.ShapeDtypeStruct(s, F32) for s, _ in outs],
            in_specs=specs,
            out_specs=[pl.BlockSpec(memory_space=m) for _, m in outs],
            scratch_shapes=list(scratch),
            input_output_aliases=alias or {},
            compiler_params=pltpu.CompilerParams(vmem_limit_bytes=limit * MIB),
            name=name,
            cost_estimate=cost and pl.CostEstimate(flops=cost[0], bytes_accessed=cost[1], transcendentals=0),
        )(*args)

    return run


VM = pltpu.VMEM


HALF = LEV // 2


def pair_of(i):
    return rows_of(i), rows_of(LEV - 1 - i)


def thirds(tri, wet, vd, tiles, beside=None):
    zero = jnp.zeros((ROWS, LANES), F32)

    def one(i, carry):
        low, rat, low2, rat2 = ([], [], [], [])
        top, bottom = pair_of(i)
        for t in tiles:
            w = wet(t, i)
            up = vd(t, i) * w * wet(t, i + 1)
            p, q = carry[0][t - tiles[0]], carry[1][t - tiles[0]]
            inv = 1.0 / (1.0 + p + up - p * q)
            r = up * inv
            tri[0, t - tiles[0], top, :] = p
            tri[1, t - tiles[0], top, :] = inv
            tri[2, t - tiles[0], top, :] = r
            low.append(up)
            rat.append(r)
            j = LEV - 1 - i
            up = vd(t, j - 1) * wet(t, j - 1) * wet(t, j)
            p, q = carry[2][t - tiles[0]], carry[3][t - tiles[0]]
            inv = 1.0 / (1.0 + p + up - p * q)
            r = up * inv
            tri[0, t - tiles[0], bottom, :] = p
            tri[1, t - tiles[0], bottom, :] = inv
            tri[2, t - tiles[0], bottom, :] = r
            low2.append(up)
            rat2.append(r)
        if beside is not None:
            beside(i)
        return low, rat, low2, rat2

    def body(m, carry):
        return one(2 * m + 1, one(2 * m, carry))

    n = len(tiles)
    lax.fori_loop(0, HALF // 2, body, tuple([zero] * n for _ in range(4)))


def eliminate(rhs, put, get, tri, items, beside=None):
    zero = jnp.zeros((ROWS, LANES), F32)
    n = len(items)

    def inwards(i, carry):
        out = ([], [])
        for side, at in enumerate(pair_of(i)):
            for c, (key, t) in enumerate(items):
                x = (rhs(key, t, at) + tri(0, t, at) * carry[side][c]) * tri(1, t, at)
                put(key, t, at, x)
                out[side].append(x)
        return out

    ends = lax.fori_loop(0, HALF, inwards, ([zero] * n, [zero] * n))
    at, bt = pair_of(HALF - 1)
    start = ([], [])
    for c, (key, t) in enumerate(items):
        r, r2 = tri(2, t, at), tri(2, t, bt)
        y = (ends[0][c] + r * ends[1][c]) * (1.0 / (1.0 - r * r2))
        y2 = ends[1][c] + r2 * y
        put(key, t, at, y)
        put(key, t, bt, y2)
        start[0].append(y)
        start[1].append(y2)
    if beside is not None:
        beside(HALF - 1, start)

    def outwards(k, carry):
        out = ([], [])
        for side, at in enumerate(pair_of(HALF - 2 - k)):
            for c, (key, t) in enumerate(items):
                x = get(key, t, at) + tri(2, t, at) * carry[side][c]
                put(key, t, at, x)
                out[side].append(x)
        if beside is not None:
            beside(HALF - 2 - k, out)
        return out

    return lax.fori_loop(0, HALF - 1, outwards, start)


def first_solve(ids, seed, flow, vd, wet, fld, tri, pxa, pxb, wbuf, pw, sems):
    def tile_copy(src, dst, k):
        copy = pltpu.make_async_copy(src, dst, sems.at[k])
        copy.start()
        return copy

    def place(f, t):
        return fld.at[f, t].reshape(LEV, ROWS, LANES)

    early, late = [], []
    for t in range(2):
        cols = pl.ds(t * LANES, LANES)
        early.append(tile_copy(wet.at[:, :, cols], wbuf.at[t], 8 * t))
        early.append(tile_copy(vd.at[:, :, cols], place(VD, t), 8 * t + 1))
        for v in range(2):
            early.append(tile_copy(flow.at[v, :, :, cols], place(UE + v, t), 8 * t + 2 + v))
    for t in range(2):
        cols = pl.ds(t * LANES, LANES)
        for v in range(4):
            late.append(tile_copy(seed.at[:, v, :, cols], place(v, t), 8 * t + 4 + v))
    for copy in early:
        copy.wait()

    def wet_to_float(i, carry):
        for k in range(8):
            for t in range(2):
                fld[WET, t, rows_of(8 * i + k), :] = wbuf[t, 8 * i + k].astype(F32)
        return carry

    lax.fori_loop(0, LEV // 8, wet_to_float, 0)
    lane = iota((ROWS, LANES), 1)
    first8 = lane < 8
    odd = lax.rem(ids[0], 2) == 1

    def pack(at, fields):
        out = jnp.zeros((ROWS, LANES), F32)
        for f in fields:
            edge = jnp.where(first8, fld[f, 0, at, :], fld[f, 1, at, :])
            mine = (lane >= 16 * f) & (lane < 16 * f + 16)
            by = (16 * f + 8) % LANES
            out = jnp.where(mine, pltpu.roll(edge, by, 1) if by else edge, out)
        return out

    def statics(i):
        top, bottom = pair_of(i)
        pw[top, :] = pack(top, range(4, 8))
        pw[bottom, :] = pack(bottom, range(4, 8))

    thirds(
        tri,
        lambda t, level: fld[WET, t, rows_of(level), :],
        lambda t, level: fld[VD, t, rows_of(level), :],
        (0, 1),
        statics,
    )
    for copy in late:
        copy.wait()

    def put(v, t, at, x):
        fld[v, t, at, :] = x

    for pair in ((0, 1), (2, 3)):
        eliminate(
            lambda v, t, at: fld[v, t, at, :] * fld[WET, t, at, :],
            put,
            lambda v, t, at: fld[v, t, at, :],
            lambda k, t, at: tri[k, t, at, :],
            [(v, t) for v in pair for t in range(2)],
        )

    low = lax.rem(lane, 16) < 8

    def states(n, carry):
        for i in [4 * n + k for k in range(4)]:
            top, bottom = pair_of(i)
            a = pw[top, :] + pack(top, range(4))
            b = pw[bottom, :] + pack(bottom, range(4))
            east = jnp.where(low, a, pltpu.roll(b, 8, 1))
            west = jnp.where(low, pltpu.roll(a, LANES - 8, 1), b)
            at = rows_of(i)
            pxa[at, :] = jnp.where(odd, west, east)
            pxb[at, :] = jnp.where(odd, east, west)
        return carry

    lax.fori_loop(0, HALF // 4, states, 0)


def spread(west, east, half, low):
    if half == 0:
        return jnp.where(low, west, pltpu.roll(east, 8, 1))
    return jnp.where(low, pltpu.roll(west, LANES - 8, 1), east)


def outer_of(both, f):
    by = (120 - 16 * f) % LANES
    return pltpu.roll(both, by, 1) if by else both


OUTER = 5 * 2 * LEV
ROWS_1 = OUTER + LEV
ROWS_2 = 2 * 2 * LEV + 2 * 8
BLOCKS_2 = ROWS_2 // 8


def edge_pack(tiles8):
    lane = iota((8, LANES), 1)
    packed = jnp.zeros((8, LANES), F32)
    for g, t in enumerate(tiles8):
        turned = pltpu.roll(t, (16 * g + 8) % LANES, 1)
        packed = jnp.where((lane >= 16 * g) & (lane < 16 * g + 16), turned, packed)
    return packed


def edge_unpack(packed, g):
    return pltpu.roll(packed, (-(16 * g + 8)) % LANES, 1)


def even_tile(ids):
    return lax.rem(ids[1], 2) == 0


def turn(even, x, y):
    return jnp.where(even, y, x), jnp.where(even, x, y)


def put_edges(even, pick, fields, oa, ob):
    for f in range(fields):
        for t in range(2):
            for g in range(8):
                n, s = pick(f, t, g)
                at = pl.ds((f * 2 + t) * LEV + 8 * g, 8)
                oa[at, :], ob[at, :] = turn(even, n, s)
        outer = [pick(f, 2, g) for g in range(8)]
        n = edge_pack([o[0] for o in outer])
        s = edge_pack([o[1] for o in outer])
        at = pl.ds(fields * 2 * LEV + 8 * f, 8)
        oa[at, :], ob[at, :] = turn(even, n, s)


def edge_rows(ref, g):
    north = ref[pl.ds(g * 8 * ROWS + ROWS - 1, 8, stride=ROWS), :]
    south = ref[pl.ds(g * 8 * ROWS, 8, stride=ROWS), :]
    return north, south


def main_edges(ids, fld, ya, yb):
    even = even_tile(ids)
    for k, f in enumerate((0, 1, WET, 2, 3)):
        for t in range(2):
            for g in range(8):
                n, s = edge_rows(fld.at[f, t], g)
                if f == WET:
                    n = n * (KAPPA - 0.5 * edge_rows(fld.at[VN, t], g)[0])
                at = pl.ds((2 * k + t) * LEV + 8 * g, 8)
                ya[at, :], yb[at, :] = turn(even, n, s)


def outer_edges(ids, xa, xb, ya_in, yb_in, ya, yb):
    face, tile = ids[0], ids[1]
    odd = lax.rem(face, 2) == 1
    even = even_tile(ids)
    for g in range(4):
        na, sa = edge_rows(xa, g)
        nb, sb = edge_rows(xb, g)
        west = (jnp.where(odd, na, nb), jnp.where(odd, sa, sb))
        east = (jnp.where(odd, nb, na), jnp.where(odd, sb, sa))
        for first, inside, (n, s) in ((0, face > 0, west), (HALF, face < 3, east)):
            n = jnp.where(inside, n, 0.0)
            s = jnp.where(inside, s, 0.0)
            at = pl.ds(OUTER + first + 8 * g, 8)
            ya[at, :], yb[at, :] = turn(even, n, s)


def local_weights(ids, w0, w1, w2, w3, wloc, pieces):
    face = ids[0]
    for k, w in enumerate((w0, w1, w2, w3)):
        pieces[k] = w[...]
    lane4 = iota((4, LANES), 1)
    for d in range(4):
        slot = jnp.bitwise_xor(face, d)
        for c in range(2):
            for t in range(3):
                at = pl.ds(4 * d, 4)
                if t < 2:
                    first = pl.multiple_of((2 * face + t) * LANES, LANES)
                    wloc[c, t, at, :] = pieces[slot, c, :, pl.ds(first, LANES)]
                    continue
                first = pl.multiple_of(jnp.minimum(2 * face + 2, 7) * LANES, LANES)
                e = pieces[slot, c, :, pl.ds(first, LANES)]
                first = pl.multiple_of(jnp.maximum(2 * face - 1, 0) * LANES, LANES)
                w = pieces[slot, c, :, pl.ds(first, LANES)]
                w = jnp.where((lane4 >= 120) & (face > 0), w, 0.0)
                wloc[c, t, at, :] = jnp.where((lane4 < 8) & (face < 3), e, w)


def coefficients(ids, fld, xa, xb, fe, cf, tri):
    row = iota((ROWS, LANES), 0)
    face = ids[0]
    odd = lax.rem(face, 2) == 1
    lane = iota((ROWS, LANES), 1)
    on_east = (lane < 8) & (face < 3)
    on_west = (lane >= 120) & (face > 0)

    outside = on_east | on_west
    low = lax.rem(lane, 16) < 8

    def unpack(n, carry):
        for i in [4 * n + k for k in range(4)]:
            a, b = xa[rows_of(i), :], xb[rows_of(i), :]
            from_west = jnp.where(odd, a, b)
            from_east = jnp.where(odd, b, a)
            for half, at in enumerate(pair_of(i)):
                both = spread(from_west, from_east, half, low)
                for f in range(8):
                    fe[f, at, :] = jnp.where(outside, outer_of(both, f), 0.0)
        return carry

    lax.fori_loop(0, HALF // 4, unpack, 0)
    def body(i):
        for at in pair_of(i):

            def get(f):
                return [fld[f, 0, at, :], fld[f, 1, at, :], fe[f, at, :]]

            wet, ue, vn = (get(f) for f in (WET, UE, VN))
            wet_e = east_of(wet)
            qw_w = west_of([w * (KAPPA - 0.5 * u) for w, u in zip(wet, ue)])
            for t in range(3):
                w = wet[t]
                ce = w * (KAPPA + 0.5 * ue[t]) * wet_e[t]
                cw = w * qw_w[t]
                wn = jnp.where(row == ROWS - 1, 1.0, pltpu.roll(w, ROWS - 1, 0))
                qs = jnp.where(row == 0, 1.0, pltpu.roll(w * (KAPPA - 0.5 * vn[t]), 1, 0))
                cf[0, t, at, :] = ce
                cf[1, t, at, :] = cw
                cf[2, t, at, :] = w * (KAPPA + 0.5 * vn[t]) * wn
                cf[3, t, at, :] = w * qs
                cf[4, t, at, :] = w - ce - cw

    thirds(
        tri,
        lambda t, level: fe[WET, rows_of(level), :],
        lambda t, level: fe[VD, rows_of(level), :],
        (2,),
        body,
    )


def slot_of(level):
    return jnp.where(level < HALF, level, LEV + HALF - 1 - level)


def take_first_edges(ids, ya, yb, hn, hs, first):
    even = even_tile(ids)
    lane = iota((8, LANES), 1)

    def both(at):
        a, b = ya[at, :], yb[at, :]
        return turn(even, a, b)

    for f, k in enumerate((0, 1, 2) if first else (3, 4)):
        for t in range(2):
            for g in range(8):
                at = pl.ds(8 * g, 8)
                n, s = both(pl.ds((2 * k + t) * LEV + 8 * g, 8))
                hn[f, t, at, :] = n
                hs[f, t, at, :] = s
    low = lax.rem(lane, 16) < 8
    for g in range(4):
        wests = both(pl.ds(OUTER + 8 * g, 8))
        easts = both(pl.ds(OUTER + HALF + 8 * g, 8))
        for half in range(2):
            spreads = [spread(w, e, half, low) for w, e in zip(wests, easts)]

            def outer(side, f):
                return outer_of(spreads[side], f)

            at = pl.ds(HALF * half + 8 * g, 8)
            for f, k in enumerate((0, 1) if first else (2, 3)):
                hn[f, 2, at, :] = outer(0, k)
                hs[f, 2, at, :] = outer(1, k)
            if first:
                hn[2, 2, at, :] = outer(0, WET)
                hs[2, 2, at, :] = outer(1, WET) * (KAPPA - 0.5 * outer(1, VN))


def take_edges(ids, load, hn, hs, groups=(0, 8)):
    even = even_tile(ids)
    for f in range(2):
        oa, ob = load(32 + f)
        on, os = turn(even, oa, ob)
        for g in range(*groups):
            at = pl.ds(8 * g, 8)
            for t in range(2):
                a, b = load((f * 2 + t) * 8 + g)
                hn[f, t, at, :], hs[f, t, at, :] = turn(even, a, b)
            hn[f, 2, at, :] = edge_unpack(on, g)
            hs[f, 2, at, :] = edge_unpack(os, g)


def stencil(y, ref, level, coef, north_row, south_row, tiles=3):
    e, w = east_of(y), west_of(y)
    sub = iota((8, LANES), 0)
    base = pl.multiple_of(level * ROWS, ROWS)
    out = []
    for t in range(tiles):
        n = jnp.concatenate(
            [
                ref(t)[pl.ds(base + 1, 8), :],
                jnp.where(sub == 7, north_row[t], pltpu.roll(y[t][8:16], 7, 0)),
            ],
            0,
        )
        s = jnp.concatenate(
            [
                jnp.where(sub == 0, south_row[t], pltpu.roll(y[t][0:8], 1, 0)),
                ref(t)[pl.ds(base + 7, 8), :],
            ],
            0,
        )
        ce, cw, cn, cs, cc = coef[t]
        out.append(cc * y[t] + ce * e[t] + cw * w[t] + cn * n + cs * s)
    return out


def step(first, v0, ids, fld, fe, cfi, trm, tre, ya, yb, *refs):
    if first:
        wloc, cf, sol, oa, ob, fo, hn, hs = refs
    else:
        sol, oa, ob, fo, hn, hs = refs
    even = even_tile(ids)
    row = iota((ROWS, LANES), 0)
    take_first_edges(ids, ya, yb, hn, hs, first)

    def get(v, at):
        return [fld[v0 + v, 0, at, :], fld[v0 + v, 1, at, :], fe[v0 + v, at, :]]

    north_in = jnp.where(ids[1] < 31, 1.0, 0.0).astype(F32)
    south_in = jnp.where(ids[1] > 0, 1.0, 0.0).astype(F32)

    def apply(i, carry):
        for k in range(UNROLL_S):
            level = UNROLL_S * i + k
            at = rows_of(level)
            ones = [pl.ds(level, 1), pl.ds(level, 1), pl.ds(slot_of(level), 1)]
            coef = []
            for t in range(3):
                ce, cw, cn, cs, cc = (cfi[c, t, at, :] for c in range(5))
                if first:
                    cn = jnp.where(row == ROWS - 1, cn * (hn[2, t, ones[t], :] * north_in), cn)
                    cs = jnp.where(row == 0, cs * (hs[2, t, ones[t], :] * south_in), cs)
                    cc = cc - cn - cs
                    cf[2, t, at, :] = cn
                    cf[3, t, at, :] = cs
                    cf[4, t, at, :] = cc
                coef.append((ce, cw, cn, cs, cc))
            for v in range(2):
                n = [hn[v, t, ones[t], :] for t in range(3)]
                s = [hs[v, t, ones[t], :] for t in range(3)]
                f = v0 + v
                adj = stencil(
                    get(v, at), lambda t: fe.at[f] if t == 2 else fld.at[f, t], level, coef, n, s
                )
                for t in range(3):
                    sol[v, t, at, :] = adj[t]
        return carry

    lax.fori_loop(0, LEV // UNROLL_S, apply, 0)

    def put(v, t, at, x):
        sol[v, t, at, :] = x

    def load(v, t, at):
        return sol[v, t, at, :]

    top = eliminate(
        load,
        put,
        load,
        lambda k, t, at: tre[k, 0, at, :] if t == 2 else trm[k, t, at, :],
        [(v, t) for v in range(2) for t in range(3)],
    )[0]
    for v in range(2):
        y = get(v, pl.ds(0, ROWS))
        for t in range(3):
            fo[v, t] = y[t] + top[3 * v + t]
    put_edges(even, lambda f, t, g: edge_rows(sol.at[f, t], g), 2, oa, ob)
    if first:
        for c in range(2):
            for t in range(3):
                n = wloc[c, t, 8:16, :]
                s = wloc[c, t, 0:8, :]
                at = pl.ds(ROWS_2 + 8 * (3 * c + t), 8)
                oa[at, :], ob[at, :] = turn(even, n, s)


def last_stencil(v0, l0, nl, extra, carried, grads, *refs):
    ids, sol, cf, ya, yb = refs[:5]
    refs = refs[5:]
    fos = refs[:extra]
    refs = refs[extra:]
    if grads and carried:
        ua, ub = refs[:2]
        refs = refs[2:]
    if not grads:
        refs = refs[1:]
    if l0 or v0:
        refs = refs[1:]
    if grads:
        adj_out, g, ga, gb, hn, hs, en, es, buf, sem = refs
    else:
        adj_out, hn, hs, buf, sem = refs
    row = iota((ROWS, LANES), 0)
    even = even_tile(ids)
    low_half = iota((8, LANES), 0) < 4

    def load(block):
        if not grads:
            return ya[carried + block], yb[carried + block]
        at = pl.ds(8 * block, 8)
        return ya[at, :], yb[at, :]

    take_edges(ids, load, hn, hs, (l0 // 8, (l0 + nl) // 8))

    def edges(u, ts, ss):
        for t in range(3):
            a, b = ts[t], ss[t]
            n = jnp.where(low_half, pltpu.roll(a[8:16], 4, 0), b[8:16])
            s = jnp.where(low_half, a[0:8], pltpu.roll(b[0:8], 4, 0))
            if t < 2:
                ga[2 * u + t], gb[2 * u + t] = turn(even, n, s)
            else:
                en[u] = n
                es[u] = s

    def body(i, carry):
        for k in range(UNROLL_L):
            u = UNROLL_L * i + k
            level = l0 + u
            at = rows_of(level)
            one = pl.ds(level, 1)
            coef = [tuple(cf[c, t, at, :] for c in range(5)) for t in range(3)]
            both = []
            for v in range(2):
                y = [sol[v, t, at, :] for t in range(3)]
                n = [hn[v, t, one, :] for t in range(3)]
                s = [hs[v, t, one, :] for t in range(3)]
                x = stencil(y, lambda t: sol.at[v, t], level, coef, n, s, 3 if grads else 2)
                buf[u, v, :, 0:LANES] = x[0]
                buf[u, v, :, LANES : 2 * LANES] = x[1]
                if grads:
                    for t in range(3):
                        g[u, v, t] = x[t]
                both.append(x)
            if grads:
                edges(u, *both)
        return carry

    lax.fori_loop(0, nl // UNROLL_L, body, 0)
    copy = pltpu.make_async_copy(buf, adj_out.at[pl.ds(l0, nl), pl.ds(v0, 2)], sem)
    copy.start()
    if grads:
        for i, fo in enumerate(fos):
            pair = [[fo[v, t] for t in range(3)] for v in range(2)]
            for v in range(2):
                for t in range(3):
                    g[nl + i, v, t] = pair[v][t]
            edges(nl + i, *pair)
        units = nl + extra
        per = -(-units // 8)
        lane = iota((8, LANES), 1)
        for i in range(per):
            pn = ps = jnp.zeros((8, LANES), F32)
            for j in range(8):
                u = j * per + i
                if u < units:
                    mine = (lane >= 16 * j) & (lane < 16 * j + 16)
                    pn = jnp.where(mine, pltpu.roll(en[u], (16 * j + 8) % LANES, 1), pn)
                    ps = jnp.where(mine, pltpu.roll(es[u], (16 * j + 8) % LANES, 1), ps)
            ga[2 * units + i], gb[2 * units + i] = turn(even, pn, ps)
        if carried:
            for i in range(BLOCKS_2):
                ga[2 * units + per + i] = ua[pl.ds(8 * i, 8), :]
                gb[2 * units + per + i] = ub[pl.ds(8 * i, 8), :]
    copy.wait()


def smooth(units, u0, u1, ids, g, ga, gb, wloc, ya, yb, after, z0, z1, z2, z3, w5, hn, hs):
    del after
    zs = (z0, z1, z2, z3)
    face, tile = ids[0], ids[1]
    even = even_tile(ids)
    has_n, has_s = tile < 31, tile > 0
    sub = iota((8, LANES), 0)
    lane = iota((8, LANES), 1)
    low_half = sub < 4

    def stack3(lo, m0, m1, hi):
        r0, r1 = pltpu.roll(m0, 4, 0), pltpu.roll(m1, 4, 0)
        return [
            jnp.where(low_half, lo, r0),
            jnp.where(low_half, r0, r1),
            jnp.where(low_half, r1, hi),
        ]

    def north_of(k3):
        turned = [pltpu.roll(x, 7, 0) for x in k3]
        return [
            jnp.where(sub == 7, turned[1], turned[0]),
            jnp.where(sub == 7, turned[2], turned[1]),
            turned[2],
        ]

    def south_of(k3, below=None):
        turned = [pltpu.roll(x, 1, 0) for x in k3]
        return [
            turned[0] if below is None else jnp.where(sub == 0, below, turned[0]),
            jnp.where(sub == 0, turned[0], turned[1]),
            jnp.where(sub == 0, turned[1], turned[2]),
        ]

    we, wn, below = [], [], []
    for c, dest in ((0, we), (1, wn)):
        for t in range(3):
            at = pl.ds(ROWS_2 + 8 * (3 * c + t), 8)
            a, b = ya[at, :], yb[at, :]
            a, b = turn(even, a, b)
            hi = jnp.where(has_n, a, 0.0)
            lo = jnp.where(has_s, b, 0.0)
            if c == 1:
                below.append(pltpu.roll(lo, 5, 0))
            dest.append(
                stack3(pltpu.roll(lo, 4, 0), wloc[c, t, 0:8, :], wloc[c, t, 8:16, :], pltpu.roll(hi, 4, 0))
            )
    for k in range(3):
        cw3 = west_of([we[t][k] for t in range(3)])
        for t in range(3):
            ok = jnp.ones((8, LANES), F32)
            if k == 0:
                ok = jnp.where(low_half & (tile == 0), 0.0, ok)
            if k == 2:
                ok = jnp.where((~low_half) & (tile == 31), 0.0, ok)
            if t == 2:
                inside = ((lane < 64) & (face < 3)) | ((lane >= 64) & (face > 0))
                ok = jnp.where(inside, ok, 0.0)
            ce = we[t][k] * ok
            cw = cw3[t] * ok
            cn = wn[t][k] * ok
            cs = south_of(wn[t], below[t])[k] * ok
            w5[0, t, k] = ce
            w5[1, t, k] = cw
            w5[2, t, k] = cn
            w5[3, t, k] = cs
            w5[4, t, k] = 1.0 - ce - cw - cn - cs

    per = -(-units // 8)
    for u in range(u0, u1):
        j, i = divmod(u, per)
        a, b = ga[2 * units + i], gb[2 * units + i]
        a, b = turn(even, a, b)
        n = edge_unpack(a, j)
        s = edge_unpack(b, j)
        u -= u0
        hn[u] = jnp.where(has_n, n, 0.0)
        hs[u] = jnp.where(has_s, s, 0.0)

    bit0 = lax.rem(face, 2) == 1
    bit1 = face >= 2

    def body(i, carry):
        fields = []
        for u in [UNROLL_M * i + k for k in range(UNROLL_M)]:
            hi, lo = [], []
            for t in range(2):
                a, b = ga[2 * (u0 + u) + t], gb[2 * (u0 + u) + t]
                a, b = turn(even, a, b)
                hi.append(jnp.where(has_n, a, 0.0))
                lo.append(jnp.where(has_s, b, 0.0))
            hi.append(hn[u])
            lo.append(hs[u])
            for v in range(2):
                x = []
                for t in range(3):
                    m = g[u0 + u, v, t]
                    top = pltpu.roll(hi[t], 4, 0) if v == 0 else hi[t]
                    bottom = lo[t] if v == 0 else pltpu.roll(lo[t], 4, 0)
                    x.append(stack3(bottom, m[0:8], m[8:16], top))
                fields.append(x)
        for sweep in range(4):
            kept = 3 if sweep < 3 else 2
            coefs = [[[w5[c, t, k] for c in range(5)] for k in range(3)] for t in range(3)]
            swept = []
            for x in fields:
                ns = [north_of(x[t]) for t in range(kept)]
                ss = [south_of(x[t]) for t in range(kept)]
                new = [[], [], []]
                for k in range(3):
                    at_k = [x[t][k] for t in range(3)]
                    e, w = east_of(at_k), west_of(at_k)
                    for t in range(kept):
                        ce, cw, cn, cs, cc = coefs[t][k]
                        new[t].append(
                            cc * x[t][k] + ce * e[t] + cw * w[t] + cn * ns[t][k] + cs * ss[t][k]
                        )
                swept.append(new)
            fields = swept
        for c, x in enumerate(fields):
            u = UNROLL_M * i + c // 2
            for t in range(2):
                p = [pltpu.roll(x[t][0], 4, 0), x[t][1], pltpu.roll(x[t][1], 4, 0), x[t][2]]
                p = [jnp.where(bit0, p[d ^ 1], p[d]) for d in range(4)]
                p = [jnp.where(bit1, p[d ^ 2], p[d]) for d in range(4)]
                for k in range(4):
                    zs[k][2 * u + c % 2, :, t * LANES : (t + 1) * LANES] = p[k][0:4]
        return carry

    lax.fori_loop(0, (u1 - u0) // UNROLL_M, body, 0)


def gather_rows(first, size, ids, z0, z1, z2, z3, *refs):
    out, sem = refs[-2:]
    copies = []
    for k, z in enumerate((z0, z1, z2, z3)):
        cols = pl.multiple_of(jnp.bitwise_xor(ids[0], k) * 256, 256)
        dst = out.at[pl.ds(first, size), :, pl.ds(cols, 256)]
        copies.append(pltpu.make_async_copy(z, dst, sem.at[k]))
    for copy in copies:
        copy.start()
    for copy in copies:
        copy.wait()


def on_device(adjoint_seed, face_flow, vert_diff, wet_mask, smooth_weights):
    ids = jnp.stack([lax.axis_index("face"), lax.axis_index("tile")]).astype(jnp.int32)
    tiles = lax.axis_size("tile")
    pair_a = [(i, i ^ 1) for i in range(tiles)]
    pair_b = []
    for t in range(tiles):
        for f in range(4):
            if t in (0, tiles - 1):
                partner = 4 * t + (f ^ 1)
            else:
                partner = 4 * (t + 1 if t % 2 else t - 1) + f
            pair_b.append((4 * t + f, partner))
    side_a = [(0, 1), (1, 0), (2, 3), (3, 2)]
    side_b = [(0, 0), (1, 2), (2, 1), (3, 3)]
    hbm, any_space = pltpu.HBM, pl.ANY

    def across(a, b):
        return lax.ppermute(a, ("tile", "face"), pair_b), lax.ppermute(b, "tile", pair_a)

    def to_face(x, k):
        return lax.ppermute(x, "face", [(i, i ^ k) for i in range(4)])

    edge = (ROWS, LANES)
    packed = (HALF * ROWS, LANES)
    fld, tri, pxa, pxb = call(
        first_solve,
        [((8, 2, FLAT, LANES), VM), ((3, 2, FLAT, LANES), VM), (packed, VM), (packed, VM)],
        [
            VM((2, LEV) + edge, jnp.int32),
            VM((FLAT, LANES), F32),
            pltpu.SemaphoreType.DMA((16,)),
        ],
        limit=5,
        ins=[None] + [hbm] * 4,
        name="first_solve",
    )(ids, adjoint_seed, face_flow, vert_diff, wet_mask)
    weights = [smooth_weights] + [to_face(smooth_weights, k) for k in (1, 2, 3)]
    (wloc,) = call(
        local_weights,
        [((2, 3) + edge, VM)],
        [VM((4, 2, 4, 1024), F32)],
        limit=4,
        name="local_weights",
    )(ids, *weights)
    pxa, pxb, wloc = lax.optimization_barrier((pxa, pxb, wloc))
    xa = lax.ppermute(pxa, "face", side_a)
    xb = lax.ppermute(pxb, "face", side_b)
    rows_1 = ((ROWS_1, LANES), VM)
    ya, yb = call(main_edges, [rows_1, rows_1], limit=4, name="main_edges")(ids, fld)
    ya, yb = call(
        outer_edges, [rows_1, rows_1], limit=4, alias={3: 0, 4: 1}, name="outer_edges"
    )(ids, xa, xb, ya, yb)
    ya, yb = across(ya, yb)
    fe, cf, tre = call(
        coefficients,
        [((8, FLAT, LANES), VM), ((5, 3, FLAT, LANES), VM), ((3, 1, FLAT, LANES), VM)],
        limit=4,
        name="coefficients",
    )(ids, fld, xa, xb)
    halo = VM((3, 3, LEV, LANES), F32)
    sol_shape = ((2, 3, FLAT, LANES), VM)
    fo_shape = ((2, 3) + edge, VM)
    rows_w = ((ROWS_2 + 48, LANES), VM)
    rows_2 = ((ROWS_2, LANES), VM)
    cf, sol_t, ta, tb, fo_t = call(
        functools.partial(step, True, 0),
        [((5, 3, FLAT, LANES), VM), sol_shape, rows_w, rows_w, fo_shape],
        [halo, halo],
        limit=4,
        alias={3: 0},
        name="step_ts",
    )(ids, fld, fe, cf, tri, tre, ya, yb, wloc)
    ta, tb = across(ta, tb)
    sol_u, ua, ub, fo_u = call(
        functools.partial(step, False, 2),
        [sol_shape, rows_2, rows_2, fo_shape],
        [halo, halo],
        limit=4,
        name="step_uv",
    )(ids, fld, fe, cf, tri, tre, ya, yb)

    adj_shape = adjoint_seed.shape
    adj = None
    chunks = []
    for l0, l1 in CHUNKS:
        nl = l1 - l0
        fos = [fo_t, fo_u] if l1 == LEV else []
        units = nl + len(fos)
        per = -(-units // 8)
        args = [ids, sol_t, cf, ta, tb] + fos
        blocks = 2 * units + per
        carried = 0
        if len(chunks) == CARRIER:
            args += [ua, ub]
            carried = blocks
            blocks += BLOCKS_2
        spaces = [None] + [VM] * (len(args) - 1)
        alias = {}
        if adj is not None:
            alias = {len(args): 0}
            args.append(adj)
            spaces.append(any_space)
        adj, g, ga, gb = call(
            functools.partial(last_stencil, 0, l0, nl, len(fos), carried, True),
            [
                (adj_shape, any_space),
                ((units, 2, 3) + edge, VM),
                ((blocks, 8, LANES), VM),
                ((blocks, 8, LANES), VM),
            ],
            [
                halo,
                halo,
                VM((units, 8, LANES), F32),
                VM((units, 8, LANES), F32),
                VM((nl, 2, ROWS, 256), F32),
                pltpu.SemaphoreType.DMA,
            ],
            limit=6,
            alias=alias,
            ins=spaces,
            name="last_ts_%d" % l0,
        )(*args)
        ga, gb = across(ga, gb)
        chunks.append((units, g, ga, gb, carried))

    controls = None
    after = chunks[-1][1]
    sent = []
    first = 0

    def gather(controls, first, size, parts):
        args = [ids] + parts
        alias = {}
        if controls is not None:
            alias = {len(args): 0}
            args.append(controls)
        (controls,) = call(
            functools.partial(gather_rows, first, size),
            [((2 * (LEV + 2), 4, 1024), any_space)],
            [pltpu.SemaphoreType.DMA((4,))],
            ins=[None] + [any_space] * (len(args) - 1),
            limit=4,
            alias=alias,
            name="gather_%d" % first,
        )(*args)
        return controls

    for c, u0, u1 in PIECES:
        units, g, ga, gb, _ = chunks[c]
        n = u1 - u0
        zs = call(
            functools.partial(smooth, units, u0, u1),
            [((2 * n, 4, 256), VM)] * 4,
            [
                VM((5, 3, 3, 8, LANES), F32),
                VM((n, 8, LANES), F32),
                VM((n, 8, LANES), F32),
            ],
            ins=[None] + [VM] * 6 + [any_space],
            limit=4,
            cost=(2 * n * 4 * 24 * 384 * 9, 2 * n * 4 * (16 * 384 + 16 * 256)),
            name="smooth_%d_%d" % (c, u0),
        )(ids, g, ga, gb, wloc, ta, tb, after)
        after = zs[0]
        sent.append((first, 2 * n, [zs[0]] + [to_face(zs[k], k) for k in (1, 2, 3)]))
        first += 2 * n
    _, _, ga, gb, carried = chunks[CARRIER]
    (adj,) = call(
        functools.partial(last_stencil, 2, 0, LEV, 0, carried, False),
        [(adj_shape, any_space)],
        [halo, halo, VM((LEV, 2, ROWS, 256), F32), pltpu.SemaphoreType.DMA],
        limit=6,
        alias={6: 0},
        ins=[None] + [VM] * 4 + [any_space] * 2,
        cost=(LEV * 2 * ROWS * 256 * 9, LEV * ROWS * 4 * (2 * 384 + 2 * 256 + 5 * 384)),
        name="last_uv",
    )(ids, sol_u, cf, ga, gb, after, adj)
    for start, size, parts in sent:
        controls = gather(controls, start, size, parts)
    return adj, controls


def solution(mesh):
    placed = (
        P(None, None, "tile", "face"),
        P(None, None, "tile", "face"),
        P(None, "tile", "face"),
        P(None, "tile", "face"),
        P(None, ("tile", "face"), None),
    )
    return jax.shard_map(
        on_device,
        mesh=mesh,
        in_specs=placed,
        out_specs=(P(None, None, "tile", "face"), P(None, ("tile", "face"), None)),
        check_vma=False,
    )
```
